128 devices in a mesh: dp: 8 (over y, core), tensor: 16 (over z, x).
Axes of the slice: x: 4, y: 4, z: 4, core: 2. Of those that a mesh axis runs over, the one named last changes fastest.
Arguments:
- ids: int32 [6144], P(('dp', 'tensor')), may hold values from 0 to 16383, as said below
- doc_lengths: int32 [16], replicated, may hold values from 1 to 3072, 6144 in all
- table: bfloat16 [16384, 4096], P('tensor'), may hold values from -6 to 6
- attn_gain: float32 [4096], replicated, may hold values from 0.1 to 1.9
- wq: bfloat16 [4096, 4096], P(None, 'tensor')
- wkv: bfloat16 [4096, 2048], P(None, 'tensor')
- wo: bfloat16 [4096, 4096], P('tensor'), may hold values from -0.09375 to 0.09375
- mlp_gain: float32 [4096], replicated, may hold values from 0.1 to 1.9
- w_gate: bfloat16 [4096, 7168], P(None, 'tensor'), may hold values from -0.09375 to 0.09375
- w_up: bfloat16 [4096, 7168], P(None, 'tensor'), may hold values from -0.09375 to 0.09375
- w_down: bfloat16 [7168, 4096], P('tensor'), may hold values from -0.0625 to 0.0625
Outputs:
- layer_out: bfloat16 [6144, 4096], P(('dp', 'tensor'))
The draws below stay inside these ranges and needn't reach their ends.
Inputs may be any that keep to these rules, and one draw needn't show every extreme that they name: ids name added rows. In each aligned block of 48 tokens (the tokens of one device), at most 6 ids lie in any one owner range r * 1024 to (r + 1) * 1024 - 1, and in every block some range holds exactly 6.
All inputs are finite; a program needn't handle non-finite values.
Results may differ from the reference program's by a relative error of at most 0.022.
The reference program's roundings to bfloat16 on the way count: a program that leaves them out, or rounds other values in their place, can miss the bound.
Values may be sent and summed in bfloat16 or wider, within the bound.
A program may use at most 192 MiB of HBM per device.

```python
import math
import jax
import jax.numpy as jnp
import numpy as np
from jax import lax

D = 4096
QH = 32
KVH = 8
HD = 128
FF = 7168
NEWV = 16384
TOKENS = 6144
TOK_SP = 48
CAP = 6
ROWS_OWN = 1024
NDOC = 16
MAXDOC = 3072
N_TENSOR = 16


def query_weights(base_key):
    return jax.random.normal(jax.random.fold_in(base_key, 101), (D, QH * HD), jnp.float32) * D ** (-0.5)


def draw_wq(key, part):
    return query_weights(key).astype(jnp.bfloat16)


def draw_wkv(key, part):
    fresh = jax.random.normal(jax.random.fold_in(key, 202), (D, KVH, 2, HD), jnp.float32) * D ** (-0.5)
    return fresh.reshape(D, KVH * 2 * HD).astype(jnp.bfloat16)


def draw_ids(key, part):
    slot_count = N_TENSOR * CAP

    def one_block(block_key):
        first_key, second_key, third_key, fourth_key = jax.random.split(block_key, 4)
        ranking = jax.random.permutation(first_key, slot_count)
        busiest = jax.random.randint(second_key, (), 0, N_TENSOR)
        owner_of = jnp.arange(slot_count, dtype=jnp.int32) // CAP
        ranking = ranking - jnp.where(owner_of == busiest, slot_count, 0)
        chosen = jnp.argsort(ranking)[:TOK_SP]
        owners = jax.random.permutation(third_key, chosen // CAP)
        within = jax.random.randint(fourth_key, (TOK_SP,), 0, ROWS_OWN)
        return owners * ROWS_OWN + within
    block_keys = jax.random.split(key, TOKENS // TOK_SP)
    return jax.vmap(one_block)(block_keys).reshape(TOKENS).astype(jnp.int32)


def levels(stream_key, shape, shards, least, high):
    level = 1.0
    for position, parts in shards:
        steps = jax.random.uniform(jax.random.fold_in(jax.random.fold_in(stream_key, 6), position), (parts,), jnp.float32, least / len(shards), high / len(shards))
        level = level * jnp.repeat(jnp.exp(steps), shape[position] // parts).reshape((-1,) + (1,) * (len(shape) - 1 - position))
    return level


def profile(number_of, total, limit, lean):
    weights = [(1 << 20) // math.isqrt(rank ** lean) + 1 for rank in range(2, number_of + 1)]
    surplus, counts = total - limit - (number_of - 1), [1] * (number_of - 1)
    while surplus > 0:
        free = [i for i in range(number_of - 1) if counts[i] < limit]
        mass, budget = sum([weights[i] for i in free]), surplus
        for i in free:
            extra = min(limit - counts[i], max(1, budget * weights[i] // mass), surplus)
            counts[i] = counts[i] + extra
            surplus = surplus - extra
    return np.array([limit] + counts)


def uneven(rng, number_of, total, bound, slope):
    if number_of == 2:
        one = jax.random.randint(rng, (), max(1, total - bound), min(bound, total - 1) + 1)
        return jnp.stack([one, total - one])
    sizes = jnp.asarray(profile(number_of, total, bound, slope), jnp.int32)
    twos = (number_of - 1) // 2
    giver, sink = sizes[1:1 + 2 * twos:2], sizes[2:2 + 2 * twos:2]
    margin = jnp.minimum(giver - 1, bound - sink)
    passed = jax.random.randint(jax.random.fold_in(rng, 1), (twos,), 0, 1 << 20) % (margin + 1)
    sizes = sizes.at[1:1 + 2 * twos:2].set(giver - passed).at[2:2 + 2 * twos:2].set(sink + passed)
    return sizes[jax.random.permutation(jax.random.fold_in(rng, 2), number_of)]


def gaussian(rng, shape, deviation, reach, cuts=(), kind=jnp.bfloat16):
    drawn = deviation * jax.random.normal(rng, shape, jnp.float32)
    if cuts:
        drawn = drawn * levels(rng, shape, cuts, -0.22, 0.18)
    return jnp.clip(drawn, -reach, reach).astype(kind)


def setup_inputs(seed: int = 0) -> dict:
    seeds = jax.random.split(jax.random.key(seed), 12)
    return {
        "ids": draw_ids(jax.random.fold_in(seeds[11], 71), 0),
        "doc_lengths": uneven(seeds[1], NDOC, TOKENS, MAXDOC, 2).astype(jnp.int32),
        "table": gaussian(seeds[2], (NEWV, D), 1.0, 6.0, ((0, 16),)),
        "attn_gain": jnp.clip(1.0 + 0.18 * jax.random.normal(seeds[3], (D,), jnp.float32), 0.1, 1.9),
        "wq": draw_wq(jax.random.fold_in(seeds[11], 71), 0),
        "wkv": draw_wkv(jax.random.fold_in(seeds[11], 71), 0),
        "wo": gaussian(seeds[6], (QH * HD, D), (QH * HD) ** -0.5, 0.09375, ((0, 16),)),
        "mlp_gain": jnp.clip(1.0 + 0.18 * jax.random.normal(seeds[7], (D,), jnp.float32), 0.1, 1.9),
        "w_gate": gaussian(seeds[8], (D, FF), D ** -0.5, 0.09375, ((1, 16),)),
        "w_up": gaussian(seeds[9], (D, FF), D ** -0.5, 0.09375, ((1, 16),)),
        "w_down": gaussian(seeds[10], (FF, D), FF ** -0.5, 0.0625, ((0, 16),)),
    }


EPSILON = 1e-05
ROPE_BASE = 500000.0

def rms_scale(rows_in, gain):
    widened = rows_in.astype(jnp.float32)
    scaled = widened * lax.rsqrt(lax.optimization_barrier(jnp.mean(widened * widened, axis=-1, keepdims=True)) + EPSILON) * gain
    return scaled.astype(jnp.bfloat16)

def document_info(positions, doc_lengths):
    ends = jnp.cumsum(doc_lengths).astype(jnp.int32)
    starts = ends - doc_lengths
    began = starts[None, :] <= positions[:, None]
    documents = lax.optimization_barrier(jnp.sum(began.astype(jnp.int32), axis=1)) - 1
    first_pos = lax.optimization_barrier(jnp.max(jnp.where(began, starts[None, :], 0), axis=1))
    return (documents, positions - first_pos)

def rotate(projected, offsets):
    half_dim = projected.shape[-1] // 2
    inverse = ROPE_BASE ** (-jnp.arange(half_dim, dtype=jnp.float32) * 2.0 / projected.shape[-1])
    angle = offsets.astype(jnp.float32)[:, None] * inverse[None, :]
    cosine = jnp.concatenate([jnp.cos(angle), jnp.cos(angle)], axis=-1)[:, None, :]
    sine = jnp.concatenate([jnp.sin(angle), jnp.sin(angle)], axis=-1)[:, None, :]
    turned = jnp.concatenate([-projected[..., half_dim:], projected[..., :half_dim]], axis=-1)
    return projected * cosine + turned * sine

def tensor_sum(left_rows, right_rows, pieces):
    width = left_rows.shape[1] // pieces

    def add_block(block_index, running):
        left_part = lax.dynamic_slice_in_dim(left_rows, block_index * width, width, 1)
        right_part = lax.dynamic_slice_in_dim(right_rows, block_index * width, width, 0)
        product = jnp.dot(left_part, right_part, preferred_element_type=jnp.float32).astype(jnp.bfloat16)
        return running + lax.optimization_barrier(product).astype(jnp.float32)
    start_value = jnp.zeros((left_rows.shape[0], right_rows.shape[1]), jnp.float32)
    return lax.fori_loop(0, pieces, add_block, start_value)

def reference(ids, doc_lengths, table, attn_gain, wq, wkv, wo, mlp_gain, w_gate, w_up, w_down):
    embedded = table[ids]
    positions = jnp.arange(TOKENS, dtype=jnp.int32)
    documents, offsets = document_info(positions, doc_lengths)
    normed = rms_scale(embedded, attn_gain)
    queries = rotate(jnp.dot(normed, wq, preferred_element_type=jnp.float32).reshape(TOKENS, QH, HD), offsets).astype(jnp.bfloat16)
    projected = jnp.dot(normed, wkv, preferred_element_type=jnp.float32).reshape(TOKENS, KVH, 2, HD)
    keys = rotate(projected[:, :, 0, :], offsets).astype(jnp.bfloat16)
    values = projected[:, :, 1, :].astype(jnp.bfloat16)
    allowed = (positions[None, :] <= positions[:, None]) & (documents[None, :] == documents[:, None])
    group_size = QH // KVH
    score_scale = HD ** (-0.5)

    def one_head(head_index):
        kv_index = head_index // group_size
        query_head = lax.dynamic_index_in_dim(queries, head_index, 1, False).astype(jnp.float32)
        key_head = lax.dynamic_index_in_dim(keys, kv_index, 1, False).astype(jnp.float32)
        value_head = lax.dynamic_index_in_dim(values, kv_index, 1, False)
        scores = jnp.dot(query_head, key_head.T, precision=lax.Precision.HIGHEST) * score_scale
        scores = jnp.where(allowed, scores, -jnp.inf)
        row_max = lax.optimization_barrier(jnp.max(scores, axis=-1, keepdims=True))
        weights = jnp.exp(scores - row_max)
        denominator = lax.optimization_barrier(jnp.sum(weights, axis=-1, keepdims=True))
        summed = jnp.dot(weights.astype(jnp.bfloat16), value_head, preferred_element_type=jnp.float32)
        return summed / denominator
    heads_out = lax.map(one_head, jnp.arange(QH, dtype=jnp.int32))
    attended = jnp.transpose(heads_out, (1, 0, 2)).reshape(TOKENS, QH * HD).astype(jnp.bfloat16)
    stream = (embedded.astype(jnp.float32) + tensor_sum(attended, wo, N_TENSOR)).astype(jnp.bfloat16)
    normed_mlp = rms_scale(stream, mlp_gain)
    gate_part = jnp.dot(normed_mlp, w_gate, preferred_element_type=jnp.float32)
    up_part = jnp.dot(normed_mlp, w_up, preferred_element_type=jnp.float32)
    hidden = (jax.nn.silu(gate_part) * up_part).astype(jnp.bfloat16)
    return (stream.astype(jnp.float32) + tensor_sum(hidden, w_down, N_TENSOR)).astype(jnp.bfloat16)
```

```python
import functools

import jax
import jax.numpy as jnp
from jax import lax
from jax.experimental import pallas as pl
from jax.experimental.pallas import tpu as pltpu
from jax.sharding import PartitionSpec as P

HD = 128
SIDE = 4
GROUP = SIDE * SIDE
SLOTS = 8
MAXDOC = 3072

EPSILON = 1e-05
ROPE_BASE = 500000.0
NEGATIVE = -1e30
MESH = pl.DeviceIdType.MESH
VMEM = pltpu.VMEM
DMA = pltpu.SemaphoreType.DMA
BF16 = jnp.bfloat16
F32 = jnp.float32


def document_info(positions, doc_lengths):
    ends = jnp.cumsum(doc_lengths)
    starts = ends - doc_lengths
    began = starts[None, :] <= positions[:, None]
    first_pos = jnp.max(jnp.where(began, starts[None, :], 0), axis=1)
    return first_pos, positions - first_pos


def rotate(projected, offsets):
    half_dim = projected.shape[-1] // 2
    inverse = ROPE_BASE ** (-jnp.arange(half_dim, dtype=jnp.float32) * 2.0 / projected.shape[-1])
    angle = offsets.astype(jnp.float32)[:, None] * inverse[None, :]
    cosine = jnp.concatenate([jnp.cos(angle), jnp.cos(angle)], axis=-1)[:, None, :]
    sine = jnp.concatenate([jnp.sin(angle), jnp.sin(angle)], axis=-1)[:, None, :]
    turned = jnp.concatenate([-projected[..., half_dim:], projected[..., :half_dim]], axis=-1)
    return projected * cosine + turned * sine


def wrap(v):
    return lax.rem(v + 2 * SIDE, SIDE)


def place(z, x):
    return wrap(z) * SIDE + wrap(x)


def here():
    t = lax.axis_index("tensor")
    return t // SIDE, lax.rem(t, SIDE)


def greet(peers):
    barrier = pltpu.get_barrier_semaphore()
    for peer in peers:
        pl.semaphore_signal(barrier, inc=1, device_id=peer, device_id_type=MESH)
    pl.semaphore_wait(barrier, len(peers))


def torus_peers(z, x):
    return [{"tensor": place(z + a, x + b)} for a, b in ((0, 1), (0, -1), (1, 0), (-1, 0))]


def remote(src, dst, send_sem, recv_sem, peer):
    return pltpu.make_async_remote_copy(
        src_ref=src, dst_ref=dst, send_sem=send_sem, recv_sem=recv_sem,
        device_id=peer, device_id_type=MESH,
    )


def ring_gather(buf, ssem, rsem, z, x):
    half = buf.shape[-1] // 2
    quarter = half // 2
    started = []

    def block(h, first, second):
        return place(z + second, x + first) if h == 0 else place(z + first, x + second)

    def view(h, first, second, part):
        start, size = (h * half, half) if part == 0 else (h * half + (part - 1) * quarter, quarter)
        return buf.at[block(h, first, second), :, pl.ds(start, size)]

    def send(h, n, first, second, part, axis, d):
        ref = view(h, first, second, part)
        peer = {"tensor": block(h, d, 0) if axis == 0 else block(h, 0, d)}
        copy = remote(ref, ref, ssem.at[h, n], rsem.at[h, n], peer)
        copy.start()
        started.append(copy)

    def recv(h, n, first, second, part):
        ref = view(h, first, second, part)
        remote(ref, ref, ssem.at[h, n], rsem.at[h, n], {"tensor": block(h, 1, 0)}).wait_recv()

    offsets = (0, -1, 1, 2)
    for h in range(2):
        send(h, 0, 0, 0, 0, 0, 1)
        send(h, 1, 0, 0, 0, 0, -1)
    for h in range(2):
        send(h, 4, 0, 0, 0, 1, 1)
        send(h, 5, 0, 0, 0, 1, -1)
    for h in range(2):
        recv(h, 0, -1, 0, 0)
        send(h, 2, -1, 0, 1, 0, 1)
        recv(h, 1, 1, 0, 0)
        send(h, 3, 1, 0, 2, 0, -1)
        for n in (1, 2):
            send(h, 4 + 2 * n, offsets[n], 0, 0, 1, 1)
            send(h, 5 + 2 * n, offsets[n], 0, 0, 1, -1)

    def relay(n):
        k = offsets[n]
        for h in range(2):
            recv(h, 4 + 2 * n, k, -1, 0)
            send(h, 12 + 2 * n, k, -1, 1, 1, 1)
            recv(h, 5 + 2 * n, k, 1, 0)
            send(h, 13 + 2 * n, k, 1, 2, 1, -1)

    relay(0)
    for h in range(2):
        recv(h, 2, 2, 0, 1)
        recv(h, 3, 2, 0, 2)
        send(h, 10, 2, 0, 0, 1, 1)
        send(h, 11, 2, 0, 0, 1, -1)
    for n in (1, 2, 3):
        relay(n)
    for n in range(4):
        for h in range(2):
            recv(h, 12 + 2 * n, offsets[n], 2, 1)
            recv(h, 13 + 2 * n, offsets[n], 2, 2)
    for copy in started:
        copy.wait_send()


GATHER_SEMS = [DMA((2, 20)), DMA((2, 20))]


def ring_reduce(part, r1, r2, held, s1, e1, s2, e2, z, x, make, finish):
    half = part.shape[-1] // 2
    quarter = half // 2
    started = []

    def at(h, k, j):
        return (wrap(z + k), wrap(x + j)) if h == 0 else (wrap(z + j), wrap(x + k))

    def mine(h, k, j, q):
        a, b = at(h, k, j)
        return part.at[a, b, :, pl.ds(h * half + q * quarter, quarter)]

    def peer(h, axis, d):
        a, b = at(h, d, 0) if axis == 0 else at(h, 0, d)
        return {"tensor": a * SIDE + b}

    def send1(h, slot, j, src, d):
        copy = remote(src, r1.at[h, slot, j], s1.at[h, slot, j], e1.at[h, slot, j], peer(h, 0, d))
        copy.start()
        started.append(copy)

    def recv1(h, slot, j):
        ref = r1.at[h, slot, j]
        remote(ref, ref, s1.at[h, slot, j], e1.at[h, slot, j], peer(h, 0, 1)).wait_recv()

    def send2(h, slot, src, d):
        copy = remote(src, r2.at[h, slot], s2.at[h, slot], e2.at[h, slot], peer(h, 1, d))
        copy.start()
        started.append(copy)

    def recv2(h, slot):
        ref = r2.at[h, slot]
        remote(ref, ref, s2.at[h, slot], e2.at[h, slot], peer(h, 0, 1)).wait_recv()

    def load(ref):
        return ref[...].astype(F32)

    order = (2, 1, 3, 0)
    for h in range(2):
        make(h, 2)
        for j in order:
            send1(h, 0, j, mine(h, 2, j, 0), 1)
            send1(h, 3, j, mine(h, 2, j, 1), -1)
    for h in range(2):
        make(h, 1)
        for j in order:
            send1(h, 1, j, mine(h, 1, j, 1), 1)
        make(h, 3)
        for j in order:
            send1(h, 4, j, mine(h, 3, j, 0), -1)
    for j in order:
        for h in range(2):
            recv1(h, 0, j)
            r1[h, 0, j] = (load(r1.at[h, 0, j]) + load(mine(h, 1, j, 0))).astype(BF16)
            send1(h, 2, j, r1.at[h, 0, j], 1)
            recv1(h, 3, j)
            r1[h, 3, j] = (load(r1.at[h, 3, j]) + load(mine(h, 3, j, 1))).astype(BF16)
            send1(h, 5, j, r1.at[h, 3, j], -1)
    for h in range(2):
        make(h, 0)

    def arrived(h, j):
        for slot in (1, 4, 2, 5):
            recv1(h, slot, j)

    def summed(h, j, q):
        a, b = ((2, 4), (1, 5))[q]
        return load(mine(h, 0, j, q)) + load(r1.at[h, a, j]) + load(r1.at[h, b, j])

    for h in range(2):
        arrived(h, 2)
        for q, slot, d in ((0, 0, 1), (1, 3, -1)):
            held[h, 0, q] = summed(h, 2, q).astype(BF16)
            send2(h, slot, held.at[h, 0, q], d)
    for h in range(2):
        arrived(h, 1)
        held[h, 1, 1] = summed(h, 1, 1).astype(BF16)
        send2(h, 1, held.at[h, 1, 1], 1)
        arrived(h, 3)
        held[h, 2, 0] = summed(h, 3, 0).astype(BF16)
        send2(h, 4, held.at[h, 2, 0], -1)
    for h in range(2):
        recv2(h, 0)
        held[h, 1, 0] = (summed(h, 1, 0) + load(r2.at[h, 0])).astype(BF16)
        send2(h, 2, held.at[h, 1, 0], 1)
        recv2(h, 3)
        held[h, 2, 1] = (summed(h, 3, 1) + load(r2.at[h, 3])).astype(BF16)
        send2(h, 5, held.at[h, 2, 1], -1)
    for h in range(2):
        arrived(h, 0)
        for slot in (1, 4, 2, 5):
            recv2(h, slot)
        for q in range(2):
            a, b = ((2, 4), (1, 5))[q]
            value = summed(h, 0, q) + load(r2.at[h, a]) + load(r2.at[h, b])
            finish(pl.ds(h * half + q * quarter, quarter), value)
    for copy in started:
        copy.wait_send()


def reduce_scratch(rows, width):
    quarter = width // 4
    return [
        VMEM((SIDE, SIDE, rows, width), BF16),
        VMEM((2, 6, SIDE, rows, quarter), BF16),
        VMEM((2, 6, rows, quarter), BF16),
        VMEM((2, 3, 2, rows, quarter), BF16),
        DMA((2, 6, SIDE)), DMA((2, 6, SIDE)), DMA((2, 6)), DMA((2, 6)),
    ]


def products(a_ref, w_ref, part, z, x):
    rows, width = part.shape[2], part.shape[3]
    half = width // 2
    step = min(512, half)

    def make(h, k):
        def run(blocks):
            lhs = jnp.concatenate(
                [a_ref[pl.ds(pl.multiple_of((a * SIDE + b) * rows, 16), rows), :] for a, b in blocks], axis=0
            )

            def column(c, carry):
                cols = pl.ds(pl.multiple_of(h * half + c * step, step), step)
                out = jnp.dot(lhs, w_ref[:, cols], preferred_element_type=F32).astype(BF16)
                for n, (a, b) in enumerate(blocks):
                    part[a, b, :, cols] = out[n * rows:(n + 1) * rows]
                return carry

            lax.fori_loop(0, half // step, column, 0)

        if h == 0:
            run([(wrap(z + k), b) for b in range(SIDE)])
        else:
            run([(a, wrap(x + k)) for a in range(SIDE)])

    return make


def normalize(rows, gain):
    scale = lax.rsqrt(jnp.mean(rows * rows, axis=-1, keepdims=True) + EPSILON)
    return (rows * scale * gain).astype(BF16)


def share_ids_kernel(ids_ref, out_ref, ssem, rsem):
    t = lax.axis_index("tensor")
    peers = [lax.rem(t + n, GROUP) for n in range(1, GROUP)]
    greet([{"tensor": p} for p in peers])
    copies = []
    for n, p in enumerate(peers):
        copy = remote(ids_ref, out_ref.at[t], ssem.at[n], rsem.at[n], {"tensor": p})
        copy.start()
        copies.append(copy)
    out_ref[t] = ids_ref[...]
    for n in range(GROUP - 1):
        source = lax.rem(t + GROUP - 1 - n, GROUP)
        remote(ids_ref, out_ref.at[source], ssem.at[n], rsem.at[n], {"tensor": source}).wait_recv()
    for copy in copies:
        copy.wait_send()


def share_ids(ids):
    rows = ids.shape[0]
    padded = jnp.pad(ids.reshape(1, rows), ((0, 7), (0, 128 - rows)))
    out = pl.pallas_call(
        share_ids_kernel,
        out_shape=jax.ShapeDtypeStruct((GROUP, 8, 128), jnp.int32),
        in_specs=[pl.BlockSpec(memory_space=VMEM)],
        out_specs=pl.BlockSpec(memory_space=VMEM),
        scratch_shapes=[DMA((GROUP - 1,)), DMA((GROUP - 1,))],
        compiler_params=pltpu.CompilerParams(collective_id=0, has_side_effects=True),
        name="share_ids",
    )(padded)
    return out[:, 0, :rows]


def embed_kernel(found_ref, source_ref, gain_ref, emb_ref, all_ref, recv, xs, xr, gs, gr):
    z, x = here()
    t = lax.axis_index("tensor")
    peers = [lax.rem(t + n, GROUP) for n in range(1, GROUP)]
    greet([{"tensor": p} for p in peers])
    copies = []
    for n, p in enumerate(peers):
        copy = remote(found_ref.at[p], recv.at[t], xs.at[n], xr.at[n], {"tensor": p})
        copy.start()
        copies.append(copy)
    recv[t] = found_ref[t]
    for n in range(GROUP - 1):
        source = lax.rem(t + GROUP - 1 - n, GROUP)
        remote(found_ref.at[source], recv.at[source], xs.at[n], xr.at[n], {"tensor": source}).wait_recv()
    rows, width = emb_ref.shape
    lanes = lax.broadcasted_iota(jnp.int32, (rows, GROUP * SLOTS), 1)
    chosen = jnp.where(source_ref[...] == lanes, 1.0, 0.0).astype(BF16)
    step = width // 4
    total = jnp.zeros((rows, 1), F32)
    for c in range(4):
        cols = pl.ds(c * step, step)
        block = recv[:, :, cols].reshape(GROUP * SLOTS, step)
        picked = jnp.dot(chosen, block, preferred_element_type=F32)
        emb_ref[:, cols] = picked.astype(BF16)
        total += jnp.sum(picked * picked, axis=-1, keepdims=True)
    scale = lax.rsqrt(total / width + EPSILON)
    for c in range(4):
        cols = pl.ds(c * step, step)
        all_ref[t, :, cols] = (emb_ref[:, cols].astype(F32) * scale * gain_ref[:, cols]).astype(BF16)
    ring_gather(all_ref, gs, gr, z, x)
    for copy in copies:
        copy.wait_send()


def embed_and_gather(found, source, gain):
    width = found.shape[-1]
    rows = source.shape[0]
    return pl.pallas_call(
        embed_kernel,
        out_shape=(
            jax.ShapeDtypeStruct((rows, width), BF16),
            jax.ShapeDtypeStruct((GROUP, rows, width), BF16),
        ),
        in_specs=[pl.BlockSpec(memory_space=VMEM)] * 3,
        out_specs=(pl.BlockSpec(memory_space=VMEM),) * 2,
        scratch_shapes=[
            VMEM((GROUP, SLOTS, width), BF16), DMA((GROUP - 1,)), DMA((GROUP - 1,)), *GATHER_SEMS,
        ],
        compiler_params=pltpu.CompilerParams(
            collective_id=1, has_side_effects=True, vmem_limit_bytes=40 * 2**20
        ),
        name="embed_and_gather",
    )(found, source, gain)


def share_kv_kernel(own_ref, win_ref, relay, ssem, rsem):
    t = lax.axis_index("tensor")
    r = lax.axis_index("dp")
    y, c = r // 2, lax.rem(r, 2)
    kind = lax.rem(t, 2)
    partner = {"tensor": t + 1 - 2 * kind}
    up = {"dp": lax.rem(y + 1, SIDE) * 2 + c}
    down = {"dp": lax.rem(y + SIDE - 1, SIDE) * 2 + c}
    other = {"dp": y * 2 + 1 - c}
    greet([partner, up, down, other])

    def copy(n, src, dst, peer):
        return remote(src, dst, ssem.at[n], rsem.at[n], peer)

    swap = copy(0, own_ref, win_ref.at[4, kind], partner)
    swap.start()
    win_ref[4, kind] = own_ref[...]
    swap_in = copy(0, own_ref, win_ref.at[4, 1 - kind], partner)
    up_key = copy(1, win_ref.at[4, 0], win_ref.at[2, 0], up)
    up_value = copy(2, win_ref.at[4, 1], win_ref.at[2, 1], up)
    far_key = copy(3, win_ref.at[2, 0], win_ref.at[0, 0], up)
    down_value = copy(4, win_ref.at[4, 1], relay, down)
    far_value = copy(5, relay, win_ref.at[0, 1], down)
    has_up, has_far = y < SIDE - 1, y < SIDE - 2
    got_up, got_far = y > 0, y > 1
    relays = (y == SIDE - 1) | (y == 0)
    swap_in.wait_recv()

    @pl.when(has_far)
    def _():
        down_value.start()

    @pl.when(has_up)
    def _():
        up_key.start()
        up_value.start()

    near = [copy(6 + k, win_ref.at[4, k], win_ref.at[3, k], other) for k in range(2)]
    for k in range(2):
        @pl.when(c == 0)
        def _():
            near[k].start()

    @pl.when(relays)
    def _():
        down_value.wait_recv()
        far_value.start()

    @pl.when(got_up)
    def _():
        up_key.wait_recv()

        @pl.when(has_up)
        def _():
            far_key.start()

        up_value.wait_recv()

    cross0 = [copy(8 + k, win_ref.at[2, k], win_ref.at[1, k], other) for k in range(2)]
    cross1 = [copy(8 + k, win_ref.at[2, k], win_ref.at[3, k], other) for k in range(2)]

    @pl.when(got_up & (c == 0))
    def _():
        for k in range(2):
            cross0[k].start()

    @pl.when(got_up & (c == 1))
    def _():
        for k in range(2):
            cross1[k].start()

    far1 = [copy(10 + k, win_ref.at[0, k], win_ref.at[1, k], other) for k in range(2)]

    @pl.when(got_far)
    def _():
        far_key.wait_recv()
        far_value.wait_recv()

        @pl.when(c == 1)
        def _():
            for k in range(2):
                far1[k].start()

        @pl.when(c == 0)
        def _():
            for k in range(2):
                far1[k].wait_recv()

        @pl.when(c == 1)
        def _():
            for k in range(2):
                far1[k].wait_send()

    @pl.when(c == 1)
    def _():
        for k in range(2):
            near[k].wait_recv()

    @pl.when(c == 0)
    def _():
        for k in range(2):
            near[k].wait_send()

    @pl.when(got_up & (c == 0))
    def _():
        for k in range(2):
            cross1[k].wait_recv()
            cross0[k].wait_send()

    @pl.when(got_up & (c == 1))
    def _():
        for k in range(2):
            cross0[k].wait_recv()
            cross1[k].wait_send()

    @pl.when(has_far)
    def _():
        down_value.wait_send()

    @pl.when(has_up)
    def _():
        up_key.wait_send()
        up_value.wait_send()

    @pl.when(relays)
    def _():
        far_value.wait_send()

    @pl.when(got_up & has_up)
    def _():
        far_key.wait_send()

    swap.wait_send()


def share_kv(own):
    rows, width = own.shape
    return pl.pallas_call(
        share_kv_kernel,
        out_shape=jax.ShapeDtypeStruct((5, 2, rows, width), BF16),
        in_specs=[pl.BlockSpec(memory_space=VMEM)],
        out_specs=pl.BlockSpec(memory_space=VMEM),
        scratch_shapes=[VMEM((rows, width), BF16), DMA((12,)), DMA((12,))],
        compiler_params=pltpu.CompilerParams(
            collective_id=2, has_side_effects=True, vmem_limit_bytes=24 * 2**20
        ),
        name="share_kv",
    )(own)


QB = 256
KB = 256


def attention_kernel(low_ref, q_ref, first_ref, win_ref, out_ref, m_ref, l_ref, acc_ref):
    rows = q_ref.shape[0]
    per_range = rows // KB
    scale = HD ** (-0.5)
    for i in range(rows // QB):
        span = pl.ds(i * QB, QB)
        q = jnp.concatenate([q_ref[span, :HD], q_ref[span, HD:]], axis=0)
        first = first_ref[span, :]
        first = jnp.concatenate([first, first], axis=0)
        place_q = lax.broadcasted_iota(jnp.int32, (QB, 1), 0) + (4 * rows + i * QB)
        place_q = jnp.concatenate([place_q, place_q], axis=0)
        m_ref[...] = jnp.full_like(m_ref, NEGATIVE)
        l_ref[...] = jnp.zeros_like(l_ref)
        acc_ref[...] = jnp.zeros_like(acc_ref)

        def body(b, carry):
            w = b // per_range
            keys = pl.ds(pl.multiple_of((b - w * per_range) * KB, KB), KB)
            k = win_ref[w, 0, keys, :]
            v = win_ref[w, 1, keys, :]
            s = lax.dot_general(q, k, (((1,), (1,)), ((), ())), preferred_element_type=F32) * scale
            place_k = lax.broadcasted_iota(jnp.int32, (1, KB), 1) + b * KB
            s = jnp.where((place_k <= place_q) & (place_k >= first), s, NEGATIVE)
            m_old = m_ref[...]
            m_new = jnp.maximum(m_old, jnp.max(s, axis=-1, keepdims=True))
            decay = jnp.exp(m_old - m_new)
            p = jnp.exp(s - m_new)
            l_ref[...] = l_ref[...] * decay + jnp.sum(p, axis=-1, keepdims=True)
            acc_ref[...] = acc_ref[...] * decay + jnp.dot(p.astype(BF16), v, preferred_element_type=F32)
            m_ref[...] = m_new
            return carry

        lax.fori_loop(low_ref[i], 4 * per_range + (i + 1) * QB // KB, body, 0)
        out = (acc_ref[...] / l_ref[...]).astype(BF16)
        out_ref[span, :HD] = out[:QB]
        out_ref[span, HD:] = out[QB:]


def attend(low, queries, first, window):
    rows, width = queries.shape
    return pl.pallas_call(
        attention_kernel,
        out_shape=jax.ShapeDtypeStruct((rows, width), BF16),
        in_specs=[pl.BlockSpec(memory_space=pltpu.SMEM)] + [pl.BlockSpec(memory_space=VMEM)] * 3,
        out_specs=pl.BlockSpec(memory_space=VMEM),
        scratch_shapes=[VMEM((2 * QB, 1), F32), VMEM((2 * QB, 1), F32), VMEM((2 * QB, HD), F32)],
        compiler_params=pltpu.CompilerParams(vmem_limit_bytes=32 * 2**20),
        name="attend",
    )(low, queries, first, window)


def mix_kernel(att_ref, wo_ref, emb_ref, gain_ref, stream_ref, all_ref, part, r1, r2, held, s1, e1, s2, e2, gs, gr):
    z, x = here()
    t = lax.axis_index("tensor")
    greet(torus_peers(z, x))

    def finish(cols, value):
        stream_ref[:, cols] = (emb_ref[:, cols].astype(F32) + value).astype(BF16)

    ring_reduce(part, r1, r2, held, s1, e1, s2, e2, z, x, products(att_ref, wo_ref, part, z, x), finish)
    all_ref[t] = normalize(stream_ref[...].astype(F32), gain_ref[...])
    ring_gather(all_ref, gs, gr, z, x)


def mix_and_gather(attended, wo, embedded, gain):
    rows, width = embedded.shape
    return pl.pallas_call(
        mix_kernel,
        out_shape=(
            jax.ShapeDtypeStruct((rows, width), BF16),
            jax.ShapeDtypeStruct((GROUP, rows, width), BF16),
        ),
        in_specs=[pl.BlockSpec(memory_space=VMEM)] * 4,
        out_specs=(pl.BlockSpec(memory_space=VMEM),) * 2,
        scratch_shapes=[*reduce_scratch(rows, width), *GATHER_SEMS],
        compiler_params=pltpu.CompilerParams(
            collective_id=3, has_side_effects=True, vmem_limit_bytes=48 * 2**20
        ),
        name="mix_and_gather",
    )(attended, wo, embedded, gain)


def down_kernel(hid_ref, w_ref, stream_ref, out_ref, part, r1, r2, held, s1, e1, s2, e2):
    z, x = here()
    greet(torus_peers(z, x))

    def finish(cols, value):
        out_ref[:, cols] = (stream_ref[:, cols].astype(F32) + value).astype(BF16)

    ring_reduce(part, r1, r2, held, s1, e1, s2, e2, z, x, products(hid_ref, w_ref, part, z, x), finish)


def down_and_add(hidden, w_down, stream):
    rows, width = stream.shape
    return pl.pallas_call(
        down_kernel,
        out_shape=jax.ShapeDtypeStruct((rows, width), BF16),
        in_specs=[pl.BlockSpec(memory_space=VMEM)] * 3,
        out_specs=pl.BlockSpec(memory_space=VMEM),
        scratch_shapes=reduce_scratch(rows, width),
        compiler_params=pltpu.CompilerParams(
            collective_id=4, has_side_effects=True, vmem_limit_bytes=48 * 2**20
        ),
        name="down_and_add",
    )(hidden, w_down, stream)


def find_rows(ids, range_ids, table):
    t = lax.axis_index("tensor")
    owned = table.shape[0]
    count = ids.shape[0]
    inside = range_ids // owned == t
    earlier = jnp.arange(count)[:, None] < jnp.arange(count)[None, :]
    rank = jnp.sum(jnp.where(inside[:, :, None] & earlier[None], 1, 0), axis=1)
    local_rows = range_ids - t * owned
    wanted = inside[:, None, :] & (rank[:, None, :] == jnp.arange(SLOTS)[None, :, None])
    rows = jnp.sum(jnp.where(wanted, local_rows[:, None, :], 0), axis=2)
    owner = ids // owned
    own_rank = jnp.sum(jnp.where((owner[:, None] == owner[None, :]) & earlier, 1, 0), axis=0)
    found = jnp.take(table, rows.reshape(-1), axis=0).reshape(GROUP, SLOTS, -1)
    return found, (owner * SLOTS + own_rank)[:, None]


def local(ids, doc_lengths, table, attn_gain, wq, wkv, wo, mlp_gain, w_gate, w_up, w_down):
    t = lax.axis_index("tensor")
    r = lax.axis_index("dp")
    own_rows = ids.shape[0]
    width = table.shape[1]
    tok_range = own_rows * GROUP
    q_width = wq.shape[1]
    found, source = find_rows(ids, share_ids(ids), table)
    embedded, normed = embed_and_gather(found, source, attn_gain[None, :])
    normed = normed.reshape(tok_range, width)
    positions = r * tok_range + jnp.arange(tok_range, dtype=jnp.int32)
    first_pos, offsets = document_info(positions, doc_lengths)
    queries = jnp.dot(normed, wq, preferred_element_type=F32).reshape(tok_range, -1, HD)
    queries = rotate(queries, offsets).reshape(tok_range, q_width).astype(BF16)
    pairs = jnp.dot(normed, wkv, preferred_element_type=F32)
    turned = rotate(pairs[:, None, :], offsets)[:, 0, :]
    pairs = jnp.where(t % 2 == 0, turned, pairs).astype(BF16)
    window = share_kv(pairs)
    first = first_pos - (r - 4) * tok_range
    low = first[::QB] // KB
    attended = attend(low, queries, first[:, None], window)
    stream, normed_mlp = mix_and_gather(attended, wo, embedded, mlp_gain[None, :])
    normed_mlp = normed_mlp.reshape(tok_range, width)
    gate_part = jnp.dot(normed_mlp, w_gate, preferred_element_type=F32)
    up_part = jnp.dot(normed_mlp, w_up, preferred_element_type=F32)
    hidden = (jax.nn.silu(gate_part) * up_part).astype(BF16)
    return down_and_add(hidden, w_down, stream)


def solution(mesh):
    placed = (
        P(("dp", "tensor")),
        P(),
        P("tensor", None),
        P(),
        P(None, "tensor"),
        P(None, "tensor"),
        P("tensor", None),
        P(),
        P(None, "tensor"),
        P(None, "tensor"),
        P("tensor", None),
    )
    return jax.shard_map(
        local, mesh=mesh, in_specs=placed, out_specs=P(("dp", "tensor"), None), check_vma=False
    )
```

```python
import jax
import jax.numpy as jnp
from jax import lax
from jax.experimental import pallas as pl
from jax.experimental.pallas import tpu as pltpu
from jax.sharding import PartitionSpec as P

HD = 128
SIDE = 4
GROUP = SIDE * SIDE
SLOTS = 8

EPSILON = 1e-05
ROPE_BASE = 500000.0
NEGATIVE = -1e30
EXP_SCALE = HD ** (-0.5) * 1.4426950408889634
MESH = pl.DeviceIdType.MESH
VMEM = pltpu.VMEM
DMA = pltpu.SemaphoreType.DMA
BF16 = jnp.bfloat16
F32 = jnp.float32


def document_info(positions, doc_lengths):
    ends = jnp.cumsum(doc_lengths)
    starts = ends - doc_lengths
    began = starts[None, :] <= positions[:, None]
    first_pos = jnp.max(jnp.where(began, starts[None, :], 0), axis=1)
    return first_pos, positions - first_pos


def turns(offsets):
    half_dim = HD // 2
    inverse = ROPE_BASE ** (-jnp.arange(half_dim, dtype=jnp.float32) * 2.0 / HD)
    angle = offsets.astype(jnp.float32)[:, None] * inverse[None, :]
    cosine, sine = jnp.cos(angle), jnp.sin(angle)
    return jnp.concatenate([cosine, cosine], axis=-1), jnp.concatenate([-sine, sine], axis=-1)


def wrap(v):
    return lax.rem(v + 2 * SIDE, SIDE)


def place(z, x):
    return wrap(z) * SIDE + wrap(x)


def here():
    t = lax.axis_index("tensor")
    return t // SIDE, lax.rem(t, SIDE)


def greet(peers):
    barrier = pltpu.get_barrier_semaphore()
    for peer in peers:
        pl.semaphore_signal(barrier, inc=1, device_id=peer, device_id_type=MESH)
    pl.semaphore_wait(barrier, len(peers))


def torus_peers(z, x):
    return [{"tensor": place(z + a, x + b)} for a, b in ((0, 1), (0, -1), (1, 0), (-1, 0))]


def remote(src, dst, send_sem, recv_sem, peer):
    return pltpu.make_async_remote_copy(
        src_ref=src, dst_ref=dst, send_sem=send_sem, recv_sem=recv_sem,
        device_id=peer, device_id_type=MESH,
    )


def ring_gather(buf, ssem, rsem, z, x, ready):
    half = buf.shape[-1] // 2
    quarter = half // 2
    started = []

    def block(h, first, second):
        return place(z + second, x + first) if h == 0 else place(z + first, x + second)

    def view(h, first, second, part):
        start, size = (h * half, half) if part == 0 else (h * half + (part - 1) * quarter, quarter)
        return buf.at[block(h, first, second), :, pl.ds(start, size)]

    def send(h, n, first, second, part, axis, d):
        ref = view(h, first, second, part)
        peer = {"tensor": block(h, d, 0) if axis == 0 else block(h, 0, d)}
        copy = remote(ref, ref, ssem.at[h, n], rsem.at[h, n], peer)
        copy.start()
        started.append(copy)

    def recv(h, n, first, second, part):
        ref = view(h, first, second, part)
        remote(ref, ref, ssem.at[h, n], rsem.at[h, n], {"tensor": block(h, 1, 0)}).wait_recv()

    offsets = (0, -1, 1, 2)
    for h in range(2):
        send(h, 0, 0, 0, 0, 0, 1)
        send(h, 1, 0, 0, 0, 0, -1)
    for h in range(2):
        send(h, 4, 0, 0, 0, 1, 1)
        send(h, 5, 0, 0, 0, 1, -1)
    for h in range(2):
        recv(h, 0, -1, 0, 0)
        send(h, 2, -1, 0, 1, 0, 1)
        recv(h, 1, 1, 0, 0)
        send(h, 3, 1, 0, 2, 0, -1)
        for n in (1, 2):
            send(h, 4 + 2 * n, offsets[n], 0, 0, 1, 1)
            send(h, 5 + 2 * n, offsets[n], 0, 0, 1, -1)

    def relay(n):
        k = offsets[n]
        for h in range(2):
            recv(h, 4 + 2 * n, k, -1, 0)
            send(h, 12 + 2 * n, k, -1, 1, 1, 1)
            recv(h, 5 + 2 * n, k, 1, 0)
            send(h, 13 + 2 * n, k, 1, 2, 1, -1)

    relay(0)
    for h in range(2):
        recv(h, 2, 2, 0, 1)
        recv(h, 3, 2, 0, 2)
        send(h, 10, 2, 0, 0, 1, 1)
        send(h, 11, 2, 0, 0, 1, -1)
    relay(1)
    relay(2)

    def far(h, n):
        recv(h, 12 + 2 * n, offsets[n], 2, 1)
        recv(h, 13 + 2 * n, offsets[n], 2, 2)

    far(1, 0)
    ready(0)
    relay(3)
    far(1, 1)
    ready(-1)
    far(1, 2)
    ready(1)
    for n in range(4):
        far(0, n)
    far(1, 3)
    ready(2)
    for copy in started:
        copy.wait_send()


GATHER_SEMS = [DMA((2, 20)), DMA((2, 20))]


def ring_reduce(part, r1, r2, held, s1, e1, s2, e2, z, x, make, finish):
    half = part.shape[-1] // 2
    quarter = half // 2
    started = []

    def at(h, k, j):
        return (wrap(z + k), wrap(x + j)) if h == 0 else (wrap(z + j), wrap(x + k))

    def mine(h, k, j, q):
        a, b = at(h, k, j)
        return part.at[a, b, :, pl.ds(h * half + q * quarter, quarter)]

    def peer(h, axis, d):
        a, b = at(h, d, 0) if axis == 0 else at(h, 0, d)
        return {"tensor": a * SIDE + b}

    def send1(h, slot, j, src, d):
        copy = remote(src, r1.at[h, slot, j], s1.at[h, slot, j], e1.at[h, slot, j], peer(h, 0, d))
        copy.start()
        started.append(copy)

    def recv1(h, slot, j):
        ref = r1.at[h, slot, j]
        remote(ref, ref, s1.at[h, slot, j], e1.at[h, slot, j], peer(h, 0, 1)).wait_recv()

    def send2(h, slot, src, d):
        copy = remote(src, r2.at[h, slot], s2.at[h, slot], e2.at[h, slot], peer(h, 1, d))
        copy.start()
        started.append(copy)

    def recv2(h, slot):
        ref = r2.at[h, slot]
        remote(ref, ref, s2.at[h, slot], e2.at[h, slot], peer(h, 0, 1)).wait_recv()

    def load(ref):
        return ref[...].astype(F32)

    order = (2, 1, 3, 0)
    for h in range(2):
        make(h, 2)
        for j in order:
            send1(h, 0, j, mine(h, 2, j, 0), 1)
            send1(h, 3, j, mine(h, 2, j, 1), -1)
    for h in range(2):
        make(h, 1)
        for j in order:
            send1(h, 1, j, mine(h, 1, j, 1), 1)
        make(h, 3)
        for j in order:
            send1(h, 4, j, mine(h, 3, j, 0), -1)
    for j in order:
        for h in range(2):
            recv1(h, 0, j)
            r1[h, 0, j] = (load(r1.at[h, 0, j]) + load(mine(h, 1, j, 0))).astype(BF16)
            send1(h, 2, j, r1.at[h, 0, j], 1)
            recv1(h, 3, j)
            r1[h, 3, j] = (load(r1.at[h, 3, j]) + load(mine(h, 3, j, 1))).astype(BF16)
            send1(h, 5, j, r1.at[h, 3, j], -1)
    for h in range(2):
        make(h, 0)

    def arrived(h, j):
        for slot in (1, 4, 2, 5):
            recv1(h, slot, j)

    def summed(h, j, q):
        a, b = ((2, 4), (1, 5))[q]
        return load(mine(h, 0, j, q)) + load(r1.at[h, a, j]) + load(r1.at[h, b, j])

    for h in range(2):
        arrived(h, 2)
        for q, slot, d in ((0, 0, 1), (1, 3, -1)):
            held[h, 0, q] = summed(h, 2, q).astype(BF16)
            send2(h, slot, held.at[h, 0, q], d)
    for h in range(2):
        arrived(h, 1)
        held[h, 1, 1] = summed(h, 1, 1).astype(BF16)
        send2(h, 1, held.at[h, 1, 1], 1)
        arrived(h, 3)
        held[h, 2, 0] = summed(h, 3, 0).astype(BF16)
        send2(h, 4, held.at[h, 2, 0], -1)
    for h in range(2):
        recv2(h, 0)
        held[h, 1, 0] = (summed(h, 1, 0) + load(r2.at[h, 0])).astype(BF16)
        send2(h, 2, held.at[h, 1, 0], 1)
        recv2(h, 3)
        held[h, 2, 1] = (summed(h, 3, 1) + load(r2.at[h, 3])).astype(BF16)
        send2(h, 5, held.at[h, 2, 1], -1)
    for h in range(2):
        arrived(h, 0)
        for slot in (1, 4, 2, 5):
            recv2(h, slot)
        for q in range(2):
            a, b = ((2, 4), (1, 5))[q]
            value = summed(h, 0, q) + load(r2.at[h, a]) + load(r2.at[h, b])
            finish(pl.ds(h * half + q * quarter, quarter), value)
    for copy in started:
        copy.wait_send()


def reduce_scratch(rows, width):
    quarter = width // 4
    return [
        VMEM((SIDE, SIDE, rows, width), BF16),
        VMEM((2, 6, SIDE, rows, quarter), BF16),
        VMEM((2, 6, rows, quarter), BF16),
        VMEM((2, 3, 2, rows, quarter), BF16),
        DMA((2, 6, SIDE)), DMA((2, 6, SIDE)), DMA((2, 6)), DMA((2, 6)),
    ]


def products(a_ref, w_ref, part, z, x):
    rows, width = part.shape[2], part.shape[3]
    half = width // 2
    step = min(512, half)

    def make(h, k):
        def run(blocks):
            lhs = jnp.concatenate(
                [a_ref[pl.ds(pl.multiple_of((a * SIDE + b) * rows, 16), rows), :] for a, b in blocks], axis=0
            )

            def column(c, carry):
                cols = pl.ds(pl.multiple_of(h * half + c * step, step), step)
                out = jnp.dot(lhs, w_ref[:, cols], preferred_element_type=F32).astype(BF16)
                for n, (a, b) in enumerate(blocks):
                    part[a, b, :, cols] = out[n * rows:(n + 1) * rows]
                return carry

            lax.fori_loop(0, half // step, column, 0)

        if h == 0:
            run([(wrap(z + k), b) for b in range(SIDE)])
        else:
            run([(a, wrap(x + k)) for a in range(SIDE)])

    return make


def normalize(rows, gain):
    scale = lax.rsqrt(jnp.mean(rows * rows, axis=-1, keepdims=True) + EPSILON)
    return (rows * scale * gain).astype(BF16)


def row_group(all_ref, z, dz):
    rows, width = all_ref.shape[1:]
    zz = wrap(z + dz)
    lhs = all_ref[pl.ds(zz * SIDE, SIDE)].reshape(SIDE * rows, width)
    return lhs, pl.ds(pl.multiple_of(zz * SIDE * rows, 16), SIDE * rows)


def front_kernel(ids_ref, source_ref, gain_ref, cos_ref, sin_ref, table_hbm, wq_hbm, wkv_hbm,
                 emb_ref, q_ref, pair_ref,
                 table, wq, wkv, all_ids, found, recv, all_ref, load_sem, ks, kr, xs, xr, gs, gr):
    z, x = here()
    t = lax.axis_index("tensor")
    loads = [
        pltpu.make_async_copy(src, dst, load_sem.at[n])
        for n, (src, dst) in enumerate(((table_hbm, table), (wq_hbm, wq), (wkv_hbm, wkv)))
    ]
    for load in loads:
        load.start()
    peers = [lax.rem(t + n, GROUP) for n in range(1, GROUP)]
    sources = [lax.rem(t + GROUP - n, GROUP) for n in range(1, GROUP)]
    greet([{"tensor": p} for p in peers])
    copies = []
    for n, p in enumerate(peers):
        copy = remote(ids_ref, all_ids.at[t], ks.at[n], kr.at[n], {"tensor": p})
        copy.start()
        copies.append(copy)
    all_ids[t] = ids_ref[...]
    for n, p in enumerate(sources):
        remote(ids_ref, all_ids.at[p], ks.at[n], kr.at[n], {"tensor": p}).wait_recv()
    slots = GROUP * SLOTS
    owned, width = table.shape
    ids = all_ids[...].reshape(slots, 128)
    local_rows = ids - t * owned
    inside = (local_rows >= 0) & (local_rows < owned)
    square = (128, 128)
    earlier = lax.broadcasted_iota(jnp.int32, square, 0) < lax.broadcasted_iota(jnp.int32, square, 1)
    rank = jnp.dot(
        jnp.where(inside, 1.0, 0.0).astype(BF16), jnp.where(earlier, 1.0, 0.0).astype(BF16),
        preferred_element_type=F32,
    )
    slot = lax.rem(lax.broadcasted_iota(jnp.int32, (slots, 128), 0), SLOTS).astype(F32)
    wanted = jnp.sum(
        jnp.where(inside & (rank == slot), local_rows.astype(F32), 0.0), axis=1, keepdims=True
    )
    pick = lax.broadcasted_iota(jnp.int32, (slots, owned), 1).astype(F32) == wanted
    pick = jnp.where(pick, 1.0, 0.0).astype(BF16)
    loads[0].wait()
    parts = 2
    step = width // parts
    for c in range(parts):
        def fetch(b, carry):
            cols = pl.ds(pl.multiple_of(c * step + b * 512, 512), 512)
            rows = jnp.dot(pick, table[:, cols], preferred_element_type=F32).astype(BF16)
            found[:, :, cols] = rows.reshape(GROUP, SLOTS, 512)
            return carry

        lax.fori_loop(0, step // 512, fetch, 0)
        cols = pl.ds(c * step, step)
        for n, p in enumerate(peers):
            copy = remote(found.at[p, :, cols], recv.at[t, :, cols], xs.at[c, n], xr.at[c, n], {"tensor": p})
            copy.start()
            copies.append(copy)
        recv[t, :, cols] = found[t, :, cols]
    rows = emb_ref.shape[0]
    lanes = lax.broadcasted_iota(jnp.int32, (rows, slots), 1)
    chosen = jnp.where(source_ref[...] == lanes, 1.0, 0.0).astype(BF16)
    total = jnp.zeros((rows, 1), F32)
    for c in range(parts):
        cols = pl.ds(c * step, step)
        for n, p in enumerate(sources):
            ref = recv.at[p, :, cols]
            remote(ref, ref, xs.at[c, n], xr.at[c, n], {"tensor": p}).wait_recv()
        for b in range(step // 1024):
            cols = pl.ds(c * step + b * 1024, 1024)
            picked = jnp.dot(chosen, recv[:, :, cols].reshape(slots, 1024), preferred_element_type=F32)
            emb_ref[:, cols] = picked.astype(BF16)
            total += jnp.sum(picked * picked, axis=-1, keepdims=True)
    scale = lax.rsqrt(total / width + EPSILON)
    for b in range(width // 1024):
        cols = pl.ds(b * 1024, 1024)
        all_ref[t, :, cols] = (emb_ref[:, cols].astype(F32) * scale * gain_ref[:, cols]).astype(BF16)
    loads[1].wait()
    loads[2].wait()
    keys_here = lax.rem(t, 2) == 0

    def project(dz):
        lhs, span = row_group(all_ref, z, dz)
        cos, sin = cos_ref[span, :], sin_ref[span, :]
        queries = jnp.dot(lhs, wq[...], preferred_element_type=F32)
        for h in range(queries.shape[1] // HD):
            head = queries[:, h * HD:(h + 1) * HD]
            q_ref[span, h * HD:(h + 1) * HD] = (head * cos + pltpu.roll(head, HD // 2, 1) * sin).astype(BF16)
        pair = jnp.dot(lhs, wkv[...], preferred_element_type=F32)
        turned = pair * cos + pltpu.roll(pair, HD // 2, 1) * sin
        pair_ref[span, :] = jnp.where(keys_here, turned, pair).astype(BF16)

    ring_gather(all_ref, gs, gr, z, x, project)
    for copy in copies:
        copy.wait_send()


def front(ids, source, gain, cos, sin, table, wq, wkv):
    rows, width = ids.shape[0], table.shape[1]
    span = rows * GROUP
    padded = jnp.broadcast_to(jnp.pad(ids, (0, 128 - rows), constant_values=-1)[None, :], (8, 128))
    whole = pl.BlockSpec(memory_space=VMEM)
    outside = pl.BlockSpec(memory_space=pl.ANY)
    return pl.pallas_call(
        front_kernel,
        out_shape=(
            jax.ShapeDtypeStruct((rows, width), BF16),
            jax.ShapeDtypeStruct((span, wq.shape[1]), BF16),
            jax.ShapeDtypeStruct((span, wkv.shape[1]), BF16),
        ),
        in_specs=[whole] * 5 + [outside] * 3,
        out_specs=(whole,) * 3,
        scratch_shapes=[
            VMEM(table.shape, BF16), VMEM(wq.shape, BF16), VMEM(wkv.shape, BF16),
            VMEM((GROUP, 8, 128), jnp.int32),
            VMEM((GROUP, SLOTS, width), BF16), VMEM((GROUP, SLOTS, width), BF16),
            VMEM((GROUP, rows, width), BF16),
            DMA((3,)), DMA((GROUP - 1,)), DMA((GROUP - 1,)), DMA((2, GROUP - 1)), DMA((2, GROUP - 1)),
            *GATHER_SEMS,
        ],
        compiler_params=pltpu.CompilerParams(
            collective_id=0, has_side_effects=True, vmem_limit_bytes=48 * 2**20
        ),
        name="front",
    )(padded, source, gain, cos, sin, table, wq, wkv)


QB = 256


def attention(q_ref, first_ref, pair_ref, att_ref, win_ref, relay, m_ref, l_ref, acc_ref, ssem, rsem):
    t = lax.axis_index("tensor")
    r = lax.axis_index("dp")
    y, c = r // 2, lax.rem(r, 2)
    kind = lax.rem(t, 2)
    rows = q_ref.shape[0]
    blocks = rows // QB
    partner = {"tensor": t + 1 - 2 * kind}
    up = {"dp": lax.rem(y + 1, SIDE) * 2 + c}
    down = {"dp": lax.rem(y + SIDE - 1, SIDE) * 2 + c}
    other = {"dp": y * 2 + 1 - c}

    def copy(n, src, dst, peer):
        return remote(src, dst, ssem.at[n], rsem.at[n], peer)

    def step(w, i, count, causal):
        span = pl.ds(i * QB, QB)
        q = jnp.concatenate([q_ref[span, :HD], q_ref[span, HD:]], axis=0)
        first = first_ref[:, span]
        first = jnp.concatenate([first, first], axis=1)
        scores = lax.dot_general(
            win_ref[w, 0, :count, :], q, (((1,), (1,)), ((), ())), preferred_element_type=F32
        )
        at = lax.broadcasted_iota(jnp.int32, (count, 1), 0) + w * rows
        allowed = at >= first
        if causal:
            query = lax.broadcasted_iota(jnp.int32, (1, QB), 1) + (4 * rows + i * QB)
            allowed &= at <= jnp.concatenate([query, query], axis=1)
        scores = jnp.where(allowed, scores, NEGATIVE)
        top = jnp.max(scores, axis=0, keepdims=True) * EXP_SCALE
        if not causal:
            old = m_ref[i]
            top = jnp.maximum(old, top)
            decay = jnp.exp2(old - top)
        weights = jnp.exp2(scores * EXP_SCALE - top)
        total = jnp.sum(weights, axis=0, keepdims=True)
        added = lax.dot_general(
            win_ref[w, 1, :count, :], weights.astype(BF16), (((0,), (0,)), ((), ())),
            preferred_element_type=F32,
        )
        l_ref[i] = total if causal else l_ref[i] * decay + total
        acc_ref[i] = added if causal else acc_ref[i] * decay + added
        m_ref[i] = top

    def earlier(w):
        @pl.when(r + w >= 4)
        def _():
            for i in range(blocks):
                step(w, i, rows, False)

    swap = copy(0, pair_ref, win_ref.at[4, kind], partner)
    swap.start()
    win_ref[4, kind] = pair_ref[...]
    swap_in = copy(0, pair_ref, win_ref.at[4, 1 - kind], partner)
    up_key = copy(1, win_ref.at[4, 0], win_ref.at[2, 0], up)
    up_value = copy(2, win_ref.at[4, 1], win_ref.at[2, 1], up)
    far_key = copy(3, win_ref.at[2, 0], win_ref.at[0, 0], up)
    down_value = copy(4, win_ref.at[4, 1], relay, down)
    far_value = copy(5, relay, win_ref.at[0, 1], down)
    near = [copy(6 + k, win_ref.at[4, k], win_ref.at[3, k], other) for k in range(2)]
    cross0 = [copy(8 + k, win_ref.at[2, k], win_ref.at[1, k], other) for k in range(2)]
    cross1 = [copy(8 + k, win_ref.at[2, k], win_ref.at[3, k], other) for k in range(2)]
    far1 = [copy(10 + k, win_ref.at[0, k], win_ref.at[1, k], other) for k in range(2)]
    has_up, has_far = y < SIDE - 1, y < SIDE - 2
    got_up, got_far = y > 0, y > 1
    relays = (y == SIDE - 1) | (y == 0)
    swap_in.wait_recv()

    @pl.when(has_far)
    def _():
        down_value.start()

    @pl.when(has_up)
    def _():
        up_key.start()
        up_value.start()

    @pl.when(c == 0)
    def _():
        for k in range(2):
            near[k].start()

    for i in range(blocks):
        step(4, i, (i + 1) * QB, True)

    @pl.when(relays)
    def _():
        down_value.wait_recv()
        far_value.start()

    @pl.when(got_up)
    def _():
        up_key.wait_recv()

        @pl.when(has_up)
        def _():
            far_key.start()

        up_value.wait_recv()

        @pl.when(c == 0)
        def _():
            for k in range(2):
                cross0[k].start()

        @pl.when(c == 1)
        def _():
            for k in range(2):
                cross1[k].start()

    @pl.when(c == 1)
    def _():
        for k in range(2):
            near[k].wait_recv()

    earlier(2 + c)

    @pl.when(got_up & (c == 0))
    def _():
        for k in range(2):
            cross1[k].wait_recv()

    earlier(3 - c)

    @pl.when(got_far)
    def _():
        far_key.wait_recv()
        far_value.wait_recv()

        @pl.when(c == 1)
        def _():
            for k in range(2):
                far1[k].start()

    @pl.when(got_up & (c == 1))
    def _():
        for k in range(2):
            cross0[k].wait_recv()

    earlier(c)

    @pl.when(got_far & (c == 0))
    def _():
        for k in range(2):
            far1[k].wait_recv()

    earlier(1 - c)
    for i in range(blocks):
        span = pl.ds(i * QB, QB)
        out = acc_ref[i] / l_ref[i]
        att_ref[span, :HD] = out[:, :QB].T.astype(BF16)
        att_ref[span, HD:] = out[:, QB:].T.astype(BF16)

    @pl.when(c == 0)
    def _():
        for k in range(2):
            near[k].wait_send()

    @pl.when(got_up & (c == 0))
    def _():
        for k in range(2):
            cross0[k].wait_send()

    @pl.when(got_up & (c == 1))
    def _():
        for k in range(2):
            cross1[k].wait_send()

    @pl.when(got_far & (c == 1))
    def _():
        for k in range(2):
            far1[k].wait_send()

    @pl.when(has_far)
    def _():
        down_value.wait_send()

    @pl.when(has_up)
    def _():
        up_key.wait_send()
        up_value.wait_send()

    @pl.when(relays)
    def _():
        far_value.wait_send()

    @pl.when(got_up & has_up)
    def _():
        far_key.wait_send()

    swap.wait_send()


def back_kernel(pair_ref, q_ref, first_ref, emb_ref, gain_ref, wo_hbm, wg_hbm, wu_hbm, wd_hbm, out_ref,
                wo, wg, wu, wd, win, relay, m_ref, l_ref, acc_ref, att, stream, all_ref, hid, load_sem, as_, ar,
                part, r1, r2, held, s1, e1, s2, e2, part_b, r1b, r2b, held_b, s1b, e1b, s2b, e2b, gs, gr):
    z, x = here()
    t = lax.axis_index("tensor")
    r = lax.axis_index("dp")
    y, c = r // 2, lax.rem(r, 2)
    loads = [
        pltpu.make_async_copy(src, dst, load_sem.at[n])
        for n, (src, dst) in enumerate(((wo_hbm, wo), (wg_hbm, wg), (wu_hbm, wu), (wd_hbm, wd)))
    ]
    for load in loads:
        load.start()
    greet(torus_peers(z, x) + [
        {"dp": lax.rem(y + 1, SIDE) * 2 + c}, {"dp": lax.rem(y + SIDE - 1, SIDE) * 2 + c}, {"dp": y * 2 + 1 - c},
    ])
    attention(q_ref, first_ref, pair_ref, att, win, relay, m_ref, l_ref, acc_ref, as_, ar)

    def mixed(cols, value):
        stream[:, cols] = (emb_ref[:, cols].astype(F32) + value).astype(BF16)

    loads[0].wait()
    ring_reduce(part, r1, r2, held, s1, e1, s2, e2, z, x, products(att, wo, part, z, x), mixed)
    all_ref[t] = normalize(stream[...].astype(F32), gain_ref[...])
    loads[1].wait()
    loads[2].wait()

    def gate(dz):
        lhs, span = row_group(all_ref, z, dz)
        gated = jnp.dot(lhs, wg[...], preferred_element_type=F32)
        upper = jnp.dot(lhs, wu[...], preferred_element_type=F32)
        hid[span, :] = (gated / (1.0 + jnp.exp(-gated)) * upper).astype(BF16)

    ring_gather(all_ref, gs, gr, z, x, gate)

    def added(cols, value):
        out_ref[:, cols] = (stream[:, cols].astype(F32) + value).astype(BF16)

    loads[3].wait()
    ring_reduce(part_b, r1b, r2b, held_b, s1b, e1b, s2b, e2b, z, x, products(hid, wd, part_b, z, x), added)


def back(pair, queries, first, embedded, gain, wo, w_gate, w_up, w_down):
    rows, width = embedded.shape
    span = rows * GROUP
    blocks = span // QB
    whole = pl.BlockSpec(memory_space=VMEM)
    outside = pl.BlockSpec(memory_space=pl.ANY)
    return pl.pallas_call(
        back_kernel,
        out_shape=jax.ShapeDtypeStruct((rows, width), BF16),
        in_specs=[whole] * 5 + [outside] * 4,
        out_specs=whole,
        scratch_shapes=[
            VMEM(wo.shape, BF16), VMEM(w_gate.shape, BF16), VMEM(w_up.shape, BF16), VMEM(w_down.shape, BF16),
            VMEM((5, 2, span, HD), BF16), VMEM((span, HD), BF16),
            VMEM((blocks, 1, 2 * QB), F32), VMEM((blocks, 1, 2 * QB), F32), VMEM((blocks, HD, 2 * QB), F32),
            VMEM((span, 2 * HD), BF16), VMEM((rows, width), BF16),
            VMEM((GROUP, rows, width), BF16), VMEM((span, w_gate.shape[1]), BF16),
            DMA((4,)), DMA((12,)), DMA((12,)),
            *reduce_scratch(rows, width), *reduce_scratch(rows, width), *GATHER_SEMS,
        ],
        compiler_params=pltpu.CompilerParams(
            collective_id=1, has_side_effects=True, vmem_limit_bytes=62 * 2**20
        ),
        name="back",
    )(pair, queries, first, embedded, gain, wo, w_gate, w_up, w_down)


def local(ids, doc_lengths, table, attn_gain, wq, wkv, wo, mlp_gain, w_gate, w_up, w_down):
    r = lax.axis_index("dp")
    own_rows = ids.shape[0]
    tok_range = own_rows * GROUP
    owner = ids // table.shape[0]
    earlier = jnp.arange(own_rows)[:, None] < jnp.arange(own_rows)[None, :]
    own_rank = jnp.sum(jnp.where((owner[:, None] == owner[None, :]) & earlier, 1, 0), axis=0)
    source = (owner * SLOTS + own_rank)[:, None]
    positions = r * tok_range + jnp.arange(tok_range, dtype=jnp.int32)
    first_pos, offsets = document_info(positions, doc_lengths)
    cos, sin = turns(offsets)
    embedded, queries, pair = front(ids, source, attn_gain[None, :], cos, sin, table, wq, wkv)
    first = (first_pos - (r - 4) * tok_range)[None, :]
    return back(pair, queries, first, embedded, mlp_gain[None, :], wo, w_gate, w_up, w_down)


def solution(mesh):
    placed = (
        P(("dp", "tensor")),
        P(),
        P("tensor", None),
        P(),
        P(None, "tensor"),
        P(None, "tensor"),
        P("tensor", None),
        P(),
        P(None, "tensor"),
        P(None, "tensor"),
        P("tensor", None),
    )
    return jax.shard_map(
        local, mesh=mesh, in_specs=placed, out_specs=P(("dp", "tensor"), None), check_vma=False
    )
```

```python
import jax
import jax.numpy as jnp
from jax import lax
from jax.experimental import pallas as pl
from jax.experimental.pallas import tpu as pltpu
from jax.sharding import PartitionSpec as P

HD = 128
SIDE = 4
GROUP = SIDE * SIDE
SLOTS = 8

EPSILON = 1e-05
ROPE_BASE = 500000.0
NEGATIVE = -1e30
EXP_SCALE = HD ** (-0.5) * 1.4426950408889634
MESH = pl.DeviceIdType.MESH
VMEM = pltpu.VMEM
DMA = pltpu.SemaphoreType.DMA
BF16 = jnp.bfloat16
F32 = jnp.float32


def wrap(v):
    return lax.rem(v + 2 * SIDE, SIDE)


def place(z, x):
    return wrap(z) * SIDE + wrap(x)


def here():
    t = lax.axis_index("tensor")
    return t // SIDE, lax.rem(t, SIDE)


def greet(peers):
    barrier = pltpu.get_barrier_semaphore()
    for peer in peers:
        pl.semaphore_signal(barrier, inc=1, device_id=peer, device_id_type=MESH)
    pl.semaphore_wait(barrier, len(peers))


def torus_peers(z, x):
    return [{"tensor": place(z + a, x + b)} for a, b in ((0, 1), (0, -1), (1, 0), (-1, 0))]


def remote(src, dst, send_sem, recv_sem, peer):
    return pltpu.make_async_remote_copy(
        src_ref=src, dst_ref=dst, send_sem=send_sem, recv_sem=recv_sem,
        device_id=peer, device_id_type=MESH,
    )


def ring_gather(buf, ssem, rsem, z, x, ready):
    half = buf.shape[-1] // 2
    quarter = half // 2
    started = []

    def block(h, first, second):
        return place(z + second, x + first) if h == 0 else place(z + first, x + second)

    def view(h, first, second, part):
        start, size = (h * half, half) if part == 0 else (h * half + (part - 1) * quarter, quarter)
        return buf.at[block(h, first, second), :, pl.ds(start, size)]

    def send(h, n, first, second, part, axis, d):
        ref = view(h, first, second, part)
        peer = {"tensor": block(h, d, 0) if axis == 0 else block(h, 0, d)}
        copy = remote(ref, ref, ssem.at[h, n], rsem.at[h, n], peer)
        copy.start()
        started.append(copy)

    def recv(h, n, first, second, part):
        ref = view(h, first, second, part)
        remote(ref, ref, ssem.at[h, n], rsem.at[h, n], {"tensor": block(h, 1, 0)}).wait_recv()

    offsets = (0, -1, 1, 2)
    for h in range(2):
        send(h, 0, 0, 0, 0, 0, 1)
        send(h, 1, 0, 0, 0, 0, -1)
    for h in range(2):
        send(h, 4, 0, 0, 0, 1, 1)
        send(h, 5, 0, 0, 0, 1, -1)
    for h in range(2):
        recv(h, 0, -1, 0, 0)
        send(h, 2, -1, 0, 1, 0, 1)
        recv(h, 1, 1, 0, 0)
        send(h, 3, 1, 0, 2, 0, -1)
        for n in (1, 2):
            send(h, 4 + 2 * n, offsets[n], 0, 0, 1, 1)
            send(h, 5 + 2 * n, offsets[n], 0, 0, 1, -1)

    def relay(n):
        k = offsets[n]
        for h in range(2):
            recv(h, 4 + 2 * n, k, -1, 0)
            send(h, 12 + 2 * n, k, -1, 1, 1, 1)
            recv(h, 5 + 2 * n, k, 1, 0)
            send(h, 13 + 2 * n, k, 1, 2, 1, -1)

    relay(0)
    for h in range(2):
        recv(h, 2, 2, 0, 1)
        recv(h, 3, 2, 0, 2)
        send(h, 10, 2, 0, 0, 1, 1)
        send(h, 11, 2, 0, 0, 1, -1)
    relay(1)
    relay(2)

    def far(h, n):
        recv(h, 12 + 2 * n, offsets[n], 2, 1)
        recv(h, 13 + 2 * n, offsets[n], 2, 2)

    far(1, 0)
    ready(0)
    relay(3)
    far(1, 1)
    ready(-1)
    far(1, 2)
    ready(1)
    for n in range(4):
        far(0, n)
    far(1, 3)
    ready(2)
    for copy in started:
        copy.wait_send()


GATHER_SEMS = [DMA((2, 20)), DMA((2, 20))]


def ring_reduce(part, r1, r2, held, s1, e1, s2, e2, z, x, make, finish):
    half = part.shape[-1] // 2
    quarter = half // 2
    started = []

    def at(h, k, j):
        return (wrap(z + k), wrap(x + j)) if h == 0 else (wrap(z + j), wrap(x + k))

    def mine(h, k, j, q):
        a, b = at(h, k, j)
        return part.at[a, b, :, pl.ds(h * half + q * quarter, quarter)]

    def peer(h, axis, d):
        a, b = at(h, d, 0) if axis == 0 else at(h, 0, d)
        return {"tensor": a * SIDE + b}

    def send1(h, slot, j, src, d):
        copy = remote(src, r1.at[h, slot, j], s1.at[h, slot, j], e1.at[h, slot, j], peer(h, 0, d))
        copy.start()
        started.append(copy)

    def recv1(h, slot, j):
        ref = r1.at[h, slot, j]
        remote(ref, ref, s1.at[h, slot, j], e1.at[h, slot, j], peer(h, 0, 1)).wait_recv()

    def send2(h, slot, src, d):
        copy = remote(src, r2.at[h, slot], s2.at[h, slot], e2.at[h, slot], peer(h, 1, d))
        copy.start()
        started.append(copy)

    def recv2(h, slot):
        ref = r2.at[h, slot]
        remote(ref, ref, s2.at[h, slot], e2.at[h, slot], peer(h, 0, 1)).wait_recv()

    def load(ref):
        return ref[...].astype(F32)

    order = (2, 1, 3, 0)
    for h in range(2):
        make(h, 2)
        for j in order:
            send1(h, 0, j, mine(h, 2, j, 0), 1)
            send1(h, 3, j, mine(h, 2, j, 1), -1)
    for h in range(2):
        make(h, 1)
        for j in order:
            send1(h, 1, j, mine(h, 1, j, 1), 1)
        make(h, 3)
        for j in order:
            send1(h, 4, j, mine(h, 3, j, 0), -1)
    for j in order:
        for h in range(2):
            recv1(h, 0, j)
            r1[h, 0, j] = (load(r1.at[h, 0, j]) + load(mine(h, 1, j, 0))).astype(BF16)
            send1(h, 2, j, r1.at[h, 0, j], 1)
            recv1(h, 3, j)
            r1[h, 3, j] = (load(r1.at[h, 3, j]) + load(mine(h, 3, j, 1))).astype(BF16)
            send1(h, 5, j, r1.at[h, 3, j], -1)
    for h in range(2):
        make(h, 0)

    def arrived(h, j):
        for slot in (1, 4, 2, 5):
            recv1(h, slot, j)

    def summed(h, j, q):
        a, b = ((2, 4), (1, 5))[q]
        return load(mine(h, 0, j, q)) + load(r1.at[h, a, j]) + load(r1.at[h, b, j])

    for h in range(2):
        arrived(h, 2)
        for q, slot, d in ((0, 0, 1), (1, 3, -1)):
            held[h, 0, q] = summed(h, 2, q).astype(BF16)
            send2(h, slot, held.at[h, 0, q], d)
    for h in range(2):
        arrived(h, 1)
        held[h, 1, 1] = summed(h, 1, 1).astype(BF16)
        send2(h, 1, held.at[h, 1, 1], 1)
        arrived(h, 3)
        held[h, 2, 0] = summed(h, 3, 0).astype(BF16)
        send2(h, 4, held.at[h, 2, 0], -1)
    for h in range(2):
        recv2(h, 0)
        held[h, 1, 0] = (summed(h, 1, 0) + load(r2.at[h, 0])).astype(BF16)
        send2(h, 2, held.at[h, 1, 0], 1)
        recv2(h, 3)
        held[h, 2, 1] = (summed(h, 3, 1) + load(r2.at[h, 3])).astype(BF16)
        send2(h, 5, held.at[h, 2, 1], -1)
    for h in range(2):
        arrived(h, 0)
        for slot in (1, 4, 2, 5):
            recv2(h, slot)
        for q in range(2):
            a, b = ((2, 4), (1, 5))[q]
            value = summed(h, 0, q) + load(r2.at[h, a]) + load(r2.at[h, b])
            finish(pl.ds(h * half + q * quarter, quarter), value)
    for copy in started:
        copy.wait_send()


def products(a_ref, w_ref, part, z, x):
    rows, width = part.shape[2], part.shape[3]
    half = width // 2
    step = min(512, half)

    def make(h, k):
        def run(blocks):
            lhs = jnp.concatenate(
                [a_ref[pl.ds(pl.multiple_of((a * SIDE + b) * rows, 16), rows), :] for a, b in blocks], axis=0
            )

            def column(c, carry):
                cols = pl.ds(pl.multiple_of(h * half + c * step, step), step)
                out = jnp.dot(lhs, w_ref[:, cols], preferred_element_type=F32).astype(BF16)
                for n, (a, b) in enumerate(blocks):
                    part[a, b, :, cols] = out[n * rows:(n + 1) * rows]
                return carry

            lax.fori_loop(0, half // step, column, 0)

        if h == 0:
            run([(wrap(z + k), b) for b in range(SIDE)])
        else:
            run([(a, wrap(x + k)) for a in range(SIDE)])

    return make


def normalize(rows, gain):
    scale = lax.rsqrt(jnp.mean(rows * rows, axis=-1, keepdims=True) + EPSILON)
    return (rows * scale * gain).astype(BF16)


def row_group(all_ref, z, dz):
    rows, width = all_ref.shape[1:]
    zz = wrap(z + dz)
    lhs = all_ref[pl.ds(zz * SIDE, SIDE)].reshape(SIDE * rows, width)
    return lhs, pl.ds(pl.multiple_of(zz * SIDE * rows, 16), SIDE * rows)


def find_rows(ids_ref, all_ids, wanted_by, table, found, recv, emb_ref, t, peers, sources, load, ks, kr, xs, xr, meanwhile):
    copies = []
    rows, width = emb_ref.shape
    wanted_by[...] = jnp.full_like(wanted_by, -1)
    wanted_by[:, :rows] = jnp.broadcast_to(ids_ref[...], (8, rows))
    for n, p in enumerate(peers):
        copy = remote(wanted_by, all_ids.at[t], ks.at[n], kr.at[n], {"tensor": p})
        copy.start()
        copies.append(copy)
    all_ids[t] = wanted_by[...]
    slots = GROUP * SLOTS
    owned = table.shape[0]
    square = (128, 128)
    row, lane = lax.broadcasted_iota(jnp.int32, square, 0), lax.broadcasted_iota(jnp.int32, square, 1)
    own = jnp.broadcast_to(wanted_by[:1, :], square)
    owner = jnp.right_shift(own, owned.bit_length() - 1).astype(F32)
    same = (owner == owner.T) & (row < lane)
    source = owner * SLOTS + jnp.sum(jnp.where(same, 1.0, 0.0), axis=0, keepdims=True)
    chosen = jnp.where((source == row.astype(F32)) & (own >= 0), 1.0, 0.0).T[:rows].astype(BF16)
    before = jnp.where(row < lane, 1.0, 0.0).astype(BF16)
    for n, p in enumerate(sources):
        remote(wanted_by, all_ids.at[p], ks.at[n], kr.at[n], {"tensor": p}).wait_recv()
    local_rows = all_ids[...].reshape(slots, 128) - t * owned
    inside = (local_rows >= 0) & (local_rows < owned)
    rank = jnp.dot(jnp.where(inside, 1.0, 0.0).astype(BF16), before, preferred_element_type=F32)
    slot = lax.rem(row, SLOTS).astype(F32)
    wanted = jnp.sum(
        jnp.where(inside & (rank == slot), local_rows.astype(F32), 0.0), axis=1, keepdims=True
    )
    pick = lax.broadcasted_iota(jnp.int32, (slots, owned), 1).astype(F32) == wanted
    pick = jnp.where(pick, 1.0, 0.0).astype(BF16)
    load.wait()
    parts = 2
    step = width // parts
    for c in range(parts):
        def fetch(b, carry):
            cols = pl.ds(pl.multiple_of(c * step + b * 512, 512), 512)
            out = jnp.dot(pick, table[:, cols], preferred_element_type=F32).astype(BF16)
            found[:, :, cols] = out.reshape(GROUP, SLOTS, 512)
            return carry

        lax.fori_loop(0, step // 512, fetch, 0)
        cols = pl.ds(c * step, step)
        for n, p in enumerate(peers):
            copy = remote(found.at[p, :, cols], recv.at[t, :, cols], xs.at[c, n], xr.at[c, n], {"tensor": p})
            copy.start()
            copies.append(copy)
        recv[t, :, cols] = found[t, :, cols]
    meanwhile()
    total = jnp.zeros((rows, 1), F32)
    for c in range(parts):
        cols = pl.ds(c * step, step)
        for n, p in enumerate(sources):
            ref = recv.at[p, :, cols]
            remote(ref, ref, xs.at[c, n], xr.at[c, n], {"tensor": p}).wait_recv()
        for b in range(step // 1024):
            cols = pl.ds(c * step + b * 1024, 1024)
            picked = jnp.dot(chosen, recv[:, :, cols].reshape(slots, 1024), preferred_element_type=F32)
            emb_ref[:, cols] = picked.astype(BF16)
            total += jnp.sum(picked * picked, axis=-1, keepdims=True)
    return copies, total


def document_starts(lengths_ref, positions):
    first = jnp.zeros_like(positions)
    start = jnp.int32(0)
    for d in range(lengths_ref.shape[0]):
        first = jnp.where(positions >= start, start, first)
        start = start + lengths_ref[d]
    return first


QB = 256


def attention(q_ref, first_ref, pair_ref, att_ref, win_ref, relay, m_ref, l_ref, acc_ref, ssem, rsem):
    t = lax.axis_index("tensor")
    r = lax.axis_index("dp")
    y, c = r // 2, lax.rem(r, 2)
    kind = lax.rem(t, 2)
    rows = q_ref.shape[0]
    blocks = rows // QB
    partner = {"tensor": t + 1 - 2 * kind}
    up = {"dp": lax.rem(y + 1, SIDE) * 2 + c}
    down = {"dp": lax.rem(y + SIDE - 1, SIDE) * 2 + c}
    other = {"dp": y * 2 + 1 - c}

    def copy(n, src, dst, peer):
        return remote(src, dst, ssem.at[n], rsem.at[n], peer)

    def step(w, i, count, causal):
        span = pl.ds(i * QB, QB)
        q = jnp.concatenate([q_ref[span, :HD], q_ref[span, HD:]], axis=0)
        first = first_ref[:, span]
        first = jnp.concatenate([first, first], axis=1)
        scores = lax.dot_general(
            win_ref[w, 0, :count, :], q, (((1,), (1,)), ((), ())), preferred_element_type=F32
        )
        at = lax.broadcasted_iota(jnp.int32, (count, 1), 0) + w * rows
        allowed = at >= first
        if causal:
            query = lax.broadcasted_iota(jnp.int32, (1, QB), 1) + (4 * rows + i * QB)
            allowed &= at <= jnp.concatenate([query, query], axis=1)
        scores = jnp.where(allowed, scores, NEGATIVE)
        top = jnp.max(scores, axis=0, keepdims=True) * EXP_SCALE
        if not causal:
            old = m_ref[i]
            top = jnp.maximum(old, top)
            decay = jnp.exp2(old - top)
        weights = jnp.exp2(scores * EXP_SCALE - top)
        total = jnp.sum(weights, axis=0, keepdims=True)
        added = lax.dot_general(
            win_ref[w, 1, :count, :], weights.astype(BF16), (((0,), (0,)), ((), ())),
            preferred_element_type=F32,
        )
        l_ref[i] = total if causal else l_ref[i] * decay + total
        acc_ref[i] = added if causal else acc_ref[i] * decay + added
        m_ref[i] = top

    def earlier(w):
        @pl.when(r + w >= 4)
        def _():
            for i in range(blocks):
                step(w, i, rows, False)

    swap = copy(0, pair_ref, win_ref.at[4, kind], partner)
    swap.start()
    win_ref[4, kind] = pair_ref[...]
    swap_in = copy(0, pair_ref, win_ref.at[4, 1 - kind], partner)
    up_key = copy(1, win_ref.at[4, 0], win_ref.at[2, 0], up)
    up_value = copy(2, win_ref.at[4, 1], win_ref.at[2, 1], up)
    far_key = copy(3, win_ref.at[2, 0], win_ref.at[0, 0], up)
    down_value = copy(4, win_ref.at[4, 1], relay, down)
    far_value = copy(5, relay, win_ref.at[0, 1], down)
    near = [copy(6 + k, win_ref.at[4, k], win_ref.at[3, k], other) for k in range(2)]
    cross0 = [copy(8 + k, win_ref.at[2, k], win_ref.at[1, k], other) for k in range(2)]
    cross1 = [copy(8 + k, win_ref.at[2, k], win_ref.at[3, k], other) for k in range(2)]
    far1 = [copy(10 + k, win_ref.at[0, k], win_ref.at[1, k], other) for k in range(2)]
    has_up, has_far = y < SIDE - 1, y < SIDE - 2
    got_up, got_far = y > 0, y > 1
    relays = (y == SIDE - 1) | (y == 0)
    swap_in.wait_recv()

    @pl.when(has_far)
    def _():
        down_value.start()

    @pl.when(has_up)
    def _():
        up_key.start()
        up_value.start()

    @pl.when(c == 0)
    def _():
        for k in range(2):
            near[k].start()

    for i in range(blocks):
        step(4, i, (i + 1) * QB, True)

    @pl.when(relays)
    def _():
        down_value.wait_recv()
        far_value.start()

    @pl.when(got_up)
    def _():
        up_key.wait_recv()

        @pl.when(has_up)
        def _():
            far_key.start()

        up_value.wait_recv()

        @pl.when(c == 0)
        def _():
            for k in range(2):
                cross0[k].start()

        @pl.when(c == 1)
        def _():
            for k in range(2):
                cross1[k].start()

    @pl.when(c == 1)
    def _():
        for k in range(2):
            near[k].wait_recv()

    earlier(2 + c)

    @pl.when(got_up & (c == 0))
    def _():
        for k in range(2):
            cross1[k].wait_recv()

    earlier(3 - c)

    @pl.when(got_far)
    def _():
        far_key.wait_recv()
        far_value.wait_recv()

        @pl.when(c == 1)
        def _():
            for k in range(2):
                far1[k].start()

    @pl.when(got_up & (c == 1))
    def _():
        for k in range(2):
            cross0[k].wait_recv()

    earlier(c)

    @pl.when(got_far & (c == 0))
    def _():
        for k in range(2):
            far1[k].wait_recv()

    earlier(1 - c)
    for i in range(blocks):
        span = pl.ds(i * QB, QB)
        out = acc_ref[i] / l_ref[i]
        att_ref[span, :HD] = out[:, :QB].T.astype(BF16)
        att_ref[span, HD:] = out[:, QB:].T.astype(BF16)

    @pl.when(c == 0)
    def _():
        for k in range(2):
            near[k].wait_send()

    @pl.when(got_up & (c == 0))
    def _():
        for k in range(2):
            cross0[k].wait_send()

    @pl.when(got_up & (c == 1))
    def _():
        for k in range(2):
            cross1[k].wait_send()

    @pl.when(got_far & (c == 1))
    def _():
        for k in range(2):
            far1[k].wait_send()

    @pl.when(has_far)
    def _():
        down_value.wait_send()

    @pl.when(has_up)
    def _():
        up_key.wait_send()
        up_value.wait_send()

    @pl.when(relays)
    def _():
        far_value.wait_send()

    @pl.when(got_up & has_up)
    def _():
        far_key.wait_send()

    swap.wait_send()


def layer_kernel(ids_ref, lengths_ref, inverse_ref, attn_gain_ref, mlp_gain_ref,
                 table_hbm, wq_hbm, wkv_hbm, wo_hbm, wg_hbm, wu_hbm, wd_hbm, out_ref,
                 table, wq, wkv, wo, wg, wu, wd, load_sem,
                 wanted_by, all_ids, found, recv, ks, kr, xs, xr,
                 emb, all_ref, q, pair, cos_ref, sin_ref, first_ref, gs, gr,
                 win, relay, m_ref, l_ref, acc_ref, att, as_, ar,
                 stream, hid, gs2, gr2,
                 part, r1, r2, held, s1, e1, s2, e2, s1b, e1b, s2b, e2b):
    z, x = here()
    t = lax.axis_index("tensor")
    r = lax.axis_index("dp")
    y, c = r // 2, lax.rem(r, 2)
    loads = [
        pltpu.make_async_copy(src, dst, load_sem.at[n])
        for n, (src, dst) in enumerate((
            (table_hbm, table), (wq_hbm, wq), (wkv_hbm, wkv), (wo_hbm, wo), (wg_hbm, wg), (wu_hbm, wu), (wd_hbm, wd)
        ))
    ]
    for load in loads:
        load.start()
    peers = [lax.rem(t + n, GROUP) for n in range(1, GROUP)]
    sources = [lax.rem(t + GROUP - n, GROUP) for n in range(1, GROUP)]
    greet([{"tensor": p} for p in peers] + [
        {"dp": lax.rem(y + 1, SIDE) * 2 + c}, {"dp": lax.rem(y + SIDE - 1, SIDE) * 2 + c}, {"dp": y * 2 + 1 - c},
    ])
    rows, width = emb.shape
    span_rows = rows * GROUP

    def positions():
        lanes = r * span_rows + lax.broadcasted_iota(jnp.int32, (1, span_rows), 1)
        first_ref[...] = document_starts(lengths_ref, lanes) - (r - 4) * span_rows
        sign = jnp.where(lax.broadcasted_iota(jnp.int32, (1, HD), 1) < HD // 2, -1.0, 1.0)

        def turn(b, carry):
            at = pl.ds(pl.multiple_of(b * 64, 64), 64)
            place_of = r * span_rows + b * 64 + lax.broadcasted_iota(jnp.int32, (64, HD), 0)
            angle = (place_of - document_starts(lengths_ref, place_of)).astype(F32) * inverse_ref[...]
            cos_ref[at, :] = jnp.cos(angle)
            sin_ref[at, :] = jnp.sin(angle) * sign
            return carry

        lax.fori_loop(0, span_rows // 64, turn, 0)

    copies, total = find_rows(
        ids_ref, all_ids, wanted_by, table, found, recv, emb, t, peers, sources, loads[0], ks, kr, xs, xr, positions
    )
    scale = lax.rsqrt(total / width + EPSILON)
    for b in range(width // 1024):
        cols = pl.ds(b * 1024, 1024)
        all_ref[t, :, cols] = (emb[:, cols].astype(F32) * scale * attn_gain_ref[:, cols]).astype(BF16)
    loads[1].wait()
    loads[2].wait()
    keys_here = lax.rem(t, 2) == 0

    def project(dz):
        lhs, span = row_group(all_ref, z, dz)
        cos, sin = cos_ref[span, :], sin_ref[span, :]
        queries = jnp.dot(lhs, wq[...], preferred_element_type=F32)
        for h in range(queries.shape[1] // HD):
            head = queries[:, h * HD:(h + 1) * HD]
            q[span, h * HD:(h + 1) * HD] = (head * cos + pltpu.roll(head, HD // 2, 1) * sin).astype(BF16)
        both = jnp.dot(lhs, wkv[...], preferred_element_type=F32)
        turned = both * cos + pltpu.roll(both, HD // 2, 1) * sin
        pair[span, :] = jnp.where(keys_here, turned, both).astype(BF16)

    ring_gather(all_ref, gs, gr, z, x, project)
    attention(q, first_ref, pair, att, win, relay, m_ref, l_ref, acc_ref, as_, ar)

    def mixed(cols, value):
        stream[:, cols] = (emb[:, cols].astype(F32) + value).astype(BF16)

    loads[3].wait()
    ring_reduce(part, r1, r2, held, s1, e1, s2, e2, z, x, products(att, wo, part, z, x), mixed)
    all_ref[t] = normalize(stream[...].astype(F32), mlp_gain_ref[...])
    loads[4].wait()
    loads[5].wait()

    def gate(dz):
        lhs, span = row_group(all_ref, z, dz)
        across = (((1,), (1,)), ((), ()))
        gated = lax.dot_general(lhs, wg[...], across, preferred_element_type=F32)
        upper = lax.dot_general(lhs, wu[...], across, preferred_element_type=F32)
        hid[span, :] = (gated / (1.0 + jnp.exp(-gated)) * upper).astype(BF16)

    ring_gather(all_ref, gs2, gr2, z, x, gate)

    def added(cols, value):
        out_ref[:, cols] = (stream[:, cols].astype(F32) + value).astype(BF16)

    loads[6].wait()
    ring_reduce(part, r1, r2, held, s1b, e1b, s2b, e2b, z, x, products(hid, wd, part, z, x), added)
    for copy in copies:
        copy.wait_send()


def layer(ids, lengths, inverse, attn_gain, mlp_gain, table, wq, wkv, wo, wg, wu, wd):
    rows, width = ids.shape[1], table.shape[1]
    span = rows * GROUP
    blocks = span // QB
    quarter = width // 4
    whole = pl.BlockSpec(memory_space=VMEM)
    outside = pl.BlockSpec(memory_space=pl.ANY)
    peers = DMA((GROUP - 1,))
    reduce_sems = [DMA((2, 6, SIDE)), DMA((2, 6, SIDE)), DMA((2, 6)), DMA((2, 6))]
    return pl.pallas_call(
        layer_kernel,
        out_shape=jax.ShapeDtypeStruct((rows, width), BF16),
        in_specs=[whole, pl.BlockSpec(memory_space=pltpu.SMEM)] + [whole] * 3 + [outside] * 7,
        out_specs=whole,
        scratch_shapes=[
            *[VMEM(w.shape, BF16) for w in (table, wq, wkv, wo, wg, wu, wd)], DMA((7,)),
            VMEM((8, 128), jnp.int32), VMEM((GROUP, 8, 128), jnp.int32),
            VMEM((GROUP, SLOTS, width), BF16), VMEM((GROUP, SLOTS, width), BF16),
            peers, peers, DMA((2, GROUP - 1)), DMA((2, GROUP - 1)),
            VMEM((rows, width), BF16), VMEM((GROUP, rows, width), BF16),
            VMEM((span, wq.shape[1]), BF16), VMEM((span, HD), BF16),
            VMEM((span, HD), F32), VMEM((span, HD), F32), VMEM((1, span), jnp.int32), *GATHER_SEMS,
            VMEM((5, 2, span, HD), BF16), VMEM((span, HD), BF16),
            VMEM((blocks, 1, 2 * QB), F32), VMEM((blocks, 1, 2 * QB), F32), VMEM((blocks, HD, 2 * QB), F32),
            VMEM((span, 2 * HD), BF16), DMA((12,)), DMA((12,)),
            VMEM((rows, width), BF16), VMEM((span, wg.shape[0]), BF16), *GATHER_SEMS,
            VMEM((SIDE, SIDE, rows, width), BF16),
            VMEM((2, 6, SIDE, rows, quarter), BF16),
            VMEM((2, 6, rows, quarter), BF16),
            VMEM((2, 3, 2, rows, quarter), BF16),
            *reduce_sems, *reduce_sems,
        ],
        compiler_params=pltpu.CompilerParams(
            collective_id=0, has_side_effects=True, vmem_limit_bytes=63 * 2**20
        ),
        name="layer",
    )(ids, lengths, inverse, attn_gain, mlp_gain, table, wq, wkv, wo, wg, wu, wd)


def local(ids, doc_lengths, table, attn_gain, wq, wkv, wo, mlp_gain, w_gate, w_up, w_down):
    inverse = ROPE_BASE ** (-jnp.arange(HD // 2, dtype=jnp.float32) * 2.0 / HD)
    inverse = jnp.concatenate([inverse, inverse])[None, :]
    return layer(
        ids[None, :], doc_lengths, inverse, attn_gain[None, :], mlp_gain[None, :],
        table, wq, wkv, wo, w_gate.T, w_up.T, w_down,
    )


def solution(mesh):
    placed = (
        P(("dp", "tensor")),
        P(),
        P("tensor", None),
        P(),
        P(None, "tensor"),
        P(None, "tensor"),
        P("tensor", None),
        P(),
        P(None, "tensor"),
        P(None, "tensor"),
        P("tensor", None),
    )
    return jax.shard_map(
        local, mesh=mesh, in_specs=placed, out_specs=P(("dp", "tensor"), None), check_vma=False
    )
```

```python
import jax
import jax.numpy as jnp
from jax import lax
from jax.experimental import pallas as pl
from jax.experimental.pallas import tpu as pltpu
from jax.sharding import PartitionSpec as P

HD = 128
SIDE = 4
GROUP = SIDE * SIDE
SLOTS = 8

EPSILON = 1e-05
ROPE_BASE = 500000.0
NEGATIVE = -1e30
EXP_SCALE = HD ** (-0.5) * 1.4426950408889634
MESH = pl.DeviceIdType.MESH
VMEM = pltpu.VMEM
DMA = pltpu.SemaphoreType.DMA
BF16 = jnp.bfloat16
F32 = jnp.float32


def wrap(v):
    return lax.rem(v + 2 * SIDE, SIDE)


def place(z, x):
    return wrap(z) * SIDE + wrap(x)


def here():
    t = lax.axis_index("tensor")
    return t // SIDE, lax.rem(t, SIDE)


def greet(peers):
    barrier = pltpu.get_barrier_semaphore()
    for peer in peers:
        pl.semaphore_signal(barrier, inc=1, device_id=peer, device_id_type=MESH)
    pl.semaphore_wait(barrier, len(peers))


def remote(src, dst, send_sem, recv_sem, peer):
    return pltpu.make_async_remote_copy(
        src_ref=src, dst_ref=dst, send_sem=send_sem, recv_sem=recv_sem,
        device_id=peer, device_id_type=MESH,
    )


def weave(*streams):
    pending = [[next(g), n, g] for n, g in enumerate(streams)]
    while pending:
        pending.sort(key=lambda entry: entry[:2])
        entry = pending[0]
        entry[0] = next(entry[2], None)
        if entry[0] is None:
            pending.pop(0)


def ring_gather(buf, span, ssem, rsem, z, x, base):
    half = buf.shape[-1] // 2
    quarter = half // 2
    started = []

    def block(h, first, second):
        return place(z + second, x + first) if h == 0 else place(z + first, x + second)

    def view(h, first, second, part):
        start, size = (h * half, half) if part == 0 else (h * half + (part - 1) * quarter, quarter)
        return buf.at[block(h, first, second), span, pl.ds(start, size)]

    def send(h, n, first, second, part, axis, d):
        ref = view(h, first, second, part)
        peer = {"tensor": block(h, d, 0) if axis == 0 else block(h, 0, d)}
        copy = remote(ref, ref, ssem.at[h, n], rsem.at[h, n], peer)
        copy.start()
        started.append(copy)

    def recv(h, n, first, second, part):
        ref = view(h, first, second, part)
        remote(ref, ref, ssem.at[h, n], rsem.at[h, n], {"tensor": block(h, 1, 0)}).wait_recv()

    offsets = (0, -1, 1, 2)

    def relay(n):
        k = offsets[n]
        for h in range(2):
            recv(h, 4 + 2 * n, k, -1, 0)
            send(h, 12 + 2 * n, k, -1, 1, 1, 1)
            recv(h, 5 + 2 * n, k, 1, 0)
            send(h, 13 + 2 * n, k, 1, 2, 1, -1)

    times = [base + v for v in GATHER_TIMES]
    yield times[0]
    for h in range(2):
        send(h, 0, 0, 0, 0, 0, 1)
        send(h, 1, 0, 0, 0, 0, -1)
    for h in range(2):
        send(h, 4, 0, 0, 0, 1, 1)
        send(h, 5, 0, 0, 0, 1, -1)
    yield times[1]
    for h in range(2):
        recv(h, 0, -1, 0, 0)
        send(h, 2, -1, 0, 1, 0, 1)
        recv(h, 1, 1, 0, 0)
        send(h, 3, 1, 0, 2, 0, -1)
        for n in (1, 2):
            send(h, 4 + 2 * n, offsets[n], 0, 0, 1, 1)
            send(h, 5 + 2 * n, offsets[n], 0, 0, 1, -1)
    yield times[2]
    relay(0)
    yield times[3]
    for h in range(2):
        recv(h, 2, 2, 0, 1)
        recv(h, 3, 2, 0, 2)
        send(h, 10, 2, 0, 0, 1, 1)
        send(h, 11, 2, 0, 0, 1, -1)
    for n in (1, 2, 3):
        yield times[3 + n]
        relay(n)
    yield times[7]
    for n in range(4):
        for h in range(2):
            recv(h, 12 + 2 * n, offsets[n], 2, 1)
            recv(h, 13 + 2 * n, offsets[n], 2, 2)
    for copy in started:
        copy.wait_send()


GATHER_TIMES = (0, 4, 5.5, 7, 9, 11, 14, 18)
REDUCE_TIMES = (5, 10, 13, 16)


def ring_reduce(part, span, r1, r2, held, s1, e1, s2, e2, z, x, base, finish):
    half = part.shape[-1] // 2
    quarter = half // 2
    started = []

    def columns(h, q):
        return pl.ds(h * half + q * quarter, quarter)

    def bundle(h, k, q):
        if h == 0:
            return part.at[wrap(z + k), :, span, columns(h, q)]
        return part.at[:, wrap(x + k), span, columns(h, q)]

    def mine(h, j, q):
        if h == 0:
            return part.at[z, wrap(x + j), span, columns(h, q)]
        return part.at[wrap(z + j), x, span, columns(h, q)]

    def other(h, j):
        return wrap(x + j) if h == 0 else wrap(z + j)

    def peer(h, axis, d):
        along_z = (h == 0) == (axis == 0)
        return {"tensor": place(z + d, x) if along_z else place(z, x + d)}

    def send1(h, slot, src, d):
        copy = remote(src, r1.at[h, slot], s1.at[h, slot], e1.at[h, slot], peer(h, 0, d))
        copy.start()
        started.append(copy)

    def recv1(h, slot):
        ref = r1.at[h, slot]
        remote(ref, ref, s1.at[h, slot], e1.at[h, slot], peer(h, 0, 1)).wait_recv()

    def send2(h, slot, src, d):
        copy = remote(src, r2.at[h, slot], s2.at[h, slot], e2.at[h, slot], peer(h, 1, d))
        copy.start()
        started.append(copy)

    def recv2(h, slot):
        ref = r2.at[h, slot]
        remote(ref, ref, s2.at[h, slot], e2.at[h, slot], peer(h, 0, 1)).wait_recv()

    def load(ref):
        return ref[...].astype(F32)

    def summed(h, j, q):
        a, b = ((2, 4), (1, 5))[q]
        n = other(h, j)
        return load(mine(h, j, q)) + load(r1.at[h, a, n]) + load(r1.at[h, b, n])

    times = [base + v for v in REDUCE_TIMES]
    for h in range(2):
        send1(h, 0, bundle(h, 2, 0), 1)
        send1(h, 3, bundle(h, 2, 1), -1)
    for h in range(2):
        send1(h, 1, bundle(h, 1, 1), 1)
        send1(h, 4, bundle(h, -1, 0), -1)
    yield times[0]
    for h in range(2):
        for slot, k, q, d in ((0, 1, 0, 1), (3, -1, 1, -1)):
            recv1(h, slot)
            r1[h, slot] = (load(r1.at[h, slot]) + load(bundle(h, k, q))).astype(BF16)
            send1(h, slot + 2, r1.at[h, slot], d)
    yield times[1]
    for h in range(2):
        for slot in (1, 4, 2, 5):
            recv1(h, slot)
        for place_, j, q, slot, d in ((0, 2, 0, 0, 1), (0, 2, 1, 3, -1), (1, 1, 1, 1, 1), (2, -1, 0, 4, -1)):
            held[h, place_, q] = summed(h, j, q).astype(BF16)
            send2(h, slot, held.at[h, place_, q], d)
    yield times[2]
    for h in range(2):
        for place_, j, q, slot, d in ((1, 1, 0, 0, 1), (2, -1, 1, 3, -1)):
            recv2(h, slot)
            held[h, place_, q] = (summed(h, j, q) + load(r2.at[h, slot])).astype(BF16)
            send2(h, slot + 2, held.at[h, place_, q], d)
    yield times[3]
    for h in range(2):
        for slot in (1, 4, 2, 5):
            recv2(h, slot)
        for q in range(2):
            a, b = ((2, 4), (1, 5))[q]
            finish(columns(h, q), summed(h, 0, q) + load(r2.at[h, a]) + load(r2.at[h, b]))
    for copy in started:
        copy.wait_send()


def product(lhs, w_ref, part, span):
    rows = lhs.shape[0] // GROUP

    def column(c, carry):
        cols = pl.ds(pl.multiple_of(c * 512, 512), 512)
        out = jnp.dot(lhs, w_ref[:, cols], preferred_element_type=F32).astype(BF16)
        part[:, :, span, cols] = out.reshape(SIDE, SIDE, rows, 512)
        return carry

    lax.fori_loop(0, part.shape[-1] // 512, column, 0)


def normalize(rows, gain):
    scale = lax.rsqrt(jnp.mean(rows * rows, axis=-1, keepdims=True) + EPSILON)
    return (rows * scale * gain).astype(BF16)


def find_rows(ids_ref, all_ids, wanted_by, table, found, recv, emb_ref, t, peers, sources, load, ks, kr, xs, xr, meanwhile):
    copies = []
    rows, width = emb_ref.shape
    wanted_by[...] = jnp.full_like(wanted_by, -1)
    wanted_by[:, :rows] = jnp.broadcast_to(ids_ref[...], (8, rows))
    for n, p in enumerate(peers):
        copy = remote(wanted_by, all_ids.at[t], ks.at[n], kr.at[n], {"tensor": p})
        copy.start()
        copies.append(copy)
    all_ids[t] = wanted_by[...]
    slots = GROUP * SLOTS
    owned = table.shape[0]
    square = (128, 128)
    row, lane = lax.broadcasted_iota(jnp.int32, square, 0), lax.broadcasted_iota(jnp.int32, square, 1)
    own = jnp.broadcast_to(wanted_by[:1, :], square)
    owner = jnp.right_shift(own, owned.bit_length() - 1).astype(F32)
    same = (owner == owner.T) & (row < lane)
    source = owner * SLOTS + jnp.sum(jnp.where(same, 1.0, 0.0), axis=0, keepdims=True)
    chosen = jnp.where((source == row.astype(F32)) & (own >= 0), 1.0, 0.0).T[:rows].astype(BF16)
    before = jnp.where(row < lane, 1.0, 0.0).astype(BF16)
    for n, p in enumerate(sources):
        remote(wanted_by, all_ids.at[p], ks.at[n], kr.at[n], {"tensor": p}).wait_recv()
    local_rows = all_ids[...].reshape(slots, 128) - t * owned
    inside = (local_rows >= 0) & (local_rows < owned)
    rank = jnp.dot(jnp.where(inside, 1.0, 0.0).astype(BF16), before, preferred_element_type=F32)
    slot = lax.rem(row, SLOTS).astype(F32)
    wanted = jnp.sum(
        jnp.where(inside & (rank == slot), local_rows.astype(F32), 0.0), axis=1, keepdims=True
    )
    pick = lax.broadcasted_iota(jnp.int32, (slots, owned), 1).astype(F32) == wanted
    pick = jnp.where(pick, 1.0, 0.0).astype(BF16)
    load.wait()
    parts = 2
    step = width // parts
    for c in range(parts):
        def fetch(b, carry):
            cols = pl.ds(pl.multiple_of(c * step + b * 512, 512), 512)
            out = jnp.dot(pick, table[:, cols], preferred_element_type=F32).astype(BF16)
            found[:, :, cols] = out.reshape(GROUP, SLOTS, 512)
            return carry

        lax.fori_loop(0, step // 512, fetch, 0)
        cols = pl.ds(c * step, step)
        for n, p in enumerate(peers):
            copy = remote(found.at[p, :, cols], recv.at[t, :, cols], xs.at[c, n], xr.at[c, n], {"tensor": p})
            copy.start()
            copies.append(copy)
        recv[t, :, cols] = found[t, :, cols]
    meanwhile()
    total = jnp.zeros((rows, 1), F32)
    for c in range(parts):
        cols = pl.ds(c * step, step)
        for n, p in enumerate(sources):
            ref = recv.at[p, :, cols]
            remote(ref, ref, xs.at[c, n], xr.at[c, n], {"tensor": p}).wait_recv()
        for b in range(step // 1024):
            cols = pl.ds(c * step + b * 1024, 1024)
            picked = jnp.dot(chosen, recv[:, :, cols].reshape(slots, 1024), preferred_element_type=F32)
            emb_ref[:, cols] = picked.astype(BF16)
            total += jnp.sum(picked * picked, axis=-1, keepdims=True)
    return copies, total


def document_starts(lengths_ref, positions):
    first = jnp.zeros_like(positions)
    start = jnp.int32(0)
    for d in range(lengths_ref.shape[0]):
        first = jnp.where(positions >= start, start, first)
        start = start + lengths_ref[d]
    return first


QB = 256
CHUNKS = 3


class Attention:
    def __init__(self, q, first, at, keys_at, att, win, relay, top, total, acc, ssem, rsem):
        self.refs = q, first, at, keys_at, att, win, top, total, acc
        t = lax.axis_index("tensor")
        self.r = r = lax.axis_index("dp")
        self.y, self.c = y, c = r // 2, lax.rem(r, 2)
        self.kind = kind = lax.rem(t, 2)
        partner = {"tensor": t + 1 - 2 * kind}
        up = {"dp": lax.rem(y + 1, SIDE) * 2 + c}
        down = {"dp": lax.rem(y + SIDE - 1, SIDE) * 2 + c}
        other = {"dp": y * 2 + 1 - c}

        def copies(chunk):
            def copy(n, src, dst, peer):
                return remote(src, dst, ssem.at[chunk, n], rsem.at[chunk, n], peer)

            def block(w, k):
                return win.at[w, k, chunk]

            own = block(4, kind)
            return {
                "swap": copy(0, own, own, partner),
                "swap_in": copy(0, own, block(4, 1 - kind), partner),
                "up": [copy(1 + k, block(4, k), block(2, k), up) for k in range(2)],
                "far_key": copy(3, block(2, 0), block(0, 0), up),
                "down_value": copy(4, block(4, 1), relay.at[chunk], down),
                "far_value": copy(5, relay.at[chunk], block(0, 1), down),
                "near": [copy(6 + k, block(4, k), block(3, k), other) for k in range(2)],
                "cross0": [copy(8 + k, block(2, k), block(1, k), other) for k in range(2)],
                "cross1": [copy(8 + k, block(2, k), block(3, k), other) for k in range(2)],
                "far1": [copy(10 + k, block(0, k), block(1, k), other) for k in range(2)],
            }

        self.copies = copies
        self.has_up, self.has_far = y < SIDE - 1, y < SIDE - 2
        self.got_up, self.got_far = y > 0, y > 1
        self.relays = (y == SIDE - 1) | (y == 0)

    def exchange(self, chunk, base):
        c = self.c
        d = self.copies(chunk)

        def when(condition, *acts):
            @pl.when(condition)
            def _():
                for act in acts:
                    act()

        def starts(name):
            return [copy.start for copy in d[name]]

        def recvs(name):
            return [copy.wait_recv for copy in d[name]]

        def sends(name):
            return [copy.wait_send for copy in d[name]]

        d["swap"].start()
        yield base + 3.5
        d["swap_in"].wait_recv()
        when(self.has_far, d["down_value"].start)
        when(self.has_up, *starts("up"))
        when(c == 0, *starts("near"))
        yield base + 8
        when(self.relays, d["down_value"].wait_recv, d["far_value"].start)
        when(self.got_up, d["up"][0].wait_recv)
        when(self.got_up & self.has_up, d["far_key"].start)
        when(self.got_up, d["up"][1].wait_recv)
        when(self.got_up & (c == 0), *starts("cross0"))
        when(self.got_up & (c == 1), *starts("cross1"))
        when(c == 1, *recvs("near"))
        yield base + 10
        when(self.got_up & (c == 0), *recvs("cross1"))
        yield base + 13
        when(self.got_far, d["far_key"].wait_recv, d["far_value"].wait_recv)
        when(self.got_far & (c == 1), *starts("far1"))
        when(self.got_up & (c == 1), *recvs("cross0"))
        yield base + 15
        when(self.got_far & (c == 0), *recvs("far1"))
        d["swap"].wait_send()
        when(c == 0, *sends("near"))
        when(self.got_up & (c == 0), *sends("cross0"))
        when(self.got_up & (c == 1), *sends("cross1"))
        when(self.got_far & (c == 1), *sends("far1"))
        when(self.has_far, d["down_value"].wait_send)
        when(self.has_up, *sends("up"))
        when(self.relays, d["far_value"].wait_send)
        when(self.got_up & self.has_up, d["far_key"].wait_send)

    def step(self, w, chunk, own):
        q, first_ref, at_ref, keys_at, att, win, m_ref, l_ref, acc_ref = self.refs
        rows = CHUNKS * QB
        span = pl.ds(chunk * QB, QB)
        queries = jnp.concatenate([q[span, :HD], q[span, HD:]], axis=0)
        first = first_ref[:, span]
        first = jnp.concatenate([first, first], axis=1)
        keys = win[w, 0].reshape(rows, HD)
        scores = lax.dot_general(keys, queries, (((1,), (1,)), ((), ())), preferred_element_type=F32)
        at = keys_at[...] + w * rows
        allowed = at >= first
        if own:
            query = at_ref[:, span]
            allowed &= at <= jnp.concatenate([query, query], axis=1)
        scores = jnp.where(allowed, scores, NEGATIVE)
        top = jnp.max(scores, axis=0, keepdims=True) * EXP_SCALE
        if not own:
            old = m_ref[chunk]
            top = jnp.maximum(old, top)
            decay = jnp.exp2(old - top)
        weights = jnp.exp2(scores * EXP_SCALE - top)
        total = jnp.sum(weights, axis=0, keepdims=True)
        added = lax.dot_general(
            win[w, 1].reshape(rows, HD), weights.astype(BF16), (((0,), (0,)), ((), ())), preferred_element_type=F32
        )
        l_ref[chunk] = total if own else l_ref[chunk] * decay + total
        acc_ref[chunk] = added if own else acc_ref[chunk] * decay + added
        m_ref[chunk] = top

    def earlier(self, w, chunk):
        @pl.when(self.r + w >= 4)
        def _():
            self.step(w, chunk, False)

    def finish(self, chunk):
        q, first_ref, at_ref, keys_at, att, win, m_ref, l_ref, acc_ref = self.refs
        span = pl.ds(chunk * QB, QB)
        out = acc_ref[chunk] / l_ref[chunk]
        att[span, :HD] = out[:, :QB].T.astype(BF16)
        att[span, HD:] = out[:, QB:].T.astype(BF16)


def layer_kernel(ids_ref, lengths_ref, inverse_ref, attn_gain_ref, mlp_gain_ref,
                 table_hbm, wq_hbm, wkv_hbm, wo_hbm, wg_hbm, wu_hbm, wd_hbm, out_ref,
                 table, wq, wkv, wo, wg, wu, wd, load_sem,
                 wanted_by, all_ids, found, recv, ks, kr, xs, xr,
                 emb, all_ref, q, cos_ref, sin_ref, first_ref, at_ref, keys_at, gs, gr,
                 win, relay, m_ref, l_ref, acc_ref, att, as_, ar,
                 stream, hid, gs2, gr2,
                 part, r1, r2, held, s1, e1, s2, e2, s1b, e1b, s2b, e2b):
    z, x = here()
    t = lax.axis_index("tensor")
    r = lax.axis_index("dp")
    y, c = r // 2, lax.rem(r, 2)
    loads = [
        pltpu.make_async_copy(src, dst, load_sem.at[n])
        for n, (src, dst) in enumerate((
            (table_hbm, table), (wq_hbm, wq), (wkv_hbm, wkv), (wo_hbm, wo), (wg_hbm, wg), (wu_hbm, wu), (wd_hbm, wd)
        ))
    ]
    for load in loads:
        load.start()
    peers = [lax.rem(t + n, GROUP) for n in range(1, GROUP)]
    sources = [lax.rem(t + GROUP - n, GROUP) for n in range(1, GROUP)]
    greet([{"tensor": p} for p in peers] + [
        {"dp": lax.rem(y + 1, SIDE) * 2 + c}, {"dp": lax.rem(y + SIDE - 1, SIDE) * 2 + c}, {"dp": y * 2 + 1 - c},
    ])
    rows, width = emb.shape
    span_rows = rows * GROUP
    each = rows // CHUNKS
    spans = [pl.ds(chunk * each, each) for chunk in range(CHUNKS)]

    def within(n):
        chunk = n // QB
        return (n - chunk * QB) // each * rows + chunk * each + lax.rem(n, each)

    def positions():
        lanes = within(lax.broadcasted_iota(jnp.int32, (1, span_rows), 1))
        first_ref[...] = document_starts(lengths_ref, r * span_rows + lanes) - (r - 4) * span_rows
        at_ref[...] = 4 * span_rows + lanes
        keys_at[...] = within(lax.broadcasted_iota(jnp.int32, (span_rows, 1), 0))
        sign = jnp.where(lax.broadcasted_iota(jnp.int32, (1, HD), 1) < HD // 2, -1.0, 1.0)

        def turn(b, carry):
            rows_of = pl.ds(pl.multiple_of(b * 64, 64), 64)
            place_of = r * span_rows + within(b * 64 + lax.broadcasted_iota(jnp.int32, (64, HD), 0))
            angle = (place_of - document_starts(lengths_ref, place_of)).astype(F32) * inverse_ref[...]
            cos_ref[rows_of, :] = jnp.cos(angle)
            sin_ref[rows_of, :] = jnp.sin(angle) * sign
            return carry

        lax.fori_loop(0, span_rows // 64, turn, 0)

    copies, total = find_rows(
        ids_ref, all_ids, wanted_by, table, found, recv, emb, t, peers, sources, loads[0], ks, kr, xs, xr, positions
    )
    scale = lax.rsqrt(total / width + EPSILON)
    for b in range(width // 1024):
        cols = pl.ds(b * 1024, 1024)
        all_ref[t, :, cols] = (emb[:, cols].astype(F32) * scale * attn_gain_ref[:, cols]).astype(BF16)
    loads[1].wait()
    loads[2].wait()
    keys_here = lax.rem(t, 2) == 0
    attention = Attention(q, first_ref, at_ref, keys_at, att, win, relay, m_ref, l_ref, acc_ref, as_, ar)

    def project(chunk):
        lhs = all_ref[:, spans[chunk], :].reshape(QB, width)
        span = pl.ds(chunk * QB, QB)
        cos, sin = cos_ref[span, :], sin_ref[span, :]
        queries = jnp.dot(lhs, wq[...], preferred_element_type=F32)
        for h in range(queries.shape[1] // HD):
            head = queries[:, h * HD:(h + 1) * HD]
            q[span, h * HD:(h + 1) * HD] = (head * cos + pltpu.roll(head, HD // 2, 1) * sin).astype(BF16)
        both = jnp.dot(lhs, wkv[...], preferred_element_type=F32)
        turned = both * cos + pltpu.roll(both, HD // 2, 1) * sin
        win[4, attention.kind, chunk] = jnp.where(keys_here, turned, both).astype(BF16)

    last = CHUNKS - 1
    exchanges = []

    def head(chunk):
        base = 9 * chunk
        yield from ring_gather(all_ref, spans[chunk], gs.at[chunk], gr.at[chunk], z, x, base)
        project(chunk)
        if chunk < last:
            yield from attention.exchange(chunk, base + 20)
        else:
            exchanges.append(attention.exchange(chunk, 0))
            next(exchanges[0])

    weave(*[head(chunk) for chunk in range(CHUNKS)])
    exchange = exchanges[0]
    next(exchange)
    for chunk in range(CHUNKS):
        attention.step(4, chunk, True)
    next(exchange)
    for chunk in range(CHUNKS):
        attention.earlier(2 + c, chunk)
    next(exchange)
    for chunk in range(CHUNKS):
        attention.earlier(3 - c, chunk)
    next(exchange)
    loads[3].wait()

    def tail(chunk):
        rows_of = spans[chunk]
        span = pl.ds(chunk * QB, QB)
        base = TAIL_TIMES[0] * chunk
        yield TAIL_TIMES[1] * chunk
        attention.earlier(c, chunk)
        if chunk == 0:
            for _ in exchange:
                pass
        attention.earlier(1 - c, chunk)
        attention.finish(chunk)
        product(att[span, :], wo, part, rows_of)

        def mixed(cols, value):
            stream[rows_of, cols] = (emb[rows_of, cols].astype(F32) + value).astype(BF16)

        buffers = r1.at[chunk], r2.at[chunk], held.at[chunk]
        sems = [s.at[chunk] for s in (s1, e1, s2, e2)]
        yield from ring_reduce(part, rows_of, *buffers, *sems, z, x, base, mixed)
        all_ref[t, rows_of] = normalize(stream[rows_of, :].astype(F32), mlp_gain_ref[...])
        base += REDUCE_TIMES[-1] + 1
        yield from ring_gather(all_ref, rows_of, gs2.at[chunk], gr2.at[chunk], z, x, base)
        if chunk == 0:
            for n in (4, 5, 6):
                loads[n].wait()
        lhs = all_ref[:, rows_of, :].reshape(QB, width)
        across = (((1,), (1,)), ((), ()))
        gated = lax.dot_general(lhs, wg[...], across, preferred_element_type=F32)
        upper = lax.dot_general(lhs, wu[...], across, preferred_element_type=F32)
        hid[...] = (gated / (1.0 + jnp.exp(-gated)) * upper).astype(BF16)
        base += GATHER_TIMES[-1] + 3
        yield base
        product(hid[...], wd, part, rows_of)

        def added(cols, value):
            out_ref[rows_of, cols] = (stream[rows_of, cols].astype(F32) + value).astype(BF16)

        sems = [s.at[chunk] for s in (s1b, e1b, s2b, e2b)]
        yield from ring_reduce(part, rows_of, *buffers, *sems, z, x, base + 3, added)

    weave(*[tail(chunk) for chunk in range(CHUNKS)])
    for copy in copies:
        copy.wait_send()


TAIL_TIMES = (9, 3)


def layer(ids, lengths, inverse, attn_gain, mlp_gain, table, wq, wkv, wo, wg, wu, wd):
    rows, width = ids.shape[1], table.shape[1]
    span = rows * GROUP
    each = rows // CHUNKS
    quarter = width // 4
    whole = pl.BlockSpec(memory_space=VMEM)
    outside = pl.BlockSpec(memory_space=pl.ANY)
    peers = DMA((GROUP - 1,))
    gather_sems = [DMA((CHUNKS, 2, 20))] * 2
    reduce_sems = [DMA((CHUNKS, 2, 6))] * 4
    return pl.pallas_call(
        layer_kernel,
        out_shape=jax.ShapeDtypeStruct((rows, width), BF16),
        in_specs=[whole, pl.BlockSpec(memory_space=pltpu.SMEM)] + [whole] * 3 + [outside] * 7,
        out_specs=whole,
        scratch_shapes=[
            *[VMEM(w.shape, BF16) for w in (table, wq, wkv, wo, wg, wu, wd)], DMA((7,)),
            VMEM((8, 128), jnp.int32), VMEM((GROUP, 8, 128), jnp.int32),
            VMEM((GROUP, SLOTS, width), BF16), VMEM((GROUP, SLOTS, width), BF16),
            peers, peers, DMA((2, GROUP - 1)), DMA((2, GROUP - 1)),
            VMEM((rows, width), BF16), VMEM((GROUP, rows, width), BF16),
            VMEM((span, wq.shape[1]), BF16),
            VMEM((span, HD), F32), VMEM((span, HD), F32),
            VMEM((1, span), jnp.int32), VMEM((1, span), jnp.int32), VMEM((span, 1), jnp.int32), *gather_sems,
            VMEM((5, 2, CHUNKS, QB, HD), BF16), VMEM((CHUNKS, QB, HD), BF16),
            VMEM((CHUNKS, 1, 2 * QB), F32), VMEM((CHUNKS, 1, 2 * QB), F32), VMEM((CHUNKS, HD, 2 * QB), F32),
            VMEM((span, 2 * HD), BF16), DMA((CHUNKS, 12)), DMA((CHUNKS, 12)),
            VMEM((rows, width), BF16), VMEM((QB, wg.shape[0]), BF16), *gather_sems,
            VMEM((SIDE, SIDE, rows, width), BF16),
            VMEM((CHUNKS, 2, 6, SIDE, each, quarter), BF16),
            VMEM((CHUNKS, 2, 6, each, quarter), BF16),
            VMEM((CHUNKS, 2, 3, 2, each, quarter), BF16),
            *reduce_sems, *reduce_sems,
        ],
        compiler_params=pltpu.CompilerParams(
            collective_id=0, has_side_effects=True, vmem_limit_bytes=63 * 2**20
        ),
        name="layer",
    )(ids, lengths, inverse, attn_gain, mlp_gain, table, wq, wkv, wo, wg, wu, wd)


def local(ids, doc_lengths, table, attn_gain, wq, wkv, wo, mlp_gain, w_gate, w_up, w_down):
    inverse = ROPE_BASE ** (-jnp.arange(HD // 2, dtype=jnp.float32) * 2.0 / HD)
    inverse = jnp.concatenate([inverse, inverse])[None, :]
    return layer(
        ids[None, :], doc_lengths, inverse, attn_gain[None, :], mlp_gain[None, :],
        table, wq, wkv, wo, w_gate.T, w_up.T, w_down,
    )


def solution(mesh):
    placed = (
        P(("dp", "tensor")),
        P(),
        P("tensor", None),
        P(),
        P(None, "tensor"),
        P(None, "tensor"),
        P("tensor", None),
        P(),
        P(None, "tensor"),
        P(None, "tensor"),
        P("tensor", None),
    )
    return jax.shard_map(
        local, mesh=mesh, in_specs=placed, out_specs=P(("dp", "tensor"), None), check_vma=False
    )
```

```python
import jax
import jax.numpy as jnp
from jax import lax
from jax.experimental import pallas as pl
from jax.experimental.pallas import tpu as pltpu
from jax.sharding import PartitionSpec as P

HD = 128
SIDE = 4
GROUP = SIDE * SIDE
SLOTS = 8
UNIT = 16
UNITS = 3

EPSILON = 1e-05
ROPE_BASE = 500000.0
NEGATIVE = -1e30
EXP_SCALE = HD ** (-0.5) * 1.4426950408889634
MESH = pl.DeviceIdType.MESH
VMEM = pltpu.VMEM
DMA = pltpu.SemaphoreType.DMA
BF16 = jnp.bfloat16
F32 = jnp.float32


def wrap(v):
    return lax.rem(v + 2 * SIDE, SIDE)


def place(z, x):
    return wrap(z) * SIDE + wrap(x)


def here():
    t = lax.axis_index("tensor")
    return t // SIDE, lax.rem(t, SIDE)


def greet(peers):
    barrier = pltpu.get_barrier_semaphore()
    for peer in peers:
        pl.semaphore_signal(barrier, inc=1, device_id=peer, device_id_type=MESH)
    pl.semaphore_wait(barrier, len(peers))


def remote(src, dst, send_sem, recv_sem, peer):
    return pltpu.make_async_remote_copy(
        src_ref=src, dst_ref=dst, send_sem=send_sem, recv_sem=recv_sem,
        device_id=peer, device_id_type=MESH,
    )


def ring_gather(buf, ssem, rsem, z, x, ready):
    half = buf.shape[-1] // 2
    quarter = half // 2
    started = []

    def block(h, first, second):
        return place(z + second, x + first) if h == 0 else place(z + first, x + second)

    def view(h, first, second, part):
        start, size = (h * half, half) if part == 0 else (h * half + (part - 1) * quarter, quarter)
        return buf.at[block(h, first, second), :, pl.ds(start, size)]

    def send(h, n, first, second, part, axis, d):
        ref = view(h, first, second, part)
        peer = {"tensor": block(h, d, 0) if axis == 0 else block(h, 0, d)}
        copy = remote(ref, ref, ssem.at[h, n], rsem.at[h, n], peer)
        copy.start()
        started.append(copy)

    def recv(h, n, first, second, part):
        ref = view(h, first, second, part)
        remote(ref, ref, ssem.at[h, n], rsem.at[h, n], {"tensor": block(h, 1, 0)}).wait_recv()

    offsets = (0, -1, 1, 2)
    for h in range(2):
        send(h, 0, 0, 0, 0, 0, 1)
        send(h, 1, 0, 0, 0, 0, -1)
    for h in range(2):
        send(h, 4, 0, 0, 0, 1, 1)
        send(h, 5, 0, 0, 0, 1, -1)
    for h in range(2):
        recv(h, 0, -1, 0, 0)
        send(h, 2, -1, 0, 1, 0, 1)
        recv(h, 1, 1, 0, 0)
        send(h, 3, 1, 0, 2, 0, -1)
        for n in (1, 2):
            send(h, 4 + 2 * n, offsets[n], 0, 0, 1, 1)
            send(h, 5 + 2 * n, offsets[n], 0, 0, 1, -1)

    def relay(n):
        k = offsets[n]
        for h in range(2):
            recv(h, 4 + 2 * n, k, -1, 0)
            send(h, 12 + 2 * n, k, -1, 1, 1, 1)
            recv(h, 5 + 2 * n, k, 1, 0)
            send(h, 13 + 2 * n, k, 1, 2, 1, -1)

    relay(0)
    for h in range(2):
        recv(h, 2, 2, 0, 1)
        recv(h, 3, 2, 0, 2)
        send(h, 10, 2, 0, 0, 1, 1)
        send(h, 11, 2, 0, 0, 1, -1)
    relay(1)
    relay(2)

    def far(h, n):
        recv(h, 12 + 2 * n, offsets[n], 2, 1)
        recv(h, 13 + 2 * n, offsets[n], 2, 2)

    far(1, 0)
    ready(0)
    relay(3)
    far(1, 1)
    ready(-1)
    far(1, 2)
    ready(1)
    for n in range(4):
        far(0, n)
    far(1, 3)
    ready(2)
    for copy in started:
        copy.wait_send()


GATHER_SEMS = [DMA((2, 20)), DMA((2, 20))]


def ring_reduce(part, r1, r2, held, s1, e1, s2, e2, z, x, make, finish):
    half = part.shape[-1] // 2
    quarter = half // 2
    started = []

    def at(h, k, j):
        return (wrap(z + k), wrap(x + j)) if h == 0 else (wrap(z + j), wrap(x + k))

    def mine(h, k, j, q):
        a, b = at(h, k, j)
        return part.at[a, pl.ds(b * UNITS, UNITS), :, pl.ds(h * half + q * quarter, quarter)]

    def peer(h, axis, d):
        a, b = at(h, d, 0) if axis == 0 else at(h, 0, d)
        return {"tensor": a * SIDE + b}

    def send1(h, slot, j, src, d):
        copy = remote(src, r1.at[h, slot, j], s1.at[h, slot, j], e1.at[h, slot, j], peer(h, 0, d))
        copy.start()
        started.append(copy)

    def recv1(h, slot, j):
        ref = r1.at[h, slot, j]
        remote(ref, ref, s1.at[h, slot, j], e1.at[h, slot, j], peer(h, 0, 1)).wait_recv()

    def send2(h, slot, src, d):
        copy = remote(src, r2.at[h, slot], s2.at[h, slot], e2.at[h, slot], peer(h, 1, d))
        copy.start()
        started.append(copy)

    def recv2(h, slot):
        ref = r2.at[h, slot]
        remote(ref, ref, s2.at[h, slot], e2.at[h, slot], peer(h, 0, 1)).wait_recv()

    def load(ref):
        return ref[...].astype(F32)

    order = (2, 1, 3, 0)
    for h in range(2):
        make(h, 2)
        for j in order:
            send1(h, 0, j, mine(h, 2, j, 0), 1)
            send1(h, 3, j, mine(h, 2, j, 1), -1)
    for h in range(2):
        make(h, 1)
        for j in order:
            send1(h, 1, j, mine(h, 1, j, 1), 1)
        make(h, 3)
        for j in order:
            send1(h, 4, j, mine(h, 3, j, 0), -1)
    for j in order:
        for h in range(2):
            recv1(h, 0, j)
            r1[h, 0, j] = (load(r1.at[h, 0, j]) + load(mine(h, 1, j, 0))).astype(BF16)
            send1(h, 2, j, r1.at[h, 0, j], 1)
            recv1(h, 3, j)
            r1[h, 3, j] = (load(r1.at[h, 3, j]) + load(mine(h, 3, j, 1))).astype(BF16)
            send1(h, 5, j, r1.at[h, 3, j], -1)
    for h in range(2):
        make(h, 0)

    def arrived(h, j):
        for slot in (1, 4, 2, 5):
            recv1(h, slot, j)

    def summed(h, j, q):
        a, b = ((2, 4), (1, 5))[q]
        return load(mine(h, 0, j, q)) + load(r1.at[h, a, j]) + load(r1.at[h, b, j])

    for h in range(2):
        arrived(h, 2)
        for q, slot, d in ((0, 0, 1), (1, 3, -1)):
            held[h, 0, q] = summed(h, 2, q).astype(BF16)
            send2(h, slot, held.at[h, 0, q], d)
    for h in range(2):
        arrived(h, 1)
        held[h, 1, 1] = summed(h, 1, 1).astype(BF16)
        send2(h, 1, held.at[h, 1, 1], 1)
        arrived(h, 3)
        held[h, 2, 0] = summed(h, 3, 0).astype(BF16)
        send2(h, 4, held.at[h, 2, 0], -1)
    for h in range(2):
        recv2(h, 0)
        held[h, 1, 0] = (summed(h, 1, 0) + load(r2.at[h, 0])).astype(BF16)
        send2(h, 2, held.at[h, 1, 0], 1)
        recv2(h, 3)
        held[h, 2, 1] = (summed(h, 3, 1) + load(r2.at[h, 3])).astype(BF16)
        send2(h, 5, held.at[h, 2, 1], -1)
    for h in range(2):
        arrived(h, 0)
        for slot in (1, 4, 2, 5):
            recv2(h, slot)
        for q in range(2):
            a, b = ((2, 4), (1, 5))[q]
            value = summed(h, 0, q) + load(r2.at[h, a]) + load(r2.at[h, b])
            finish(pl.ds(h * half + q * quarter, quarter), flat(value))
    for copy in started:
        copy.wait_send()


def products(a_ref, w_ref, part, z, x):
    rows, width = UNITS * UNIT, part.shape[3]
    half = width // 2
    step = min(512, half)

    def make(h, k):
        def run(blocks):
            lhs = jnp.concatenate(
                [a_ref[pl.ds(pl.multiple_of((a * SIDE + b) * rows, 16), rows), :] for a, b in blocks], axis=0
            )

            def column(c, carry):
                cols = pl.ds(pl.multiple_of(h * half + c * step, step), step)
                out = jnp.dot(lhs, w_ref[:, cols], preferred_element_type=F32).astype(BF16)
                for n, (a, b) in enumerate(blocks):
                    block = out[n * rows:(n + 1) * rows].reshape(UNITS, UNIT, step)
                    part[a, pl.ds(b * UNITS, UNITS), :, cols] = block
                return carry

            lax.fori_loop(0, half // step, column, 0)

        if h == 0:
            run([(wrap(z + k), b) for b in range(SIDE)])
        else:
            run([(a, wrap(x + k)) for a in range(SIDE)])

    return make


def flat(block):
    return block.reshape(-1, block.shape[-1])


class Spread:
    def __init__(self, wo_hbm, part, ssem, rsem, ysem, yrem, csem, crem, z, x):
        r = lax.axis_index("dp")
        self.y, self.c = r // 2, lax.rem(r, 2)
        self.wo, self.part, self.z, self.x = wo_hbm, part, z, x
        self.sems = (ssem, rsem), (ysem, yrem), (csem, crem)
        self.half = part.shape[-1] // 2
        self.started = []
        self.slices = [(o, h) for h in range(2) for o in (1, 2, 3)]

    def share(self, dy, other=False):
        c = 1 - self.c if other else self.c
        return lax.rem(self.y + dy + SIDE, SIDE) * 2 + c

    def columns(self, h, q):
        quarter = self.half // 2
        return pl.ds(h * self.half, self.half) if q is None else pl.ds(h * self.half + q * quarter, quarter)

    def view(self, o, share, h, q=None):
        unit = 16 * (o - 1) + 2 * share
        a = unit // 12
        return self.part.at[a, pl.ds(unit - a * 12, 2), :, self.columns(h, q)]

    def copy(self, phase, index, src, dst, peer, start):
        send, recv = self.sems[phase]
        copy = remote(src, dst, send.at[index], recv.at[index], peer)
        if start:
            copy.start()
            self.started.append(copy)
        else:
            copy.wait_recv()

    def along(self, h, d):
        return {"tensor": place(self.z + d, self.x) if h == 0 else place(self.z, self.x + d)}

    def plane(self, start):
        own = self.share(0)
        for h in range(2):
            mine = self.wo.at[pl.ds(2 * own, 2), :, self.columns(h, None)]
            for n, (o, d) in enumerate(((3, 1), (1, -1))):
                dst = self.view(o, own, h)
                self.copy(0, h * 4 + n, mine if start else dst, dst, self.along(h, d), start)

    def plane_far(self, start):
        own = self.share(0)
        for h in range(2):
            for n, (o, d) in enumerate(((3, 1), (1, -1))):
                dst = self.view(2, own, h, n)
                self.copy(0, h * 4 + 2 + n, self.view(o, own, h, n) if start else dst, dst, self.along(h, d), start)

    def around(self, d):
        return {"dp": lax.rem(self.y + d + SIDE, SIDE) * 2 + self.c}

    def ring(self, start):
        for n, (o, h) in enumerate(self.slices):
            for k, d in enumerate((1, -1)):
                ref = self.view(o, self.share(0 if start else -d), h)
                self.copy(1, k * 9 + n, ref, ref, self.around(d), start)

    def ring_far(self, start):
        for n in range(3):
            for k, d in enumerate((1, -1)):
                o, h = self.slices[3 * k + n]
                ref = self.view(o, self.share(-d if start else -2 * d), h)
                self.copy(1, k * 9 + 6 + n, ref, ref, self.around(d), start)

    def cores(self, start, steps):
        peer = {"dp": self.y * 2 + 1 - self.c}
        for dy in steps:
            for n, (o, h) in enumerate(self.slices):
                ref = self.view(o, self.share(dy, not start), h)
                self.copy(2, dy * 6 + n, ref, ref, peer, start)

    def drain(self):
        for copy in self.started:
            copy.wait_send()


def short_reduce(att, att_z, att_x, wo, part, mine, got, ssem, rsem, bs, br, z, x, finish):
    half = part.shape[-1] // 2
    quarter = half // 2
    started = []

    def along(h, d):
        return {"tensor": place(z + d, x) if h == 0 else place(z, x + d)}

    def across(h, d):
        return along(1 - h, d)

    def rows_for(h, d):
        return att.at[wrap(z + d)] if h == 0 else att.at[:, pl.ds(wrap(x + d) * UNITS, UNITS)]

    def landing(h, o):
        return (att_z, att_x)[h].at[o - 1]

    def move(h, o):
        return remote(rows_for(h, o), landing(h, SIDE - o), bs.at[h, o - 1], br.at[h, o - 1], along(h, o))

    for h in range(2):
        for o in (2, 1, 3):
            copy = move(h, o)
            copy.start()
            started.append(copy)

    def block(h, j, q):
        n = wrap(x + j) if h == 0 else wrap(z + j)
        return mine.at[h, pl.ds(n * UNITS, UNITS), :, pl.ds(q * quarter, quarter)]

    def send(h, slot, src, d):
        copy = remote(src, got.at[h, slot], ssem.at[h, slot], rsem.at[h, slot], across(h, d))
        copy.start()
        started.append(copy)

    def recv(h, slot):
        ref = got.at[h, slot]
        remote(ref, ref, ssem.at[h, slot], rsem.at[h, slot], across(h, 1)).wait_recv()

    def load(ref):
        return ref[...].astype(F32)

    step = min(512, quarter)

    def make(h, q):
        own = flat(rows_for(h, 0)[...])
        others = jnp.concatenate([flat(landing(h, o)[...]) for o in (1, 2, 3)], axis=1)

        def column(c, carry):
            at = pl.multiple_of(q * quarter + c * step, step)
            cols = pl.ds(h * half + at, step)
            out = jnp.dot(own, flat(wo[:, :, cols]), preferred_element_type=F32)
            weights = part[:, :, :, cols].reshape(3 * own.shape[1], step)
            out = out + jnp.dot(others, weights, preferred_element_type=F32)
            mine[h, :, :, pl.ds(at, step)] = out.astype(BF16).reshape(SIDE * UNITS, UNIT, step)
            return carry

        lax.fori_loop(0, quarter // step, column, 0)

    for q in range(2):
        for h in range(2):
            if q == 0:
                for o in (3, 1, 2):
                    move(h, SIDE - o).wait_recv()
            make(h, q)
            d = 1 - 2 * q
            send(h, 3 * q, block(h, 2, q), d)
            send(h, (4, 1)[q], block(h, -d, q), -d)
    for h in range(2):
        for slot, q, d in ((0, 0, 1), (3, 1, -1)):
            recv(h, slot)
            got[h, slot] = (load(got.at[h, slot]) + load(block(h, d, q))).astype(BF16)
            send(h, slot + 2, got.at[h, slot], d)
    for h in range(2):
        for slot in (1, 4, 2, 5):
            recv(h, slot)
        for q in range(2):
            a, b = ((2, 4), (1, 5))[q]
            value = load(block(h, 0, q)) + load(got.at[h, a]) + load(got.at[h, b])
            finish(pl.ds(h * half + q * quarter, quarter), flat(value))
    for copy in started:
        copy.wait_send()


def normalize(rows, gain):
    scale = lax.rsqrt(jnp.mean(rows * rows, axis=-1, keepdims=True) + EPSILON)
    return (rows * scale * gain).astype(BF16)


def row_group(all_ref, z, dz):
    rows, width = all_ref.shape[1:]
    zz = wrap(z + dz)
    lhs = all_ref[pl.ds(zz * SIDE, SIDE)].reshape(SIDE * rows, width)
    return lhs, pl.ds(pl.multiple_of(zz * SIDE * rows, 16), SIDE * rows)


def find_rows(ids_ref, all_ids, wanted_by, table, found, recv, emb_ref, t, peers, sources, load, ks, kr, xs, xr, meanwhile):
    copies = []
    rows, width = emb_ref.shape
    wanted_by[...] = jnp.full_like(wanted_by, -1)
    wanted_by[:, :rows] = jnp.broadcast_to(ids_ref[...], (8, rows))
    for n, p in enumerate(peers):
        copy = remote(wanted_by, all_ids.at[t], ks.at[n], kr.at[n], {"tensor": p})
        copy.start()
        copies.append(copy)
    all_ids[t] = wanted_by[...]
    slots = GROUP * SLOTS
    owned = table.shape[0]
    square = (128, 128)
    row, lane = lax.broadcasted_iota(jnp.int32, square, 0), lax.broadcasted_iota(jnp.int32, square, 1)
    own = jnp.broadcast_to(wanted_by[:1, :], square)
    owner = jnp.right_shift(own, owned.bit_length() - 1).astype(F32)
    same = (owner == owner.T) & (row < lane)
    source = owner * SLOTS + jnp.sum(jnp.where(same, 1.0, 0.0), axis=0, keepdims=True)
    chosen = jnp.where((source == row.astype(F32)) & (own >= 0), 1.0, 0.0).T[:rows].astype(BF16)
    before = jnp.where(row < lane, 1.0, 0.0).astype(BF16)
    for n, p in enumerate(sources):
        remote(wanted_by, all_ids.at[p], ks.at[n], kr.at[n], {"tensor": p}).wait_recv()
    local_rows = all_ids[...].reshape(slots, 128) - t * owned
    inside = (local_rows >= 0) & (local_rows < owned)
    rank = jnp.dot(jnp.where(inside, 1.0, 0.0).astype(BF16), before, preferred_element_type=F32)
    slot = lax.rem(row, SLOTS).astype(F32)
    wanted = jnp.sum(
        jnp.where(inside & (rank == slot), local_rows.astype(F32), 0.0), axis=1, keepdims=True
    )
    pick = lax.broadcasted_iota(jnp.int32, (slots, owned), 1).astype(F32) == wanted
    pick = jnp.where(pick, 1.0, 0.0).astype(BF16)
    load.wait()
    parts = 2
    step = width // parts
    for c in range(parts):
        def fetch(b, carry):
            cols = pl.ds(pl.multiple_of(c * step + b * 512, 512), 512)
            out = jnp.dot(pick, table[:, cols], preferred_element_type=F32).astype(BF16)
            found[:, :, cols] = out.reshape(GROUP, SLOTS, 512)
            return carry

        lax.fori_loop(0, step // 512, fetch, 0)
        cols = pl.ds(c * step, step)
        for n, p in enumerate(peers):
            copy = remote(found.at[p, :, cols], recv.at[t, :, cols], xs.at[c, n], xr.at[c, n], {"tensor": p})
            copy.start()
            copies.append(copy)
        recv[t, :, cols] = found[t, :, cols]
    meanwhile()
    total = jnp.zeros((rows, 1), F32)
    for c in range(parts):
        cols = pl.ds(c * step, step)
        for n, p in enumerate(sources):
            ref = recv.at[p, :, cols]
            remote(ref, ref, xs.at[c, n], xr.at[c, n], {"tensor": p}).wait_recv()
        for b in range(step // 1024):
            cols = pl.ds(c * step + b * 1024, 1024)
            picked = jnp.dot(chosen, recv[:, :, cols].reshape(slots, 1024), preferred_element_type=F32)
            emb_ref[:, cols] = picked.astype(BF16)
            total += jnp.sum(picked * picked, axis=-1, keepdims=True)
    return copies, total


def document_starts(lengths_ref, positions):
    first = jnp.zeros_like(positions)
    start = jnp.int32(0)
    for d in range(lengths_ref.shape[0]):
        first = jnp.where(positions >= start, start, first)
        start = start + lengths_ref[d]
    return first


QB = 256


def attention(q_ref, first_ref, pair_ref, att_ref, win_ref, relay, m_ref, l_ref, acc_ref, ssem, rsem):
    t = lax.axis_index("tensor")
    r = lax.axis_index("dp")
    y, c = r // 2, lax.rem(r, 2)
    kind = lax.rem(t, 2)
    rows = q_ref.shape[0]
    blocks = rows // QB
    partner = {"tensor": t + 1 - 2 * kind}
    up = {"dp": lax.rem(y + 1, SIDE) * 2 + c}
    down = {"dp": lax.rem(y + SIDE - 1, SIDE) * 2 + c}
    other = {"dp": y * 2 + 1 - c}

    def copy(n, src, dst, peer):
        return remote(src, dst, ssem.at[n], rsem.at[n], peer)

    def step(w, i, count, causal):
        span = pl.ds(i * QB, QB)
        q = jnp.concatenate([q_ref[span, :HD], q_ref[span, HD:]], axis=0)
        first = first_ref[:, span]
        first = jnp.concatenate([first, first], axis=1)
        scores = lax.dot_general(
            win_ref[w, 0, :count, :], q, (((1,), (1,)), ((), ())), preferred_element_type=F32
        )
        at = lax.broadcasted_iota(jnp.int32, (count, 1), 0) + w * rows
        allowed = at >= first
        if causal:
            query = lax.broadcasted_iota(jnp.int32, (1, QB), 1) + (4 * rows + i * QB)
            allowed &= at <= jnp.concatenate([query, query], axis=1)
        scores = jnp.where(allowed, scores, NEGATIVE)
        top = jnp.max(scores, axis=0, keepdims=True) * EXP_SCALE
        if not causal:
            old = m_ref[i]
            top = jnp.maximum(old, top)
            decay = jnp.exp2(old - top)
        weights = jnp.exp2(scores * EXP_SCALE - top)
        total = jnp.sum(weights, axis=0, keepdims=True)
        added = lax.dot_general(
            win_ref[w, 1, :count, :], weights.astype(BF16), (((0,), (0,)), ((), ())),
            preferred_element_type=F32,
        )
        l_ref[i] = total if causal else l_ref[i] * decay + total
        acc_ref[i] = added if causal else acc_ref[i] * decay + added
        m_ref[i] = top

    def earlier(w):
        @pl.when(r + w >= 4)
        def _():
            for i in range(blocks):
                step(w, i, rows, False)

    swap = copy(0, pair_ref, win_ref.at[4, kind], partner)
    swap.start()
    win_ref[4, kind] = pair_ref[...]
    swap_in = copy(0, pair_ref, win_ref.at[4, 1 - kind], partner)
    up_key = copy(1, win_ref.at[4, 0], win_ref.at[2, 0], up)
    up_value = copy(2, win_ref.at[4, 1], win_ref.at[2, 1], up)
    far_key = copy(3, win_ref.at[2, 0], win_ref.at[0, 0], up)
    down_value = copy(4, win_ref.at[4, 1], relay, down)
    far_value = copy(5, relay, win_ref.at[0, 1], down)
    near = [copy(6 + k, win_ref.at[4, k], win_ref.at[3, k], other) for k in range(2)]
    cross0 = [copy(8 + k, win_ref.at[2, k], win_ref.at[1, k], other) for k in range(2)]
    cross1 = [copy(8 + k, win_ref.at[2, k], win_ref.at[3, k], other) for k in range(2)]
    far1 = [copy(10 + k, win_ref.at[0, k], win_ref.at[1, k], other) for k in range(2)]
    has_up, has_far = y < SIDE - 1, y < SIDE - 2
    got_up, got_far = y > 0, y > 1
    relays = (y == SIDE - 1) | (y == 0)
    swap_in.wait_recv()

    @pl.when(has_far)
    def _():
        down_value.start()

    @pl.when(has_up)
    def _():
        up_key.start()
        up_value.start()

    @pl.when(c == 0)
    def _():
        for k in range(2):
            near[k].start()

    for i in range(blocks):
        step(4, i, (i + 1) * QB, True)

    @pl.when(relays)
    def _():
        down_value.wait_recv()
        far_value.start()

    @pl.when(got_up)
    def _():
        up_key.wait_recv()

        @pl.when(has_up)
        def _():
            far_key.start()

        up_value.wait_recv()

        @pl.when(c == 0)
        def _():
            for k in range(2):
                cross0[k].start()

        @pl.when(c == 1)
        def _():
            for k in range(2):
                cross1[k].start()

    @pl.when(c == 1)
    def _():
        for k in range(2):
            near[k].wait_recv()

    earlier(2 + c)

    @pl.when(got_up & (c == 0))
    def _():
        for k in range(2):
            cross1[k].wait_recv()

    earlier(3 - c)

    @pl.when(got_far)
    def _():
        far_key.wait_recv()
        far_value.wait_recv()

        @pl.when(c == 1)
        def _():
            for k in range(2):
                far1[k].start()

    @pl.when(got_up & (c == 1))
    def _():
        for k in range(2):
            cross0[k].wait_recv()

    earlier(c)

    @pl.when(got_far & (c == 0))
    def _():
        for k in range(2):
            far1[k].wait_recv()

    earlier(1 - c)
    for i in range(blocks):
        out = acc_ref[i] / l_ref[i]
        for h in range(2):
            head = out[:, h * QB:(h + 1) * QB].T.astype(BF16)
            for n in range(QB // UNIT):
                unit = i * QB // UNIT + n
                att_ref[unit // 12, unit % 12, :, h * HD:(h + 1) * HD] = head[n * UNIT:(n + 1) * UNIT]

    @pl.when(c == 0)
    def _():
        for k in range(2):
            near[k].wait_send()

    @pl.when(got_up & (c == 0))
    def _():
        for k in range(2):
            cross0[k].wait_send()

    @pl.when(got_up & (c == 1))
    def _():
        for k in range(2):
            cross1[k].wait_send()

    @pl.when(got_far & (c == 1))
    def _():
        for k in range(2):
            far1[k].wait_send()

    @pl.when(has_far)
    def _():
        down_value.wait_send()

    @pl.when(has_up)
    def _():
        up_key.wait_send()
        up_value.wait_send()

    @pl.when(relays)
    def _():
        far_value.wait_send()

    @pl.when(got_up & has_up)
    def _():
        far_key.wait_send()

    swap.wait_send()


def layer_kernel(ids_ref, lengths_ref, inverse_ref, attn_gain_ref, mlp_gain_ref,
                 table_hbm, wq_hbm, wkv_hbm, wo_hbm, wg_hbm, wu_hbm, wd_hbm, out_ref,
                 table, wq, wkv, wo, wg, wu, wd, load_sem,
                 wanted_by, all_ids, found, recv, ks, kr, xs, xr,
                 emb, all_ref, q, pair, cos_ref, sin_ref, first_ref, gs, gr,
                 win, relay, m_ref, l_ref, acc_ref, att, as_, ar,
                 stream, hid, gs2, gr2,
                 part, r1, r2, held, s1, e1, s2, e2,
                 att_z, att_x, mine, got, ss, sr, bs, br, ps, pr, ys, yr, cs, cr):
    z, x = here()
    t = lax.axis_index("tensor")
    r = lax.axis_index("dp")
    y, c = r // 2, lax.rem(r, 2)
    loads = [
        pltpu.make_async_copy(src, dst, load_sem.at[n])
        for n, (src, dst) in enumerate((
            (table_hbm, table), (wq_hbm, wq), (wkv_hbm, wkv), (wo_hbm, wo), (wg_hbm, wg), (wu_hbm, wu), (wd_hbm, wd)
        ))
    ]
    for load in loads:
        load.start()
    peers = [lax.rem(t + n, GROUP) for n in range(1, GROUP)]
    sources = [lax.rem(t + GROUP - n, GROUP) for n in range(1, GROUP)]
    greet([{"tensor": p} for p in peers] + [
        {"dp": lax.rem(y + 1, SIDE) * 2 + c}, {"dp": lax.rem(y + SIDE - 1, SIDE) * 2 + c}, {"dp": y * 2 + 1 - c},
    ])
    rows, width = emb.shape
    span_rows = rows * GROUP
    spread = Spread(wo_hbm, part, ps, pr, ys, yr, cs, cr, z, x)
    spread.plane(True)

    def positions():
        spread.plane(False)
        spread.plane_far(True)
        lanes = r * span_rows + lax.broadcasted_iota(jnp.int32, (1, span_rows), 1)
        first_ref[...] = document_starts(lengths_ref, lanes) - (r - 4) * span_rows
        sign = jnp.where(lax.broadcasted_iota(jnp.int32, (1, HD), 1) < HD // 2, -1.0, 1.0)

        def turn(b, carry):
            at = pl.ds(pl.multiple_of(b * 64, 64), 64)
            place_of = r * span_rows + b * 64 + lax.broadcasted_iota(jnp.int32, (64, HD), 0)
            angle = (place_of - document_starts(lengths_ref, place_of)).astype(F32) * inverse_ref[...]
            cos_ref[at, :] = jnp.cos(angle)
            sin_ref[at, :] = jnp.sin(angle) * sign
            return carry

        lax.fori_loop(0, span_rows // 64, turn, 0)

    copies, total = find_rows(
        ids_ref, all_ids, wanted_by, table, found, recv, emb, t, peers, sources, loads[0], ks, kr, xs, xr, positions
    )
    scale = lax.rsqrt(total / width + EPSILON)
    for b in range(width // 1024):
        cols = pl.ds(b * 1024, 1024)
        all_ref[t, :, cols] = (emb[:, cols].astype(F32) * scale * attn_gain_ref[:, cols]).astype(BF16)
    loads[1].wait()
    loads[2].wait()
    keys_here = lax.rem(t, 2) == 0
    spread.plane_far(False)
    spread.ring(True)
    spread.cores(True, (0,))

    def project(dz):
        if dz == 1:
            spread.ring(False)
            spread.ring_far(True)
            spread.cores(True, (1, 3))
        lhs, span = row_group(all_ref, z, dz)
        cos, sin = cos_ref[span, :], sin_ref[span, :]
        queries = jnp.dot(lhs, wq[...], preferred_element_type=F32)
        for h in range(queries.shape[1] // HD):
            head = queries[:, h * HD:(h + 1) * HD]
            q[span, h * HD:(h + 1) * HD] = (head * cos + pltpu.roll(head, HD // 2, 1) * sin).astype(BF16)
        both = jnp.dot(lhs, wkv[...], preferred_element_type=F32)
        turned = both * cos + pltpu.roll(both, HD // 2, 1) * sin
        pair[span, :] = jnp.where(keys_here, turned, both).astype(BF16)

    ring_gather(all_ref, gs, gr, z, x, project)
    spread.ring_far(False)
    spread.cores(True, (2,))
    attention(q, first_ref, pair, att, win, relay, m_ref, l_ref, acc_ref, as_, ar)
    spread.cores(False, (0, 1, 3))

    def mixed(cols, value):
        stream[:, cols] = (emb[:, cols].astype(F32) + value).astype(BF16)

    loads[3].wait()
    spread.cores(False, (2,))
    short_reduce(att, att_z, att_x, wo, part, mine, got, ss, sr, bs, br, z, x, mixed)
    spread.drain()
    all_ref[t] = normalize(stream[...].astype(F32), mlp_gain_ref[...])
    loads[4].wait()
    loads[5].wait()

    def gate(dz):
        lhs, span = row_group(all_ref, z, dz)
        across = (((1,), (1,)), ((), ()))
        gated = lax.dot_general(lhs, wg[...], across, preferred_element_type=F32)
        upper = lax.dot_general(lhs, wu[...], across, preferred_element_type=F32)
        hid[span, :] = (gated / (1.0 + jnp.exp(-gated)) * upper).astype(BF16)

    ring_gather(all_ref, gs2, gr2, z, x, gate)

    def added(cols, value):
        out_ref[:, cols] = (stream[:, cols].astype(F32) + value).astype(BF16)

    loads[6].wait()
    ring_reduce(part, r1, r2, held, s1, e1, s2, e2, z, x, products(hid, wd, part, z, x), added)
    for copy in copies:
        copy.wait_send()


def layer(ids, lengths, inverse, attn_gain, mlp_gain, table, wq, wkv, wo, wg, wu, wd):
    rows, width = ids.shape[1], table.shape[1]
    span = rows * GROUP
    blocks = span // QB
    quarter = width // 4
    unit = (UNITS, UNIT)
    whole = pl.BlockSpec(memory_space=VMEM)
    outside = pl.BlockSpec(memory_space=pl.ANY)
    peers = DMA((GROUP - 1,))
    reduce_sems = [DMA((2, 6, SIDE)), DMA((2, 6, SIDE)), DMA((2, 6)), DMA((2, 6))]
    return pl.pallas_call(
        layer_kernel,
        out_shape=jax.ShapeDtypeStruct((rows, width), BF16),
        in_specs=[whole, pl.BlockSpec(memory_space=pltpu.SMEM)] + [whole] * 3 + [outside] * 7,
        out_specs=whole,
        scratch_shapes=[
            *[VMEM(w.shape, BF16) for w in (table, wq, wkv, wo, wg, wu, wd)], DMA((7,)),
            VMEM((8, 128), jnp.int32), VMEM((GROUP, 8, 128), jnp.int32),
            VMEM((GROUP, SLOTS, width), BF16), VMEM((GROUP, SLOTS, width), BF16),
            peers, peers, DMA((2, GROUP - 1)), DMA((2, GROUP - 1)),
            VMEM((rows, width), BF16), VMEM((GROUP, rows, width), BF16),
            VMEM((span, wq.shape[1]), BF16), VMEM((span, HD), BF16),
            VMEM((span, HD), F32), VMEM((span, HD), F32), VMEM((1, span), jnp.int32), *GATHER_SEMS,
            VMEM((5, 2, span, HD), BF16), VMEM((span, HD), BF16),
            VMEM((blocks, 1, 2 * QB), F32), VMEM((blocks, 1, 2 * QB), F32), VMEM((blocks, HD, 2 * QB), F32),
            VMEM((SIDE, SIDE * UNITS, UNIT, 2 * HD), BF16), DMA((12,)), DMA((12,)),
            VMEM((rows, width), BF16), VMEM((span, wg.shape[0]), BF16), *GATHER_SEMS,
            VMEM((SIDE, SIDE * UNITS, UNIT, width), BF16),
            VMEM((2, 6, SIDE, *unit, quarter), BF16),
            VMEM((2, 6, *unit, quarter), BF16),
            VMEM((2, 3, 2, *unit, quarter), BF16),
            *reduce_sems,
            VMEM((SIDE - 1, SIDE * UNITS, UNIT, 2 * HD), BF16), VMEM((SIDE - 1, SIDE, *unit, 2 * HD), BF16),
            VMEM((2, SIDE * UNITS, UNIT, 2 * quarter), BF16), VMEM((2, 6, *unit, quarter), BF16),
            DMA((2, 6)), DMA((2, 6)), DMA((2, 3)), DMA((2, 3)),
            DMA((8,)), DMA((8,)), DMA((18,)), DMA((18,)), DMA((24,)), DMA((24,)),
        ],
        compiler_params=pltpu.CompilerParams(
            collective_id=0, has_side_effects=True, vmem_limit_bytes=63 * 2**20
        ),
        name="layer",
    )(ids, lengths, inverse, attn_gain, mlp_gain, table, wq, wkv, wo, wg, wu, wd)


def local(ids, doc_lengths, table, attn_gain, wq, wkv, wo, mlp_gain, w_gate, w_up, w_down):
    inverse = ROPE_BASE ** (-jnp.arange(HD // 2, dtype=jnp.float32) * 2.0 / HD)
    inverse = jnp.concatenate([inverse, inverse])[None, :]
    return layer(
        ids[None, :], doc_lengths, inverse, attn_gain[None, :], mlp_gain[None, :],
        table, wq, wkv, wo.reshape(-1, UNIT, wo.shape[1]), w_gate.T, w_up.T, w_down,
    )


def solution(mesh):
    placed = (
        P(("dp", "tensor")),
        P(),
        P("tensor", None),
        P(),
        P(None, "tensor"),
        P(None, "tensor"),
        P("tensor", None),
        P(),
        P(None, "tensor"),
        P(None, "tensor"),
        P("tensor", None),
    )
    return jax.shard_map(
        local, mesh=mesh, in_specs=placed, out_specs=P(("dp", "tensor"), None), check_vma=False
    )
```

```python
import functools

import jax
import jax.numpy as jnp
from jax import lax
from jax.experimental import pallas as pl
from jax.experimental.pallas import tpu as pltpu
from jax.sharding import PartitionSpec as P

HD = 128
SIDE = 4
GROUP = SIDE * SIDE
SLOTS = 8
UNIT = 16
UNITS = 3

EPSILON = 1e-05
ROPE_BASE = 500000.0
NEGATIVE = -1e30
EXP_SCALE = HD ** (-0.5) * 1.4426950408889634
MESH = pl.DeviceIdType.MESH
VMEM = pltpu.VMEM
DMA = pltpu.SemaphoreType.DMA
BF16 = jnp.bfloat16
F32 = jnp.float32


def wrap(v):
    return lax.rem(v + 2 * SIDE, SIDE)


def place(z, x):
    return wrap(z) * SIDE + wrap(x)


def here():
    t = lax.axis_index("tensor")
    return t // SIDE, lax.rem(t, SIDE)


def greet(peers):
    barrier = pltpu.get_barrier_semaphore()
    for peer in peers:
        pl.semaphore_signal(barrier, inc=1, device_id=peer, device_id_type=MESH)
    pl.semaphore_wait(barrier, len(peers))


def remote(src, dst, send_sem, recv_sem, peer):
    return pltpu.make_async_remote_copy(
        src_ref=src, dst_ref=dst, send_sem=send_sem, recv_sem=recv_sem,
        device_id=peer, device_id_type=MESH,
    )


def ring_gather(buf, ssem, rsem, z, x, ready):
    half = buf.shape[-1] // 2
    quarter = half // 2
    started = []

    def block(h, first, second):
        return place(z + second, x + first) if h == 0 else place(z + first, x + second)

    def view(h, first, second, part):
        start, size = (h * half, half) if part == 0 else (h * half + (part - 1) * quarter, quarter)
        return buf.at[block(h, first, second), :, pl.ds(start, size)]

    def send(h, n, first, second, part, axis, d):
        ref = view(h, first, second, part)
        peer = {"tensor": block(h, d, 0) if axis == 0 else block(h, 0, d)}
        copy = remote(ref, ref, ssem.at[h, n], rsem.at[h, n], peer)
        copy.start()
        started.append(copy)

    def recv(h, n, first, second, part):
        ref = view(h, first, second, part)
        remote(ref, ref, ssem.at[h, n], rsem.at[h, n], {"tensor": block(h, 1, 0)}).wait_recv()

    offsets = (0, -1, 1, 2)
    for h in range(2):
        send(h, 0, 0, 0, 0, 0, 1)
        send(h, 1, 0, 0, 0, 0, -1)
    for h in range(2):
        send(h, 4, 0, 0, 0, 1, 1)
        send(h, 5, 0, 0, 0, 1, -1)
    for h in range(2):
        recv(h, 0, -1, 0, 0)
        send(h, 2, -1, 0, 1, 0, 1)
        recv(h, 1, 1, 0, 0)
        send(h, 3, 1, 0, 2, 0, -1)
        for n in (1, 2):
            send(h, 4 + 2 * n, offsets[n], 0, 0, 1, 1)
            send(h, 5 + 2 * n, offsets[n], 0, 0, 1, -1)

    def relay(n):
        k = offsets[n]
        for h in range(2):
            recv(h, 4 + 2 * n, k, -1, 0)
            send(h, 12 + 2 * n, k, -1, 1, 1, 1)
            recv(h, 5 + 2 * n, k, 1, 0)
            send(h, 13 + 2 * n, k, 1, 2, 1, -1)

    relay(0)
    for h in range(2):
        recv(h, 2, 2, 0, 1)
        recv(h, 3, 2, 0, 2)
        send(h, 10, 2, 0, 0, 1, 1)
        send(h, 11, 2, 0, 0, 1, -1)
    relay(1)
    relay(2)

    def far(h, n):
        recv(h, 12 + 2 * n, offsets[n], 2, 1)
        recv(h, 13 + 2 * n, offsets[n], 2, 2)

    far(1, 0)
    ready(0)
    relay(3)
    far(1, 1)
    ready(-1)
    far(1, 2)
    ready(1)
    for n in range(4):
        far(0, n)
    far(1, 3)
    ready(2)
    for copy in started:
        copy.wait_send()


GATHER_SEMS = [DMA((2, 20)), DMA((2, 20))]


def flat(block):
    return block.reshape(-1, block.shape[-1])


class Spread:
    def __init__(self, wo_hbm, part, ssem, rsem, ysem, yrem, csem, crem, z, x):
        r = lax.axis_index("dp")
        self.y, self.c = r // 2, lax.rem(r, 2)
        self.wo, self.part, self.z, self.x = wo_hbm, part, z, x
        self.sems = (ssem, rsem), (ysem, yrem), (csem, crem)
        self.half = part.shape[-1] // 2
        self.started = []
        self.slices = [(o, h) for h in range(2) for o in (1, 2, 3)]

    def share(self, dy, other=False):
        c = 1 - self.c if other else self.c
        return lax.rem(self.y + dy + SIDE, SIDE) * 2 + c

    def columns(self, h, q):
        quarter = self.half // 2
        return pl.ds(h * self.half, self.half) if q is None else pl.ds(h * self.half + q * quarter, quarter)

    def view(self, o, share, h, q=None):
        unit = 16 * (o - 1) + 2 * share
        a = unit // 12
        return self.part.at[a, pl.ds(unit - a * 12, 2), :, self.columns(h, q)]

    def copy(self, phase, index, src, dst, peer, start):
        send, recv = self.sems[phase]
        copy = remote(src, dst, send.at[index], recv.at[index], peer)
        if start:
            copy.start()
            self.started.append(copy)
        else:
            copy.wait_recv()

    def along(self, h, d):
        return {"tensor": place(self.z + d, self.x) if h == 0 else place(self.z, self.x + d)}

    def plane(self, start):
        own = self.share(0)
        for h in range(2):
            mine = self.wo.at[pl.ds(2 * own, 2), :, self.columns(h, None)]
            for n, (o, d) in enumerate(((3, 1), (1, -1))):
                dst = self.view(o, own, h)
                self.copy(0, h * 4 + n, mine if start else dst, dst, self.along(h, d), start)

    def plane_far(self, start):
        own = self.share(0)
        for h in range(2):
            for n, (o, d) in enumerate(((3, 1), (1, -1))):
                dst = self.view(2, own, h, n)
                self.copy(0, h * 4 + 2 + n, self.view(o, own, h, n) if start else dst, dst, self.along(h, d), start)

    def around(self, d):
        return {"dp": lax.rem(self.y + d + SIDE, SIDE) * 2 + self.c}

    def ring(self, start):
        for n, (o, h) in enumerate(self.slices):
            for k, d in enumerate((1, -1)):
                ref = self.view(o, self.share(0 if start else -d), h)
                self.copy(1, k * 9 + n, ref, ref, self.around(d), start)

    def ring_far(self, start):
        for n in range(3):
            for k, d in enumerate((1, -1)):
                o, h = self.slices[3 * k + n]
                ref = self.view(o, self.share(-d if start else -2 * d), h)
                self.copy(1, k * 9 + 6 + n, ref, ref, self.around(d), start)

    def cores(self, start, steps):
        peer = {"dp": self.y * 2 + 1 - self.c}
        for dy in steps:
            for n, (o, h) in enumerate(self.slices):
                ref = self.view(o, self.share(dy, not start), h)
                self.copy(2, dy * 6 + n, ref, ref, peer, start)

    def drain(self):
        for copy in self.started:
            copy.wait_send()


class SpreadDown:
    def __init__(self, w_hbm, blocks, sems, z, x):
        r = lax.axis_index("dp")
        self.y, self.c = r // 2, lax.rem(r, 2)
        self.w, self.blocks, self.sems, self.z, self.x = w_hbm, blocks, sems, z, x
        self.units = blocks.shape[1] // SIDE
        self.half = blocks.shape[-1] // 2
        self.started = []

    def columns(self, c, q=None):
        size = self.half if q is None else self.half // 2
        start = c * self.half + (0 if q is None else q * size)
        return pl.ds(pl.multiple_of(start, size), size)

    def rows(self, dy):
        return pl.ds(lax.rem(self.y + dy + SIDE, SIDE) * self.units, self.units)

    def view(self, o, dy, c, q=None):
        return self.blocks.at[o - 1, self.rows(dy), :, self.columns(c, q)]

    def copy(self, phase, index, src, dst, peer, start):
        send, recv = self.sems[2 * phase:2 * phase + 2]
        copy = remote(src, dst, send.at[index], recv.at[index], peer)
        if start:
            copy.start()
            self.started.append(copy)
        else:
            copy.wait_recv()

    def along(self, d):
        return {"tensor": place(self.z + d * (1 - self.c), self.x + d * self.c)}

    def plane(self, start):
        for n, (o, d) in enumerate(((3, 1), (1, -1))):
            dst = self.view(o, 0, self.c)
            src = self.w.at[self.rows(0), :, self.columns(self.c)] if start else dst
            self.copy(0, n, src, dst, self.along(d), start)

    def plane_far(self, start):
        for n, (o, d) in enumerate(((3, 1), (1, -1))):
            dst = self.view(2, 0, self.c, n)
            self.copy(0, 2 + n, self.view(o, 0, self.c, n) if start else dst, dst, self.along(d), start)

    def around(self, d):
        return {"dp": lax.rem(self.y + d + SIDE, SIDE) * 2 + self.c}

    def ring(self, start):
        for o in (1, 2, 3):
            for k, d in enumerate((1, -1)):
                ref = self.view(o, 0 if start else -d, self.c)
                self.copy(1, k * 6 + o - 1, ref, ref, self.around(d), start)

    def ring_far(self, start):
        for o in (1, 2, 3):
            for k, d in enumerate((1, -1)):
                ref = self.view(o, -d if start else -2 * d, self.c, k)
                self.copy(1, k * 6 + 2 + o, ref, ref, self.around(d), start)

    def cores(self, start, steps):
        peer = {"dp": self.y * 2 + 1 - self.c}
        for dy in steps:
            for o in (1, 2, 3):
                ref = self.view(o, dy, self.c if start else 1 - self.c)
                self.copy(2, dy * 3 + o - 1, ref, ref, peer, start)

    def drain(self):
        for copy in self.started:
            copy.wait_send()


def short_reduce(mine, got, ssem, rsem, z, x, arrive, multiply, finish):
    half = mine.shape[-1]
    quarter = half // 2
    started = []

    def block(h, j, q):
        n = wrap(x + j) if h == 0 else wrap(z + j)
        return mine.at[h, pl.ds(n * UNITS, UNITS), :, pl.ds(q * quarter, quarter)]

    def send(h, slot, src, d):
        peer = {"tensor": place(z, x + d) if h == 0 else place(z + d, x)}
        copy = remote(src, got.at[h, slot], ssem.at[h, slot], rsem.at[h, slot], peer)
        copy.start()
        started.append(copy)

    def recv(h, slot):
        ref = got.at[h, slot]
        remote(ref, ref, ssem.at[h, slot], rsem.at[h, slot], {"tensor": place(z, x + 1)}).wait_recv()

    def load(ref):
        return ref[...].astype(F32)

    step = min(512, quarter)

    def make(h, q):
        def column(c, carry):
            at = pl.multiple_of(q * quarter + c * step, step)
            out = multiply(h, pl.ds(h * half + at, step)).astype(BF16)
            mine[h, :, :, pl.ds(at, step)] = out.reshape(SIDE * UNITS, UNIT, step)
            return carry

        lax.fori_loop(0, quarter // step, column, 0)

    for q in range(2):
        for h in range(2):
            if q == 0:
                arrive(h)
            make(h, q)
            d = 1 - 2 * q
            send(h, 3 * q, block(h, 2, q), d)
            send(h, (4, 1)[q], block(h, -d, q), -d)
    for h in range(2):
        for slot, q, d in ((0, 0, 1), (3, 1, -1)):
            recv(h, slot)
            got[h, slot] = (load(got.at[h, slot]) + load(block(h, d, q))).astype(BF16)
            send(h, slot + 2, got.at[h, slot], d)
    for h in range(2):
        for slot in (1, 4, 2, 5):
            recv(h, slot)
        for q in range(2):
            a, b = ((2, 4), (1, 5))[q]
            value = load(block(h, 0, q)) + load(got.at[h, a]) + load(got.at[h, b])
            finish(pl.ds(h * half + q * quarter, quarter), flat(value))
    for copy in started:
        copy.wait_send()


def mix(att, att_z, att_x, wo, part, mine, got, ssem, rsem, bs, br, z, x, finish):
    started = []

    def rows_for(h, d):
        return att.at[wrap(z + d)] if h == 0 else att.at[:, pl.ds(wrap(x + d) * UNITS, UNITS)]

    def landing(h, o):
        return (att_z, att_x)[h].at[o - 1]

    def move(h, o):
        peer = {"tensor": place(z + o, x) if h == 0 else place(z, x + o)}
        return remote(rows_for(h, o), landing(h, SIDE - o), bs.at[h, o - 1], br.at[h, o - 1], peer)

    for h in range(2):
        for o in (2, 1, 3):
            copy = move(h, o)
            copy.start()
            started.append(copy)

    def arrive(h):
        for o in (3, 1, 2):
            move(h, SIDE - o).wait_recv()

    def multiply(h, cols):
        own = flat(rows_for(h, 0)[...])
        others = jnp.concatenate([flat(landing(h, o)[...]) for o in (1, 2, 3)], axis=1)
        out = jnp.dot(own, flat(wo[:, :, cols]), preferred_element_type=F32)
        weights = part[:, :, :, cols].reshape(others.shape[1], out.shape[1])
        return out + jnp.dot(others, weights, preferred_element_type=F32)

    short_reduce(mine, got, ssem, rsem, z, x, arrive, multiply, finish)
    for copy in started:
        copy.wait_send()


def normalize(rows, gain):
    scale = lax.rsqrt(jnp.mean(rows * rows, axis=-1, keepdims=True) + EPSILON)
    return (rows * scale * gain).astype(BF16)


def row_group(all_ref, z, dz):
    rows, width = all_ref.shape[1:]
    zz = wrap(z + dz)
    lhs = all_ref[pl.ds(zz * SIDE, SIDE)].reshape(SIDE * rows, width)
    return lhs, pl.ds(pl.multiple_of(zz * SIDE * rows, 16), SIDE * rows)


def find_rows(ids_ref, all_ids, wanted_by, table, found, recv, emb_ref, t, peers, sources, load, ks, kr, xs, xr, meanwhile):
    copies = []
    rows, width = emb_ref.shape
    wanted_by[...] = jnp.full_like(wanted_by, -1)
    wanted_by[:, :rows] = jnp.broadcast_to(ids_ref[...], (8, rows))
    for n, p in enumerate(peers):
        copy = remote(wanted_by, all_ids.at[t], ks.at[n], kr.at[n], {"tensor": p})
        copy.start()
        copies.append(copy)
    all_ids[t] = wanted_by[...]
    slots = GROUP * SLOTS
    owned = table.shape[0]
    square = (128, 128)
    row, lane = lax.broadcasted_iota(jnp.int32, square, 0), lax.broadcasted_iota(jnp.int32, square, 1)
    own = jnp.broadcast_to(wanted_by[:1, :], square)
    owner = jnp.right_shift(own, owned.bit_length() - 1).astype(F32)
    same = (owner == owner.T) & (row < lane)
    source = owner * SLOTS + jnp.sum(jnp.where(same, 1.0, 0.0), axis=0, keepdims=True)
    chosen = jnp.where((source == row.astype(F32)) & (own >= 0), 1.0, 0.0).T[:rows].astype(BF16)
    before = jnp.where(row < lane, 1.0, 0.0).astype(BF16)
    for n, p in enumerate(sources):
        remote(wanted_by, all_ids.at[p], ks.at[n], kr.at[n], {"tensor": p}).wait_recv()
    local_rows = all_ids[...].reshape(slots, 128) - t * owned
    inside = (local_rows >= 0) & (local_rows < owned)
    rank = jnp.dot(jnp.where(inside, 1.0, 0.0).astype(BF16), before, preferred_element_type=F32)
    slot = lax.rem(row, SLOTS).astype(F32)
    wanted = jnp.sum(
        jnp.where(inside & (rank == slot), local_rows.astype(F32), 0.0), axis=1, keepdims=True
    )
    pick = lax.broadcasted_iota(jnp.int32, (slots, owned), 1).astype(F32) == wanted
    pick = jnp.where(pick, 1.0, 0.0).astype(BF16)
    load.wait()
    parts = 2
    step = width // parts
    for c in range(parts):
        def fetch(b, carry):
            cols = pl.ds(pl.multiple_of(c * step + b * 512, 512), 512)
            out = jnp.dot(pick, table[:, cols], preferred_element_type=F32).astype(BF16)
            found[:, :, cols] = out.reshape(GROUP, SLOTS, 512)
            return carry

        lax.fori_loop(0, step // 512, fetch, 0)
        cols = pl.ds(c * step, step)
        for n, p in enumerate(peers):
            copy = remote(found.at[p, :, cols], recv.at[t, :, cols], xs.at[c, n], xr.at[c, n], {"tensor": p})
            copy.start()
            copies.append(copy)
        recv[t, :, cols] = found[t, :, cols]
    meanwhile()
    total = jnp.zeros((rows, 1), F32)
    for c in range(parts):
        cols = pl.ds(c * step, step)
        for n, p in enumerate(sources):
            ref = recv.at[p, :, cols]
            remote(ref, ref, xs.at[c, n], xr.at[c, n], {"tensor": p}).wait_recv()
        for b in range(step // 1024):
            cols = pl.ds(c * step + b * 1024, 1024)
            picked = jnp.dot(chosen, recv[:, :, cols].reshape(slots, 1024), preferred_element_type=F32)
            emb_ref[:, cols] = picked.astype(BF16)
            total += jnp.sum(picked * picked, axis=-1, keepdims=True)
    return copies, total


def document_starts(lengths_ref, positions):
    first = jnp.zeros_like(positions)
    start = jnp.int32(0)
    for d in range(lengths_ref.shape[0]):
        first = jnp.where(positions >= start, start, first)
        start = start + lengths_ref[d]
    return first


QB = 256


def attention(q_ref, first_ref, pair_ref, att_ref, win_ref, relay, m_ref, l_ref, acc_ref, ssem, rsem, early, late):
    t = lax.axis_index("tensor")
    r = lax.axis_index("dp")
    y, c = r // 2, lax.rem(r, 2)
    kind = lax.rem(t, 2)
    rows = q_ref.shape[0]
    blocks = rows // QB
    partner = {"tensor": t + 1 - 2 * kind}
    up = {"dp": lax.rem(y + 1, SIDE) * 2 + c}
    down = {"dp": lax.rem(y + SIDE - 1, SIDE) * 2 + c}
    other = {"dp": y * 2 + 1 - c}

    def copy(n, src, dst, peer):
        return remote(src, dst, ssem.at[n], rsem.at[n], peer)

    def step(w, i, count, causal):
        span = pl.ds(i * QB, QB)
        q = jnp.concatenate([q_ref[span, :HD], q_ref[span, HD:]], axis=0)
        first = first_ref[:, span]
        first = jnp.concatenate([first, first], axis=1)
        scores = lax.dot_general(
            win_ref[w, 0, :count, :], q, (((1,), (1,)), ((), ())), preferred_element_type=F32
        )
        at = lax.broadcasted_iota(jnp.int32, (count, 1), 0) + w * rows
        allowed = at >= first
        if causal:
            query = lax.broadcasted_iota(jnp.int32, (1, QB), 1) + (4 * rows + i * QB)
            allowed &= at <= jnp.concatenate([query, query], axis=1)
        scores = jnp.where(allowed, scores, NEGATIVE)
        top = jnp.max(scores, axis=0, keepdims=True) * EXP_SCALE
        if not causal:
            old = m_ref[i]
            top = jnp.maximum(old, top)
            decay = jnp.exp2(old - top)
        weights = jnp.exp2(scores * EXP_SCALE - top)
        total = jnp.sum(weights, axis=0, keepdims=True)
        added = lax.dot_general(
            win_ref[w, 1, :count, :], weights.astype(BF16), (((0,), (0,)), ((), ())),
            preferred_element_type=F32,
        )
        l_ref[i] = total if causal else l_ref[i] * decay + total
        acc_ref[i] = added if causal else acc_ref[i] * decay + added
        m_ref[i] = top

    def earlier(w):
        @pl.when(r + w >= 4)
        def _():
            for i in range(blocks):
                step(w, i, rows, False)

    swap = copy(0, pair_ref, win_ref.at[4, kind], partner)
    swap.start()
    win_ref[4, kind] = pair_ref[...]
    swap_in = copy(0, pair_ref, win_ref.at[4, 1 - kind], partner)
    up_key = copy(1, win_ref.at[4, 0], win_ref.at[2, 0], up)
    up_value = copy(2, win_ref.at[4, 1], win_ref.at[2, 1], up)
    far_key = copy(3, win_ref.at[2, 0], win_ref.at[0, 0], up)
    down_value = copy(4, win_ref.at[4, 1], relay, down)
    far_value = copy(5, relay, win_ref.at[0, 1], down)
    near = [copy(6 + k, win_ref.at[4, k], win_ref.at[3, k], other) for k in range(2)]
    cross0 = [copy(8 + k, win_ref.at[2, k], win_ref.at[1, k], other) for k in range(2)]
    cross1 = [copy(8 + k, win_ref.at[2, k], win_ref.at[3, k], other) for k in range(2)]
    far1 = [copy(10 + k, win_ref.at[0, k], win_ref.at[1, k], other) for k in range(2)]
    has_up, has_far = y < SIDE - 1, y < SIDE - 2
    got_up, got_far = y > 0, y > 1
    relays = (y == SIDE - 1) | (y == 0)
    swap_in.wait_recv()

    @pl.when(has_far)
    def _():
        down_value.start()

    @pl.when(has_up)
    def _():
        up_key.start()
        up_value.start()

    @pl.when(c == 0)
    def _():
        for k in range(2):
            near[k].start()

    early()
    for i in range(blocks):
        step(4, i, (i + 1) * QB, True)

    @pl.when(relays)
    def _():
        down_value.wait_recv()
        far_value.start()

    @pl.when(got_up)
    def _():
        up_key.wait_recv()

        @pl.when(has_up)
        def _():
            far_key.start()

        up_value.wait_recv()

        @pl.when(c == 0)
        def _():
            for k in range(2):
                cross0[k].start()

        @pl.when(c == 1)
        def _():
            for k in range(2):
                cross1[k].start()

    @pl.when(c == 1)
    def _():
        for k in range(2):
            near[k].wait_recv()

    earlier(2 + c)

    @pl.when(got_up & (c == 0))
    def _():
        for k in range(2):
            cross1[k].wait_recv()

    earlier(3 - c)
    late()

    @pl.when(got_far)
    def _():
        far_key.wait_recv()
        far_value.wait_recv()

        @pl.when(c == 1)
        def _():
            for k in range(2):
                far1[k].start()

    @pl.when(got_up & (c == 1))
    def _():
        for k in range(2):
            cross0[k].wait_recv()

    earlier(c)

    @pl.when(got_far & (c == 0))
    def _():
        for k in range(2):
            far1[k].wait_recv()

    earlier(1 - c)
    for i in range(blocks):
        out = acc_ref[i] / l_ref[i]
        for h in range(2):
            head = out[:, h * QB:(h + 1) * QB].T.astype(BF16)
            for n in range(QB // UNIT):
                unit = i * QB // UNIT + n
                att_ref[unit // 12, unit % 12, :, h * HD:(h + 1) * HD] = head[n * UNIT:(n + 1) * UNIT]

    @pl.when(c == 0)
    def _():
        for k in range(2):
            near[k].wait_send()

    @pl.when(got_up & (c == 0))
    def _():
        for k in range(2):
            cross0[k].wait_send()

    @pl.when(got_up & (c == 1))
    def _():
        for k in range(2):
            cross1[k].wait_send()

    @pl.when(got_far & (c == 1))
    def _():
        for k in range(2):
            far1[k].wait_send()

    @pl.when(has_far)
    def _():
        down_value.wait_send()

    @pl.when(has_up)
    def _():
        up_key.wait_send()
        up_value.wait_send()

    @pl.when(relays)
    def _():
        far_value.wait_send()

    @pl.when(got_up & has_up)
    def _():
        far_key.wait_send()

    swap.wait_send()


def layer_kernel(ids_ref, lengths_ref, inverse_ref, attn_gain_ref, mlp_gain_ref,
                 table_hbm, wq_hbm, wkv_hbm, wo_hbm, wg_hbm, wu_hbm, wd_hbm, out_ref,
                 table, wq, wkv, wo, wg, wu, wd, load_sem,
                 wanted_by, all_ids, found, recv, ks, kr, xs, xr,
                 emb, all_ref, q, pair, cos_ref, sin_ref, first_ref, gs, gr,
                 win, relay, m_ref, l_ref, acc_ref, att, as_, ar,
                 stream, hid, gs2, gr2,
                 part, att_z, att_x, mine, got, ss, sr, bs, br, ps, pr, ys, yr, cs, cr,
                 down_blocks, hid_z, hid_x, ss2, sr2, zs, zr, hs, hr, *down_sems):
    z, x = here()
    t = lax.axis_index("tensor")
    r = lax.axis_index("dp")
    y, c = r // 2, lax.rem(r, 2)
    loads = [
        pltpu.make_async_copy(src, dst, load_sem.at[n])
        for n, (src, dst) in enumerate((
            (table_hbm, table), (wq_hbm, wq), (wkv_hbm, wkv), (wo_hbm, wo), (wg_hbm, wg), (wu_hbm, wu), (wd_hbm, wd)
        ))
    ]
    for load in loads:
        load.start()
    peers = [lax.rem(t + n, GROUP) for n in range(1, GROUP)]
    sources = [lax.rem(t + GROUP - n, GROUP) for n in range(1, GROUP)]
    greet([{"tensor": p} for p in peers] + [
        {"dp": lax.rem(y + 1, SIDE) * 2 + c}, {"dp": lax.rem(y + SIDE - 1, SIDE) * 2 + c}, {"dp": y * 2 + 1 - c},
    ])
    rows, width = emb.shape
    span_rows = rows * GROUP
    spread = Spread(wo_hbm, part, ps, pr, ys, yr, cs, cr, z, x)
    spread.plane(True)
    down = SpreadDown(wd_hbm, down_blocks, down_sems, z, x)
    hidden_width = wg.shape[0]

    def positions():
        hid[:, :, :, hidden_width:] = jnp.zeros((*hid.shape[:3], hid.shape[3] - hidden_width), BF16)
        spread.plane(False)
        spread.plane_far(True)
        lanes = r * span_rows + lax.broadcasted_iota(jnp.int32, (1, span_rows), 1)
        first_ref[...] = document_starts(lengths_ref, lanes) - (r - 4) * span_rows
        sign = jnp.where(lax.broadcasted_iota(jnp.int32, (1, HD), 1) < HD // 2, -1.0, 1.0)

        def turn(b, carry):
            at = pl.ds(pl.multiple_of(b * 64, 64), 64)
            place_of = r * span_rows + b * 64 + lax.broadcasted_iota(jnp.int32, (64, HD), 0)
            angle = (place_of - document_starts(lengths_ref, place_of)).astype(F32) * inverse_ref[...]
            cos_ref[at, :] = jnp.cos(angle)
            sin_ref[at, :] = jnp.sin(angle) * sign
            return carry

        lax.fori_loop(0, span_rows // 64, turn, 0)

    copies, total = find_rows(
        ids_ref, all_ids, wanted_by, table, found, recv, emb, t, peers, sources, loads[0], ks, kr, xs, xr, positions
    )
    scale = lax.rsqrt(total / width + EPSILON)
    for b in range(width // 1024):
        cols = pl.ds(b * 1024, 1024)
        all_ref[t, :, cols] = (emb[:, cols].astype(F32) * scale * attn_gain_ref[:, cols]).astype(BF16)
    loads[1].wait()
    loads[2].wait()
    keys_here = lax.rem(t, 2) == 0
    spread.plane_far(False)
    spread.ring(True)
    spread.cores(True, (0,))

    def project(dz):
        if dz == 1:
            spread.ring(False)
            spread.ring_far(True)
            spread.cores(True, (1, 3))
        lhs, span = row_group(all_ref, z, dz)
        cos, sin = cos_ref[span, :], sin_ref[span, :]
        queries = jnp.dot(lhs, wq[...], preferred_element_type=F32)
        for h in range(queries.shape[1] // HD):
            head = queries[:, h * HD:(h + 1) * HD]
            q[span, h * HD:(h + 1) * HD] = (head * cos + pltpu.roll(head, HD // 2, 1) * sin).astype(BF16)
        both = jnp.dot(lhs, wkv[...], preferred_element_type=F32)
        turned = both * cos + pltpu.roll(both, HD // 2, 1) * sin
        pair[span, :] = jnp.where(keys_here, turned, both).astype(BF16)

    ring_gather(all_ref, gs, gr, z, x, project)
    spread.ring_far(False)
    spread.cores(True, (2,))

    def late():
        down.plane(False)
        down.plane_far(True)

    attention(
        q, first_ref, pair, att, win, relay, m_ref, l_ref, acc_ref, as_, ar, functools.partial(down.plane, True), late
    )
    spread.cores(False, (0, 1, 3))
    down.plane_far(False)
    down.ring(True)
    down.cores(True, (0,))

    def mixed(cols, value):
        stream[:, cols] = (emb[:, cols].astype(F32) + value).astype(BF16)

    loads[3].wait()
    spread.cores(False, (2,))
    mix(att, att_z, att_x, wo, part, mine, got, ss, sr, bs, br, z, x, mixed)
    spread.drain()
    all_ref[t] = normalize(stream[...].astype(F32), mlp_gain_ref[...])
    loads[4].wait()
    loads[5].wait()

    loads[6].wait()
    moves = []

    def hidden_to_z(dz):
        o = dz % SIDE
        return remote(
            hid.at[wrap(z + dz)], hid_z.at[SIDE - o - 1], zs.at[o - 1], zr.at[o - 1], {"tensor": place(z + o, x)}
        )

    def hidden_to_x(dz, o):
        src = hid.at[wrap(z + dz), pl.ds(wrap(x + o) * UNITS, UNITS)]
        dst = hid_x.at[SIDE - o - 1, wrap(z + dz)]
        return remote(src, dst, hs.at[dz % SIDE, o - 1], hr.at[dz % SIDE, o - 1], {"tensor": place(z, x + o)})

    def gate(dz):
        if dz == 0:
            down.ring(False)
            down.ring_far(True)
            down.cores(True, (1, 3))
        lhs, span = row_group(all_ref, z, dz)
        across = (((1,), (1,)), ((), ()))
        gated = lax.dot_general(lhs, wg[...], across, preferred_element_type=F32)
        upper = lax.dot_general(lhs, wu[...], across, preferred_element_type=F32)
        value = (gated / (1.0 + jnp.exp(-gated)) * upper).astype(BF16)
        hid[wrap(z + dz), :, :, :hidden_width] = value.reshape(SIDE * UNITS, UNIT, hidden_width)
        if dz:
            moves.append(hidden_to_z(dz))
        moves.extend(hidden_to_x(dz, o) for o in (2, 1, 3))
        for copy in moves[-4 if dz else -3:]:
            copy.start()

    ring_gather(all_ref, gs2, gr2, z, x, gate)
    down.ring_far(False)
    down.cores(True, (2,))

    def arrive(h):
        if h == 0:
            for dz in (-1, 1, 2):
                hidden_to_z(dz).wait_recv()
            down.cores(False, (0, 1, 3, 2))
        else:
            for dz in (0, -1, 1, 2):
                for o in (1, 3, 2):
                    hidden_to_x(dz, o).wait_recv()

    def multiply(h, cols):
        def left(block):
            return block.reshape(-1, hidden_width)

        own = hid[z, :, :, :hidden_width] if h == 0 else hid[:, pl.ds(x * UNITS, UNITS), :, :hidden_width]
        out = jnp.dot(left(own), flat(wd[:, :, cols]), preferred_element_type=F32)
        for n in range(SIDE - 1):
            block = hid_z[n, :, :, :hidden_width] if h == 0 else hid_x[n, :, :, :, :hidden_width]
            out = out + jnp.dot(left(block), flat(down_blocks[n, :, :, cols]), preferred_element_type=F32)
        return out

    def added(cols, value):
        out_ref[:, cols] = (stream[:, cols].astype(F32) + value).astype(BF16)

    short_reduce(mine, got, ss2, sr2, z, x, arrive, multiply, added)
    for copy in moves:
        copy.wait_send()
    down.drain()
    for copy in copies:
        copy.wait_send()


def layer(ids, lengths, inverse, attn_gain, mlp_gain, table, wq, wkv, wo, wg, wu, wd):
    rows, width = ids.shape[1], table.shape[1]
    span = rows * GROUP
    blocks = span // QB
    quarter = width // 4
    unit = (UNITS, UNIT)
    padded = -(-wg.shape[0] // 128) * 128
    whole = pl.BlockSpec(memory_space=VMEM)
    outside = pl.BlockSpec(memory_space=pl.ANY)
    peers = DMA((GROUP - 1,))
    return pl.pallas_call(
        layer_kernel,
        out_shape=jax.ShapeDtypeStruct((rows, width), BF16),
        in_specs=[whole, pl.BlockSpec(memory_space=pltpu.SMEM)] + [whole] * 3 + [outside] * 7,
        out_specs=whole,
        scratch_shapes=[
            *[VMEM(w.shape, BF16) for w in (table, wq, wkv, wo, wg, wu, wd)], DMA((7,)),
            VMEM((8, 128), jnp.int32), VMEM((GROUP, 8, 128), jnp.int32),
            VMEM((GROUP, SLOTS, width), BF16), VMEM((GROUP, SLOTS, width), BF16),
            peers, peers, DMA((2, GROUP - 1)), DMA((2, GROUP - 1)),
            VMEM((rows, width), BF16), VMEM((GROUP, rows, width), BF16),
            VMEM((span, wq.shape[1]), BF16), VMEM((span, HD), BF16),
            VMEM((span, HD), F32), VMEM((span, HD), F32), VMEM((1, span), jnp.int32), *GATHER_SEMS,
            VMEM((5, 2, span, HD), BF16), VMEM((span, HD), BF16),
            VMEM((blocks, 1, 2 * QB), F32), VMEM((blocks, 1, 2 * QB), F32), VMEM((blocks, HD, 2 * QB), F32),
            VMEM((SIDE, SIDE * UNITS, UNIT, 2 * HD), BF16), DMA((12,)), DMA((12,)),
            VMEM((rows, width), BF16), VMEM((SIDE, SIDE * UNITS, UNIT, padded), BF16), *GATHER_SEMS,
            VMEM((SIDE, SIDE * UNITS, UNIT, width), BF16),
            VMEM((SIDE - 1, SIDE * UNITS, UNIT, 2 * HD), BF16), VMEM((SIDE - 1, SIDE, *unit, 2 * HD), BF16),
            VMEM((2, SIDE * UNITS, UNIT, 2 * quarter), BF16), VMEM((2, 6, *unit, quarter), BF16),
            DMA((2, 6)), DMA((2, 6)), DMA((2, 3)), DMA((2, 3)),
            DMA((8,)), DMA((8,)), DMA((18,)), DMA((18,)), DMA((24,)), DMA((24,)),
            VMEM((SIDE - 1, *wd.shape), BF16),
            VMEM((SIDE - 1, SIDE * UNITS, UNIT, padded), BF16), VMEM((SIDE - 1, SIDE, *unit, padded), BF16),
            DMA((2, 6)), DMA((2, 6)), DMA((SIDE - 1,)), DMA((SIDE - 1,)), DMA((SIDE, SIDE - 1)), DMA((SIDE, SIDE - 1)),
            DMA((4,)), DMA((4,)), DMA((12,)), DMA((12,)), DMA((12,)), DMA((12,)),
        ],
        compiler_params=pltpu.CompilerParams(
            collective_id=0, has_side_effects=True, vmem_limit_bytes=63 * 2**20
        ),
        name="layer",
    )(ids, lengths, inverse, attn_gain, mlp_gain, table, wq, wkv, wo, wg, wu, wd)


def local(ids, doc_lengths, table, attn_gain, wq, wkv, wo, mlp_gain, w_gate, w_up, w_down):
    inverse = ROPE_BASE ** (-jnp.arange(HD // 2, dtype=jnp.float32) * 2.0 / HD)
    inverse = jnp.concatenate([inverse, inverse])[None, :]
    return layer(
        ids[None, :], doc_lengths, inverse, attn_gain[None, :], mlp_gain[None, :],
        table, wq, wkv, wo.reshape(-1, UNIT, wo.shape[1]), w_gate.T, w_up.T, w_down.reshape(-1, UNIT, wo.shape[1]),
    )


def solution(mesh):
    placed = (
        P(("dp", "tensor")),
        P(),
        P("tensor", None),
        P(),
        P(None, "tensor"),
        P(None, "tensor"),
        P("tensor", None),
        P(),
        P(None, "tensor"),
        P(None, "tensor"),
        P("tensor", None),
    )
    return jax.shard_map(
        local, mesh=mesh, in_specs=placed, out_specs=P(("dp", "tensor"), None), check_vma=False
    )
```

```python
import functools

import jax
import jax.numpy as jnp
import numpy as np
from jax import lax
from jax.experimental import pallas as pl
from jax.experimental.pallas import tpu as pltpu
from jax.sharding import PartitionSpec as P

HD = 128
SIDE = 4
GROUP = SIDE * SIDE
SLOTS = 8
UNIT = 16
UNITS = 3

EPSILON = 1e-05
ROPE_BASE = 500000.0
NEGATIVE = -1e30
EXP_SCALE = HD ** (-0.5) * 1.4426950408889634
MESH = pl.DeviceIdType.MESH
VMEM = pltpu.VMEM
DMA = pltpu.SemaphoreType.DMA
BF16 = jnp.bfloat16
F32 = jnp.float32


def wrap(v):
    return lax.rem(v + 2 * SIDE, SIDE)


def place(z, x):
    return wrap(z) * SIDE + wrap(x)


def here():
    t = lax.axis_index("tensor")
    return t // SIDE, lax.rem(t, SIDE)


def greet(peers):
    barrier = pltpu.get_barrier_semaphore()
    for peer in peers:
        pl.semaphore_signal(barrier, inc=1, device_id=peer, device_id_type=MESH)
    pl.semaphore_wait(barrier, len(peers))


def remote(src, dst, send_sem, recv_sem, peer):
    return pltpu.make_async_remote_copy(
        src_ref=src, dst_ref=dst, send_sem=send_sem, recv_sem=recv_sem,
        device_id=peer, device_id_type=MESH,
    )


def ring_gather(buf, ssem, rsem, z, x, ready):
    half = buf.shape[-1] // 2
    quarter = half // 2
    started = []

    def block(h, first, second):
        return place(z + second, x + first) if h == 0 else place(z + first, x + second)

    def view(h, first, second, part):
        start, size = (h * half, half) if part == 0 else (h * half + (part - 1) * quarter, quarter)
        return buf.at[block(h, first, second), :, pl.ds(start, size)]

    def send(h, n, first, second, part, axis, d):
        ref = view(h, first, second, part)
        peer = {"tensor": block(h, d, 0) if axis == 0 else block(h, 0, d)}
        copy = remote(ref, ref, ssem.at[h, n], rsem.at[h, n], peer)
        copy.start()
        started.append(copy)

    def recv(h, n, first, second, part):
        ref = view(h, first, second, part)
        remote(ref, ref, ssem.at[h, n], rsem.at[h, n], {"tensor": block(h, 1, 0)}).wait_recv()

    offsets = (0, -1, 1, 2)
    for h in range(2):
        send(h, 0, 0, 0, 0, 0, 1)
        send(h, 1, 0, 0, 0, 0, -1)
    for h in range(2):
        send(h, 4, 0, 0, 0, 1, 1)
        send(h, 5, 0, 0, 0, 1, -1)
    for h in range(2):
        recv(h, 0, -1, 0, 0)
        send(h, 2, -1, 0, 1, 0, 1)
        recv(h, 1, 1, 0, 0)
        send(h, 3, 1, 0, 2, 0, -1)
        for n in (1, 2):
            send(h, 4 + 2 * n, offsets[n], 0, 0, 1, 1)
            send(h, 5 + 2 * n, offsets[n], 0, 0, 1, -1)

    def relay(n):
        k = offsets[n]
        for h in range(2):
            recv(h, 4 + 2 * n, k, -1, 0)
            send(h, 12 + 2 * n, k, -1, 1, 1, 1)
            recv(h, 5 + 2 * n, k, 1, 0)
            send(h, 13 + 2 * n, k, 1, 2, 1, -1)

    relay(0)
    for h in range(2):
        recv(h, 2, 2, 0, 1)
        recv(h, 3, 2, 0, 2)
        send(h, 10, 2, 0, 0, 1, 1)
        send(h, 11, 2, 0, 0, 1, -1)
    relay(1)
    relay(2)

    def far(h, n):
        recv(h, 12 + 2 * n, offsets[n], 2, 1)
        recv(h, 13 + 2 * n, offsets[n], 2, 2)

    far(1, 0)
    ready(0)
    relay(3)
    far(1, 1)
    ready(-1)
    far(1, 2)
    ready(1)
    for n in range(4):
        far(0, n)
    far(1, 3)
    ready(2)
    for copy in started:
        copy.wait_send()


GATHER_SEMS = [DMA((2, 20)), DMA((2, 20))]


def flat(block):
    return block.reshape(-1, block.shape[-1])


def flat_units(block):
    return block.reshape(-1, UNIT, block.shape[-1])


class Moves:
    def __init__(self, rows, to_z, to_x, zs, zr, xs, xr, z, x):
        self.refs = rows, to_z, to_x, zs, zr, xs, xr
        self.z, self.x = z, x
        self.started = []

    def along_z(self, dz):
        rows, to_z, to_x, zs, zr, xs, xr = self.refs
        o = dz % SIDE
        peer = {"tensor": place(self.z + o, self.x)}
        return remote(rows.at[wrap(self.z + dz)], to_z.at[SIDE - o - 1], zs.at[o - 1], zr.at[o - 1], peer)

    def along_x(self, dz, o):
        rows, to_z, to_x, zs, zr, xs, xr = self.refs
        zz = wrap(self.z + dz)
        src = rows.at[zz, pl.ds(wrap(self.x + o) * UNITS, UNITS)]
        sems = xs.at[dz % SIDE, o - 1], xr.at[dz % SIDE, o - 1]
        return remote(src, to_x.at[SIDE - o - 1, zz], *sems, {"tensor": place(self.z, self.x + o)})

    def finished(self, dz):
        moves = [self.along_z(dz)] if dz else []
        moves += [self.along_x(dz, o) for o in (2, 1, 3)]
        for move in moves:
            move.start()
        self.started += moves

    def arrive(self, h):
        if h == 0:
            for dz in (-1, 1, 2):
                self.along_z(dz).wait_recv()
        else:
            for dz in (2, 1, -1, 0):
                for o in (1, 3, 2):
                    self.along_x(dz, o).wait_recv()

    def drain(self):
        for move in self.started:
            move.wait_send()


class Spread:
    def __init__(self, wo_hbm, part, ssem, rsem, ysem, yrem, csem, crem, z, x):
        r = lax.axis_index("dp")
        self.y, self.c = r // 2, lax.rem(r, 2)
        self.wo, self.part, self.z, self.x = wo_hbm, part, z, x
        self.sems = (ssem, rsem), (ysem, yrem), (csem, crem)
        self.half = part.shape[-1] // 2
        self.started = []
        self.slices = [(o, h) for h in range(2) for o in (1, 2, 3)]

    def share(self, dy, other=False):
        c = 1 - self.c if other else self.c
        return lax.rem(self.y + dy + SIDE, SIDE) * 2 + c

    def columns(self, h, q):
        quarter = self.half // 2
        return pl.ds(h * self.half, self.half) if q is None else pl.ds(h * self.half + q * quarter, quarter)

    def view(self, o, share, h, q=None):
        unit = 16 * (o - 1) + 2 * share
        a = unit // 12
        return self.part.at[a, pl.ds(unit - a * 12, 2), :, self.columns(h, q)]

    def copy(self, phase, index, src, dst, peer, start):
        send, recv = self.sems[phase]
        copy = remote(src, dst, send.at[index], recv.at[index], peer)
        if start:
            copy.start()
            self.started.append(copy)
        else:
            copy.wait_recv()

    def along(self, h, d):
        return {"tensor": place(self.z + d, self.x) if h == 0 else place(self.z, self.x + d)}

    def plane(self, start):
        own = self.share(0)
        for h in range(2):
            mine = self.wo.at[pl.ds(2 * own, 2), :, self.columns(h, None)]
            for n, (o, d) in enumerate(((3, 1), (1, -1))):
                dst = self.view(o, own, h)
                self.copy(0, h * 4 + n, mine if start else dst, dst, self.along(h, d), start)

    def plane_far(self, start):
        own = self.share(0)
        for h in range(2):
            for n, (o, d) in enumerate(((3, 1), (1, -1))):
                dst = self.view(2, own, h, n)
                self.copy(0, h * 4 + 2 + n, self.view(o, own, h, n) if start else dst, dst, self.along(h, d), start)

    def around(self, d):
        return {"dp": lax.rem(self.y + d + SIDE, SIDE) * 2 + self.c}

    def ring(self, start):
        for n, (o, h) in enumerate(self.slices):
            for k, d in enumerate((1, -1)):
                ref = self.view(o, self.share(0 if start else -d), h)
                self.copy(1, k * 9 + n, ref, ref, self.around(d), start)

    def ring_far(self, start):
        for n in range(3):
            for k, d in enumerate((1, -1)):
                o, h = self.slices[3 * k + n]
                ref = self.view(o, self.share(-d if start else -2 * d), h)
                self.copy(1, k * 9 + 6 + n, ref, ref, self.around(d), start)

    def cores(self, start, steps):
        peer = {"dp": self.y * 2 + 1 - self.c}
        for dy in steps:
            for n, (o, h) in enumerate(self.slices):
                ref = self.view(o, self.share(dy, not start), h)
                self.copy(2, dy * 6 + n, ref, ref, peer, start)

    def drain(self):
        for copy in self.started:
            copy.wait_send()


class SpreadDown:
    def __init__(self, w_hbm, blocks, sems, z, x):
        r = lax.axis_index("dp")
        self.y, self.c = r // 2, lax.rem(r, 2)
        self.w, self.blocks, self.sems, self.z, self.x = w_hbm, blocks, sems, z, x
        self.units = blocks.shape[1] // SIDE
        self.half = blocks.shape[-1] // 2
        self.started = []

    def columns(self, c, q=None):
        size = self.half if q is None else self.half // 2
        start = c * self.half + (0 if q is None else q * size)
        return pl.ds(pl.multiple_of(start, size), size)

    def rows(self, dy):
        return pl.ds(lax.rem(self.y + dy + SIDE, SIDE) * self.units, self.units)

    def view(self, o, dy, c, q=None):
        return self.blocks.at[o - 1, self.rows(dy), :, self.columns(c, q)]

    def copy(self, phase, index, src, dst, peer, start):
        send, recv = self.sems[2 * phase:2 * phase + 2]
        copy = remote(src, dst, send.at[index], recv.at[index], peer)
        if start:
            copy.start()
            self.started.append(copy)
        else:
            copy.wait_recv()

    def along(self, d):
        return {"tensor": place(self.z + d * (1 - self.c), self.x + d * self.c)}

    def plane(self, start):
        for n, (o, d) in enumerate(((3, 1), (1, -1))):
            dst = self.view(o, 0, self.c)
            src = self.w.at[self.rows(0), :, self.columns(self.c)] if start else dst
            self.copy(0, n, src, dst, self.along(d), start)

    def plane_far(self, start):
        for n, (o, d) in enumerate(((3, 1), (1, -1))):
            dst = self.view(2, 0, self.c, n)
            self.copy(0, 2 + n, self.view(o, 0, self.c, n) if start else dst, dst, self.along(d), start)

    def around(self, d):
        return {"dp": lax.rem(self.y + d + SIDE, SIDE) * 2 + self.c}

    def ring(self, start):
        for o in (1, 2, 3):
            for k, d in enumerate((1, -1)):
                ref = self.view(o, 0 if start else -d, self.c)
                self.copy(1, k * 6 + o - 1, ref, ref, self.around(d), start)

    def ring_far(self, start):
        for o in (1, 2, 3):
            for k, d in enumerate((1, -1)):
                ref = self.view(o, -d if start else -2 * d, self.c, k)
                self.copy(1, k * 6 + 2 + o, ref, ref, self.around(d), start)

    def cores(self, start, steps):
        peer = {"dp": self.y * 2 + 1 - self.c}
        for dy in steps:
            for o in (1, 2, 3):
                ref = self.view(o, dy, self.c if start else 1 - self.c)
                self.copy(2, dy * 3 + o - 1, ref, ref, peer, start)

    def drain(self):
        for copy in self.started:
            copy.wait_send()


def short_reduce(mine, got, ssem, rsem, z, x, arrive, multiply, finish):
    half = mine.shape[-1]
    quarter = half // 2
    started = []

    def block(h, j, q):
        n = wrap(x + j) if h == 0 else wrap(z + j)
        return mine.at[h, pl.ds(n * UNITS, UNITS), :, pl.ds(q * quarter, quarter)]

    def send(h, slot, src, d):
        peer = {"tensor": place(z, x + d) if h == 0 else place(z + d, x)}
        copy = remote(src, got.at[h, slot], ssem.at[h, slot], rsem.at[h, slot], peer)
        copy.start()
        started.append(copy)

    def recv(h, slot):
        ref = got.at[h, slot]
        remote(ref, ref, ssem.at[h, slot], rsem.at[h, slot], {"tensor": place(z, x + 1)}).wait_recv()

    def load(ref):
        return ref[...].astype(F32)

    step = min(512, quarter)

    def make(h, q):
        def column(c, carry):
            at = pl.multiple_of(q * quarter + c * step, step)
            out = multiply(h, pl.ds(h * half + at, step)).astype(BF16)
            mine[h, :, :, pl.ds(at, step)] = out.reshape(SIDE * UNITS, UNIT, step)
            return carry

        lax.fori_loop(0, quarter // step, column, 0)

    for q in range(2):
        for h in range(2):
            if q == 0:
                arrive(h)
            make(h, q)
            d = 1 - 2 * q
            send(h, 3 * q, block(h, 2, q), d)
            send(h, (4, 1)[q], block(h, -d, q), -d)
    for h in range(2):
        for slot, q, d in ((0, 0, 1), (3, 1, -1)):
            recv(h, slot)
            got[h, slot] = (load(got.at[h, slot]) + load(block(h, d, q))).astype(BF16)
            send(h, slot + 2, got.at[h, slot], d)
    for h in range(2):
        for slot in (1, 4, 2, 5):
            recv(h, slot)
        for q in range(2):
            a, b = ((2, 4), (1, 5))[q]
            value = load(block(h, 0, q)) + load(got.at[h, a]) + load(got.at[h, b])
            finish(pl.ds(h * half + q * quarter, quarter), flat(value))
    for copy in started:
        copy.wait_send()


def mix(moves, att, att_z, att_x, wo, part, mine, got, ssem, rsem, z, x, finish):
    def multiply(h, cols):
        own = flat(att[z] if h == 0 else att[:, pl.ds(x * UNITS, UNITS)])
        others = jnp.concatenate([flat((att_z, att_x)[h][n]) for n in range(SIDE - 1)], axis=1)
        out = jnp.dot(own, flat(wo[:, :, cols]), preferred_element_type=F32)
        weights = part[:, :, :, cols].reshape(others.shape[1], out.shape[1])
        return out + jnp.dot(others, weights, preferred_element_type=F32)

    short_reduce(mine, got, ssem, rsem, z, x, moves.arrive, multiply, finish)
    moves.drain()


def normalize(rows, gain):
    scale = lax.rsqrt(jnp.mean(rows * rows, axis=-1, keepdims=True) + EPSILON)
    return (rows * scale * gain).astype(BF16)


def row_group(all_ref, z, dz):
    rows, width = all_ref.shape[1:]
    zz = wrap(z + dz)
    lhs = all_ref[pl.ds(zz * SIDE, SIDE)].reshape(SIDE * rows, width)
    return lhs, pl.ds(pl.multiple_of(zz * SIDE * rows, 16), SIDE * rows)


def find_rows(ids_ref, all_ids, wanted_by, table, found, recv, emb_ref, t, peers, sources, load, ks, kr, xs, xr, meanwhile):
    copies = []
    rows, width = emb_ref.shape
    wanted_by[...] = jnp.full_like(wanted_by, -1)
    wanted_by[:, :rows] = jnp.broadcast_to(ids_ref[...], (8, rows))
    for n, p in enumerate(peers):
        copy = remote(wanted_by, all_ids.at[t], ks.at[n], kr.at[n], {"tensor": p})
        copy.start()
        copies.append(copy)
    all_ids[t] = wanted_by[...]
    slots = GROUP * SLOTS
    owned = table.shape[0]
    square = (128, 128)
    row, lane = lax.broadcasted_iota(jnp.int32, square, 0), lax.broadcasted_iota(jnp.int32, square, 1)
    own = jnp.broadcast_to(wanted_by[:1, :], square)
    owner = jnp.right_shift(own, owned.bit_length() - 1).astype(F32)
    same = (owner == owner.T) & (row < lane)
    source = owner * SLOTS + jnp.sum(jnp.where(same, 1.0, 0.0), axis=0, keepdims=True)
    chosen = jnp.where((source == row.astype(F32)) & (own >= 0), 1.0, 0.0).T[:rows].astype(BF16)
    before = jnp.where(row < lane, 1.0, 0.0).astype(BF16)
    for n, p in enumerate(sources):
        remote(wanted_by, all_ids.at[p], ks.at[n], kr.at[n], {"tensor": p}).wait_recv()
    local_rows = all_ids[...].reshape(slots, 128) - t * owned
    inside = (local_rows >= 0) & (local_rows < owned)
    rank = jnp.dot(jnp.where(inside, 1.0, 0.0).astype(BF16), before, preferred_element_type=F32)
    slot = lax.rem(row, SLOTS).astype(F32)
    wanted = jnp.sum(
        jnp.where(inside & (rank == slot), local_rows.astype(F32), 0.0), axis=1, keepdims=True
    )
    pick = lax.broadcasted_iota(jnp.int32, (slots, owned), 1).astype(F32) == wanted
    pick = jnp.where(pick, 1.0, 0.0).astype(BF16)
    load.wait()
    parts = 2
    step = width // parts
    for c in range(parts):
        def fetch(b, carry):
            cols = pl.ds(pl.multiple_of(c * step + b * 512, 512), 512)
            out = jnp.dot(pick, table[:, cols], preferred_element_type=F32).astype(BF16)
            found[:, :, cols] = out.reshape(GROUP, SLOTS, 512)
            return carry

        lax.fori_loop(0, step // 512, fetch, 0)
        cols = pl.ds(c * step, step)
        for n, p in enumerate(peers):
            copy = remote(found.at[p, :, cols], recv.at[t, :, cols], xs.at[c, n], xr.at[c, n], {"tensor": p})
            copy.start()
            copies.append(copy)
        recv[t, :, cols] = found[t, :, cols]
    meanwhile()
    total = jnp.zeros((rows, 1), F32)
    for c in range(parts):
        cols = pl.ds(c * step, step)
        for n, p in enumerate(sources):
            ref = recv.at[p, :, cols]
            remote(ref, ref, xs.at[c, n], xr.at[c, n], {"tensor": p}).wait_recv()
        for b in range(step // 1024):
            cols = pl.ds(c * step + b * 1024, 1024)
            picked = jnp.dot(chosen, recv[:, :, cols].reshape(slots, 1024), preferred_element_type=F32)
            emb_ref[:, cols] = picked.astype(BF16)
            total += jnp.sum(picked * picked, axis=-1, keepdims=True)
    return copies, total


def document_starts(lengths_ref, positions):
    first = jnp.zeros_like(positions)
    start = jnp.int32(0)
    for d in range(lengths_ref.shape[0]):
        first = jnp.where(positions >= start, start, first)
        start = start + lengths_ref[d]
    return first


def attention(q_ref, first_ref, pair_ref, att_ref, win_ref, relay, m_ref, l_ref, acc_ref, ssem, rsem, z, early, late, done):
    t = lax.axis_index("tensor")
    r = lax.axis_index("dp")
    y, c = r // 2, lax.rem(r, 2)
    kind = lax.rem(t, 2)
    rows = q_ref.shape[0]
    group = rows // SIDE
    partner = {"tensor": t + 1 - 2 * kind}
    up = {"dp": lax.rem(y + 1, SIDE) * 2 + c}
    down = {"dp": lax.rem(y + SIDE - 1, SIDE) * 2 + c}
    other = {"dp": y * 2 + 1 - c}

    def copy(n, src, dst, peer):
        return remote(src, dst, ssem.at[n], rsem.at[n], peer)

    def step(w, i, count, causal):
        span = pl.ds(pl.multiple_of(i * group, UNIT), group)
        q = jnp.concatenate([q_ref[span, :HD], q_ref[span, HD:]], axis=0)
        scores = lax.dot_general(
            win_ref[w, 0, :count, :], q, (((1,), (1,)), ((), ())), preferred_element_type=F32
        )
        at = lax.broadcasted_iota(jnp.int32, (count, 1), 0) + w * rows
        allowed = at >= first_ref[i]
        if causal:
            query = lax.rem(lax.broadcasted_iota(jnp.int32, (1, 2 * group), 1), group)
            allowed &= at <= query + (4 * rows + i * group)
        scores = jnp.where(allowed, scores, NEGATIVE)
        top = jnp.max(scores, axis=0, keepdims=True) * EXP_SCALE
        if not causal:
            old = m_ref[i]
            top = jnp.maximum(old, top)
            decay = jnp.exp2(old - top)
        weights = jnp.exp2(scores * EXP_SCALE - top)
        total = jnp.sum(weights, axis=0, keepdims=True)
        added = lax.dot_general(
            win_ref[w, 1, :count, :], weights.astype(BF16), (((0,), (0,)), ((), ())),
            preferred_element_type=F32,
        )
        l_ref[i] = total if causal else l_ref[i] * decay + total
        acc_ref[i] = added if causal else acc_ref[i] * decay + added
        m_ref[i] = top

    def earlier(w, steps=range(SIDE)):
        @pl.when(r + w >= 4)
        def _():
            for i in steps:
                step(w, i, rows, False)

    swap = copy(0, pair_ref, win_ref.at[4, kind], partner)
    swap.start()
    win_ref[4, kind] = pair_ref[...]
    swap_in = copy(0, pair_ref, win_ref.at[4, 1 - kind], partner)
    up_key = copy(1, win_ref.at[4, 0], win_ref.at[2, 0], up)
    up_value = copy(2, win_ref.at[4, 1], win_ref.at[2, 1], up)
    far_key = copy(3, win_ref.at[2, 0], win_ref.at[0, 0], up)
    down_value = copy(4, win_ref.at[4, 1], relay, down)
    far_value = copy(5, relay, win_ref.at[0, 1], down)
    near = [copy(6 + k, win_ref.at[4, k], win_ref.at[3, k], other) for k in range(2)]
    cross0 = [copy(8 + k, win_ref.at[2, k], win_ref.at[1, k], other) for k in range(2)]
    cross1 = [copy(8 + k, win_ref.at[2, k], win_ref.at[3, k], other) for k in range(2)]
    far1 = [copy(10 + k, win_ref.at[0, k], win_ref.at[1, k], other) for k in range(2)]
    has_up, has_far = y < SIDE - 1, y < SIDE - 2
    got_up, got_far = y > 0, y > 1
    relays = (y == SIDE - 1) | (y == 0)
    swap_in.wait_recv()

    @pl.when(has_far)
    def _():
        down_value.start()

    @pl.when(has_up)
    def _():
        up_key.start()
        up_value.start()

    @pl.when(c == 0)
    def _():
        for k in range(2):
            near[k].start()

    early()
    for i in range(SIDE):
        step(4, i, (i + 1) * group, True)

    @pl.when(relays)
    def _():
        down_value.wait_recv()
        far_value.start()

    @pl.when(got_up)
    def _():
        up_key.wait_recv()

        @pl.when(has_up)
        def _():
            far_key.start()

        up_value.wait_recv()

        @pl.when(c == 0)
        def _():
            for k in range(2):
                cross0[k].start()

        @pl.when(c == 1)
        def _():
            for k in range(2):
                cross1[k].start()

    @pl.when(c == 1)
    def _():
        for k in range(2):
            near[k].wait_recv()

    earlier(2 + c)

    @pl.when(got_up & (c == 0))
    def _():
        for k in range(2):
            cross1[k].wait_recv()

    earlier(3 - c)
    late()

    @pl.when(got_far)
    def _():
        far_key.wait_recv()
        far_value.wait_recv()

        @pl.when(c == 1)
        def _():
            for k in range(2):
                far1[k].start()

    @pl.when(got_up & (c == 1))
    def _():
        for k in range(2):
            cross0[k].wait_recv()

    order = [wrap(z + dz) for dz in (2, 1, -1, 0)]
    earlier(c, order[:2])

    @pl.when(got_far & (c == 0))
    def _():
        for k in range(2):
            far1[k].wait_recv()

    for n, i in enumerate(order):
        if n > 1:
            earlier(c, [i])
        earlier(1 - c, [i])
        out = (acc_ref[i] / l_ref[i]).T.astype(BF16)
        for h in range(2):
            att_ref[i, :, :, h * HD:(h + 1) * HD] = flat_units(out[h * group:(h + 1) * group])
        done((2, 1, -1, 0)[n])

    @pl.when(c == 0)
    def _():
        for k in range(2):
            near[k].wait_send()

    @pl.when(got_up & (c == 0))
    def _():
        for k in range(2):
            cross0[k].wait_send()

    @pl.when(got_up & (c == 1))
    def _():
        for k in range(2):
            cross1[k].wait_send()

    @pl.when(got_far & (c == 1))
    def _():
        for k in range(2):
            far1[k].wait_send()

    @pl.when(has_far)
    def _():
        down_value.wait_send()

    @pl.when(has_up)
    def _():
        up_key.wait_send()
        up_value.wait_send()

    @pl.when(relays)
    def _():
        far_value.wait_send()

    @pl.when(got_up & has_up)
    def _():
        far_key.wait_send()

    swap.wait_send()


def layer_kernel(ids_ref, lengths_ref, inverse_ref, attn_gain_ref, mlp_gain_ref,
                 table_hbm, wq_hbm, wkv_hbm, wo_hbm, wg_hbm, wu_hbm, wd_hbm, out_ref,
                 table, wq, wkv, wo, wg, wu, wd, load_sem,
                 wanted_by, all_ids, found, recv, ks, kr, xs, xr,
                 emb, all_ref, q, pair, cos_ref, sin_ref, first_ref, gs, gr,
                 win, relay, m_ref, l_ref, acc_ref, att, as_, ar,
                 stream, hid, gs2, gr2,
                 part, att_z, att_x, mine, got, ss, sr, bs, br, bxs, bxr, ps, pr, ys, yr, cs, cr,
                 down_blocks, hid_z, hid_x, ss2, sr2, zs, zr, hs, hr, *down_sems):
    z, x = here()
    t = lax.axis_index("tensor")
    r = lax.axis_index("dp")
    y, c = r // 2, lax.rem(r, 2)
    loads = [
        pltpu.make_async_copy(src, dst, load_sem.at[n])
        for n, (src, dst) in enumerate((
            (table_hbm, table), (wq_hbm, wq), (wkv_hbm, wkv), (wo_hbm, wo), (wg_hbm, wg), (wu_hbm, wu), (wd_hbm, wd)
        ))
    ]
    for load in loads:
        load.start()
    peers = [lax.rem(t + n, GROUP) for n in range(1, GROUP)]
    sources = [lax.rem(t + GROUP - n, GROUP) for n in range(1, GROUP)]
    greet([{"tensor": p} for p in peers] + [
        {"dp": lax.rem(y + 1, SIDE) * 2 + c}, {"dp": lax.rem(y + SIDE - 1, SIDE) * 2 + c}, {"dp": y * 2 + 1 - c},
    ])
    rows, width = emb.shape
    span_rows = rows * GROUP
    spread = Spread(wo_hbm, part, ps, pr, ys, yr, cs, cr, z, x)
    spread.plane(True)
    down = SpreadDown(wd_hbm, down_blocks, down_sems, z, x)
    hidden_width = wg.shape[0]

    def positions():
        hid[:, :, :, hidden_width:] = jnp.zeros((*hid.shape[:3], hid.shape[3] - hidden_width), BF16)
        spread.plane(False)
        spread.plane_far(True)
        group = span_rows // SIDE
        for i in range(SIDE):
            lanes = lax.rem(lax.broadcasted_iota(jnp.int32, (1, 2 * group), 1), group) + (r * span_rows + i * group)
            first_ref[i] = document_starts(lengths_ref, lanes) - (r - 4) * span_rows
        sign = jnp.where(lax.broadcasted_iota(jnp.int32, (1, HD), 1) < HD // 2, -1.0, 1.0)

        def turn(b, carry):
            at = pl.ds(pl.multiple_of(b * 64, 64), 64)
            place_of = r * span_rows + b * 64 + lax.broadcasted_iota(jnp.int32, (64, HD), 0)
            angle = (place_of - document_starts(lengths_ref, place_of)).astype(F32) * inverse_ref[...]
            cos_ref[at, :] = jnp.cos(angle)
            sin_ref[at, :] = jnp.sin(angle) * sign
            return carry

        lax.fori_loop(0, span_rows // 64, turn, 0)

    copies, total = find_rows(
        ids_ref, all_ids, wanted_by, table, found, recv, emb, t, peers, sources, loads[0], ks, kr, xs, xr, positions
    )
    scale = lax.rsqrt(total / width + EPSILON)
    for b in range(width // 1024):
        cols = pl.ds(b * 1024, 1024)
        all_ref[t, :, cols] = (emb[:, cols].astype(F32) * scale * attn_gain_ref[:, cols]).astype(BF16)
    loads[1].wait()
    loads[2].wait()
    keys_here = lax.rem(t, 2) == 0
    spread.plane_far(False)
    spread.ring(True)
    spread.cores(True, (0,))

    def project(dz):
        if dz == 1:
            spread.ring(False)
            spread.ring_far(True)
            spread.cores(True, (1, 3))
        lhs, span = row_group(all_ref, z, dz)
        cos, sin = cos_ref[span, :], sin_ref[span, :]
        queries = jnp.dot(lhs, wq[...], preferred_element_type=F32)
        for h in range(queries.shape[1] // HD):
            head = queries[:, h * HD:(h + 1) * HD]
            q[span, h * HD:(h + 1) * HD] = (head * cos + pltpu.roll(head, HD // 2, 1) * sin).astype(BF16)
        both = jnp.dot(lhs, wkv[...], preferred_element_type=F32)
        turned = both * cos + pltpu.roll(both, HD // 2, 1) * sin
        pair[span, :] = jnp.where(keys_here, turned, both).astype(BF16)

    ring_gather(all_ref, gs, gr, z, x, project)
    spread.ring_far(False)
    spread.cores(True, (2,))

    moves_of = Moves(att, att_z, att_x, bs, br, bxs, bxr, z, x)

    def late():
        down.plane(False)
        down.plane_far(True)

    attention(
        q, first_ref, pair, att, win, relay, m_ref, l_ref, acc_ref, as_, ar, z,
        functools.partial(down.plane, True), late, moves_of.finished
    )
    spread.cores(False, (0, 1, 3))
    down.plane_far(False)
    down.ring(True)
    down.cores(True, (0,))

    def mixed(cols, value):
        stream[:, cols] = (emb[:, cols].astype(F32) + value).astype(BF16)

    loads[3].wait()
    spread.cores(False, (2,))
    mix(moves_of, att, att_z, att_x, wo, part, mine, got, ss, sr, z, x, mixed)
    spread.drain()
    all_ref[t] = normalize(stream[...].astype(F32), mlp_gain_ref[...])
    loads[4].wait()
    loads[5].wait()

    loads[6].wait()
    hidden = Moves(hid, hid_z, hid_x, zs, zr, hs, hr, z, x)

    def gate(dz):
        if dz == 0:
            down.ring(False)
            down.ring_far(True)
            down.cores(True, (1, 3))
        lhs, span = row_group(all_ref, z, dz)
        across = (((1,), (1,)), ((), ()))
        gated = lax.dot_general(lhs, wg[...], across, preferred_element_type=F32)
        upper = lax.dot_general(lhs, wu[...], across, preferred_element_type=F32)
        value = (gated / (1.0 + jnp.exp(-gated)) * upper).astype(BF16)
        hid[wrap(z + dz), :, :, :hidden_width] = value.reshape(SIDE * UNITS, UNIT, hidden_width)
        hidden.finished(dz)

    ring_gather(all_ref, gs2, gr2, z, x, gate)
    down.ring_far(False)
    down.cores(True, (2,))

    def arrive(h):
        hidden.arrive(h)
        if h == 0:
            down.cores(False, (0, 1, 3, 2))

    def multiply(h, cols):
        def left(block):
            return block.reshape(-1, hidden_width)

        own = hid[z, :, :, :hidden_width] if h == 0 else hid[:, pl.ds(x * UNITS, UNITS), :, :hidden_width]
        out = jnp.dot(left(own), flat(wd[:, :, cols]), preferred_element_type=F32)
        for n in range(SIDE - 1):
            block = hid_z[n, :, :, :hidden_width] if h == 0 else hid_x[n, :, :, :, :hidden_width]
            out = out + jnp.dot(left(block), flat(down_blocks[n, :, :, cols]), preferred_element_type=F32)
        return out

    def added(cols, value):
        out_ref[:, cols] = (stream[:, cols].astype(F32) + value).astype(BF16)

    short_reduce(mine, got, ss2, sr2, z, x, arrive, multiply, added)
    hidden.drain()
    down.drain()
    for copy in copies:
        copy.wait_send()


def layer(ids, lengths, inverse, attn_gain, mlp_gain, table, wq, wkv, wo, wg, wu, wd):
    rows, width = ids.shape[1], table.shape[1]
    span = rows * GROUP
    group = span // SIDE
    quarter = width // 4
    unit = (UNITS, UNIT)
    padded = -(-wg.shape[0] // 128) * 128
    whole = pl.BlockSpec(memory_space=VMEM)
    outside = pl.BlockSpec(memory_space=pl.ANY)
    peers = DMA((GROUP - 1,))
    return pl.pallas_call(
        layer_kernel,
        out_shape=jax.ShapeDtypeStruct((rows, width), BF16),
        in_specs=[whole, pl.BlockSpec(memory_space=pltpu.SMEM)] + [whole] * 3 + [outside] * 7,
        out_specs=whole,
        scratch_shapes=[
            *[VMEM(w.shape, BF16) for w in (table, wq, wkv, wo, wg, wu, wd)], DMA((7,)),
            VMEM((8, 128), jnp.int32), VMEM((GROUP, 8, 128), jnp.int32),
            VMEM((GROUP, SLOTS, width), BF16), VMEM((GROUP, SLOTS, width), BF16),
            peers, peers, DMA((2, GROUP - 1)), DMA((2, GROUP - 1)),
            VMEM((rows, width), BF16), VMEM((GROUP, rows, width), BF16),
            VMEM((span, wq.shape[1]), BF16), VMEM((span, HD), BF16),
            VMEM((span, HD), F32), VMEM((span, HD), F32), VMEM((SIDE, 1, 2 * group), jnp.int32), *GATHER_SEMS,
            VMEM((5, 2, span, HD), BF16), VMEM((span, HD), BF16),
            VMEM((SIDE, 1, 2 * group), F32), VMEM((SIDE, 1, 2 * group), F32), VMEM((SIDE, HD, 2 * group), F32),
            VMEM((SIDE, SIDE * UNITS, UNIT, 2 * HD), BF16), DMA((12,)), DMA((12,)),
            VMEM((rows, width), BF16), VMEM((SIDE, SIDE * UNITS, UNIT, padded), BF16), *GATHER_SEMS,
            VMEM((SIDE, SIDE * UNITS, UNIT, width), BF16),
            VMEM((SIDE - 1, SIDE * UNITS, UNIT, 2 * HD), BF16), VMEM((SIDE - 1, SIDE, *unit, 2 * HD), BF16),
            VMEM((2, SIDE * UNITS, UNIT, 2 * quarter), BF16), VMEM((2, 6, *unit, quarter), BF16),
            DMA((2, 6)), DMA((2, 6)),
            DMA((SIDE - 1,)), DMA((SIDE - 1,)), DMA((SIDE, SIDE - 1)), DMA((SIDE, SIDE - 1)),
            DMA((8,)), DMA((8,)), DMA((18,)), DMA((18,)), DMA((24,)), DMA((24,)),
            VMEM((SIDE - 1, *wd.shape), BF16),
            VMEM((SIDE - 1, SIDE * UNITS, UNIT, padded), BF16), VMEM((SIDE - 1, SIDE, *unit, padded), BF16),
            DMA((2, 6)), DMA((2, 6)), DMA((SIDE - 1,)), DMA((SIDE - 1,)), DMA((SIDE, SIDE - 1)), DMA((SIDE, SIDE - 1)),
            DMA((4,)), DMA((4,)), DMA((12,)), DMA((12,)), DMA((12,)), DMA((12,)),
        ],
        compiler_params=pltpu.CompilerParams(
            collective_id=0, has_side_effects=True, vmem_limit_bytes=63 * 2**20
        ),
        name="layer",
    )(ids, lengths, inverse, attn_gain, mlp_gain, table, wq, wkv, wo, wg, wu, wd)


def local(ids, doc_lengths, table, attn_gain, wq, wkv, wo, mlp_gain, w_gate, w_up, w_down):
    inverse = np.float32(ROPE_BASE) ** (-np.arange(HD // 2, dtype=np.float32) * np.float32(2.0 / HD))
    inverse = jnp.asarray(np.concatenate([inverse, inverse])[None, :], F32)
    return layer(
        ids[None, :], doc_lengths, inverse, attn_gain[None, :], mlp_gain[None, :],
        table, wq, wkv, wo.reshape(-1, UNIT, wo.shape[1]), w_gate.T, w_up.T, w_down.reshape(-1, UNIT, wo.shape[1]),
    )


def solution(mesh):
    placed = (
        P(("dp", "tensor")),
        P(),
        P("tensor", None),
        P(),
        P(None, "tensor"),
        P(None, "tensor"),
        P("tensor", None),
        P(),
        P(None, "tensor"),
        P(None, "tensor"),
        P("tensor", None),
    )
    return jax.shard_map(
        local, mesh=mesh, in_specs=placed, out_specs=P(("dp", "tensor"), None), check_vma=False
    )
```

```python
import functools

import jax
import jax.numpy as jnp
import numpy as np
from jax import lax
from jax.experimental import pallas as pl
from jax.experimental.pallas import tpu as pltpu
from jax.sharding import PartitionSpec as P

HD = 128
SIDE = 4
GROUP = SIDE * SIDE
SLOTS = 8
UNIT = 16
UNITS = 3

EPSILON = 1e-05
ROPE_BASE = 500000.0
NEGATIVE = -1e30
EXP_SCALE = HD ** (-0.5) * 1.4426950408889634
MESH = pl.DeviceIdType.MESH
VMEM = pltpu.VMEM
DMA = pltpu.SemaphoreType.DMA
BF16 = jnp.bfloat16
F32 = jnp.float32


def wrap(v):
    return lax.rem(v + 2 * SIDE, SIDE)


def place(z, x):
    return wrap(z) * SIDE + wrap(x)


def here():
    t = lax.axis_index("tensor")
    return t // SIDE, lax.rem(t, SIDE)


def greet(peers):
    barrier = pltpu.get_barrier_semaphore()
    for peer in peers:
        pl.semaphore_signal(barrier, inc=1, device_id=peer, device_id_type=MESH)
    pl.semaphore_wait(barrier, len(peers))


def remote(src, dst, send_sem, recv_sem, peer):
    return pltpu.make_async_remote_copy(
        src_ref=src, dst_ref=dst, send_sem=send_sem, recv_sem=recv_sem,
        device_id=peer, device_id_type=MESH,
    )


def ring_gather(buf, ssem, rsem, z, x, ready, begun=lambda: None):
    half = buf.shape[-1] // 2
    quarter = half // 2
    started = []

    def block(h, first, second):
        return place(z + second, x + first) if h == 0 else place(z + first, x + second)

    def view(h, first, second, part):
        start, size = (h * half, half) if part == 0 else (h * half + (part - 1) * quarter, quarter)
        return buf.at[block(h, first, second), :, pl.ds(start, size)]

    def send(h, n, first, second, part, axis, d):
        ref = view(h, first, second, part)
        peer = {"tensor": block(h, d, 0) if axis == 0 else block(h, 0, d)}
        copy = remote(ref, ref, ssem.at[h, n], rsem.at[h, n], peer)
        copy.start()
        started.append(copy)

    def recv(h, n, first, second, part):
        ref = view(h, first, second, part)
        remote(ref, ref, ssem.at[h, n], rsem.at[h, n], {"tensor": block(h, 1, 0)}).wait_recv()

    offsets = (0, -1, 1, 2)
    for h in range(2):
        send(h, 0, 0, 0, 0, 0, 1)
        send(h, 1, 0, 0, 0, 0, -1)
    for h in range(2):
        send(h, 4, 0, 0, 0, 1, 1)
        send(h, 5, 0, 0, 0, 1, -1)
    begun()
    for h in range(2):
        recv(h, 0, -1, 0, 0)
        send(h, 2, -1, 0, 1, 0, 1)
        recv(h, 1, 1, 0, 0)
        send(h, 3, 1, 0, 2, 0, -1)
        for n in (1, 2):
            send(h, 4 + 2 * n, offsets[n], 0, 0, 1, 1)
            send(h, 5 + 2 * n, offsets[n], 0, 0, 1, -1)

    def relay(n):
        k = offsets[n]
        for h in range(2):
            recv(h, 4 + 2 * n, k, -1, 0)
            send(h, 12 + 2 * n, k, -1, 1, 1, 1)
            recv(h, 5 + 2 * n, k, 1, 0)
            send(h, 13 + 2 * n, k, 1, 2, 1, -1)

    relay(0)
    for h in range(2):
        recv(h, 2, 2, 0, 1)
        recv(h, 3, 2, 0, 2)
        send(h, 10, 2, 0, 0, 1, 1)
        send(h, 11, 2, 0, 0, 1, -1)
    relay(1)
    relay(2)

    def far(h, n):
        recv(h, 12 + 2 * n, offsets[n], 2, 1)
        recv(h, 13 + 2 * n, offsets[n], 2, 2)

    far(1, 0)
    ready(0)
    relay(3)
    far(1, 1)
    ready(-1)
    far(1, 2)
    ready(1)
    for n in range(4):
        far(0, n)
    far(1, 3)
    ready(2)
    for copy in started:
        copy.wait_send()


GATHER_SEMS = [DMA((2, 20)), DMA((2, 20))]


def flat(block):
    return block.reshape(-1, block.shape[-1])


def flat_units(block):
    return block.reshape(-1, UNIT, block.shape[-1])


class Moves:
    def __init__(self, rows, to_z, to_x, zs, zr, xs, xr, z, x):
        self.refs = rows, to_z, to_x, zs, zr, xs, xr
        self.z, self.x = z, x
        self.started = []

    def along_z(self, dz):
        rows, to_z, to_x, zs, zr, xs, xr = self.refs
        o = dz % SIDE
        peer = {"tensor": place(self.z + o, self.x)}
        return remote(rows.at[wrap(self.z + dz)], to_z.at[SIDE - o - 1], zs.at[o - 1], zr.at[o - 1], peer)

    def along_x(self, dz, o):
        rows, to_z, to_x, zs, zr, xs, xr = self.refs
        zz = wrap(self.z + dz)
        src = rows.at[zz, pl.ds(wrap(self.x + o) * UNITS, UNITS)]
        sems = xs.at[dz % SIDE, o - 1], xr.at[dz % SIDE, o - 1]
        return remote(src, to_x.at[SIDE - o - 1, zz], *sems, {"tensor": place(self.z, self.x + o)})

    def finished(self, dz):
        moves = [self.along_z(dz)] if dz else []
        moves += [self.along_x(dz, o) for o in (2, 1, 3)]
        for move in moves:
            move.start()
        self.started += moves

    def arrive(self, h):
        if h == 0:
            for dz in (-1, 1, 2):
                self.along_z(dz).wait_recv()
        else:
            for dz in (2, 1, -1, 0):
                for o in (1, 3, 2):
                    self.along_x(dz, o).wait_recv()

    def drain(self):
        for move in self.started:
            move.wait_send()


class Spread:
    def __init__(self, wo_hbm, part, ssem, rsem, ysem, yrem, csem, crem, z, x):
        r = lax.axis_index("dp")
        self.y, self.c = r // 2, lax.rem(r, 2)
        self.wo, self.part, self.z, self.x = wo_hbm, part, z, x
        self.sems = (ssem, rsem), (ysem, yrem), (csem, crem)
        self.half = part.shape[-1] // 2
        self.started = []
        self.slices = [(o, h) for h in range(2) for o in (1, 2, 3)]

    def share(self, dy, other=False):
        c = 1 - self.c if other else self.c
        return lax.rem(self.y + dy + SIDE, SIDE) * 2 + c

    def columns(self, h, q):
        quarter = self.half // 2
        return pl.ds(h * self.half, self.half) if q is None else pl.ds(h * self.half + q * quarter, quarter)

    def view(self, o, share, h, q=None):
        unit = 16 * (o - 1) + 2 * share
        a = unit // 12
        return self.part.at[a, pl.ds(unit - a * 12, 2), :, self.columns(h, q)]

    def copy(self, phase, index, src, dst, peer, start):
        send, recv = self.sems[phase]
        copy = remote(src, dst, send.at[index], recv.at[index], peer)
        if start:
            copy.start()
            self.started.append(copy)
        else:
            copy.wait_recv()

    def along(self, h, d):
        return {"tensor": place(self.z + d, self.x) if h == 0 else place(self.z, self.x + d)}

    def plane(self, start):
        own = self.share(0)
        for h in range(2):
            mine = self.wo.at[pl.ds(2 * own, 2), :, self.columns(h, None)]
            for n, (o, d) in enumerate(((3, 1), (1, -1))):
                dst = self.view(o, own, h)
                self.copy(0, h * 4 + n, mine if start else dst, dst, self.along(h, d), start)

    def plane_far(self, start):
        own = self.share(0)
        for h in range(2):
            for n, (o, d) in enumerate(((3, 1), (1, -1))):
                dst = self.view(2, own, h, n)
                self.copy(0, h * 4 + 2 + n, self.view(o, own, h, n) if start else dst, dst, self.along(h, d), start)

    def around(self, d):
        return {"dp": lax.rem(self.y + d + SIDE, SIDE) * 2 + self.c}

    def ring(self, start):
        for n, (o, h) in enumerate(self.slices):
            for k, d in enumerate((1, -1)):
                ref = self.view(o, self.share(0 if start else -d), h)
                self.copy(1, k * 9 + n, ref, ref, self.around(d), start)

    def ring_far(self, start):
        for n in range(3):
            for k, d in enumerate((1, -1)):
                o, h = self.slices[3 * k + n]
                ref = self.view(o, self.share(-d if start else -2 * d), h)
                self.copy(1, k * 9 + 6 + n, ref, ref, self.around(d), start)

    def cores(self, start, steps):
        peer = {"dp": self.y * 2 + 1 - self.c}
        for dy in steps:
            for n, (o, h) in enumerate(self.slices):
                ref = self.view(o, self.share(dy, not start), h)
                self.copy(2, dy * 6 + n, ref, ref, peer, start)

    def drain(self):
        for copy in self.started:
            copy.wait_send()


class SpreadDown:
    def __init__(self, w_hbm, blocks, sems, z, x):
        r = lax.axis_index("dp")
        self.y, self.c = r // 2, lax.rem(r, 2)
        self.w, self.blocks, self.sems, self.z, self.x = w_hbm, blocks, sems, z, x
        self.units = blocks.shape[1] // SIDE
        self.half = blocks.shape[-1] // 2
        self.started = []

    def columns(self, c, q=None):
        size = self.half if q is None else self.half // 2
        start = c * self.half + (0 if q is None else q * size)
        return pl.ds(pl.multiple_of(start, size), size)

    def rows(self, dy):
        return pl.ds(lax.rem(self.y + dy + SIDE, SIDE) * self.units, self.units)

    def view(self, o, dy, c, q=None):
        return self.blocks.at[o - 1, self.rows(dy), :, self.columns(c, q)]

    def copy(self, phase, index, src, dst, peer, start):
        send, recv = self.sems[2 * phase:2 * phase + 2]
        copy = remote(src, dst, send.at[index], recv.at[index], peer)
        if start:
            copy.start()
            self.started.append(copy)
        else:
            copy.wait_recv()

    def along(self, d):
        return {"tensor": place(self.z + d * (1 - self.c), self.x + d * self.c)}

    def plane(self, start):
        for n, (o, d) in enumerate(((3, 1), (1, -1))):
            dst = self.view(o, 0, self.c)
            src = self.w.at[self.rows(0), :, self.columns(self.c)] if start else dst
            self.copy(0, n, src, dst, self.along(d), start)

    def plane_far(self, start):
        for n, (o, d) in enumerate(((3, 1), (1, -1))):
            dst = self.view(2, 0, self.c, n)
            self.copy(0, 2 + n, self.view(o, 0, self.c, n) if start else dst, dst, self.along(d), start)

    def around(self, d):
        return {"dp": lax.rem(self.y + d + SIDE, SIDE) * 2 + self.c}

    def ring(self, start):
        for o in (1, 2, 3):
            for k, d in enumerate((1, -1)):
                ref = self.view(o, 0 if start else -d, self.c)
                self.copy(1, k * 6 + o - 1, ref, ref, self.around(d), start)

    def ring_far(self, start):
        for o in (1, 2, 3):
            for k, d in enumerate((1, -1)):
                ref = self.view(o, -d if start else -2 * d, self.c, k)
                self.copy(1, k * 6 + 2 + o, ref, ref, self.around(d), start)

    def cores(self, start, steps):
        peer = {"dp": self.y * 2 + 1 - self.c}
        for dy in steps:
            for o in (1, 2, 3):
                ref = self.view(o, dy, self.c if start else 1 - self.c)
                self.copy(2, dy * 3 + o - 1, ref, ref, peer, start)

    def drain(self):
        for copy in self.started:
            copy.wait_send()


def short_reduce(mine, got, ssem, rsem, z, x, arrive, multiply, finish):
    half = mine.shape[-1]
    quarter = half // 2
    started = []

    def block(h, j, q):
        n = wrap(x + j) if h == 0 else wrap(z + j)
        return mine.at[h, pl.ds(n * UNITS, UNITS), :, pl.ds(q * quarter, quarter)]

    def send(h, slot, src, d):
        peer = {"tensor": place(z, x + d) if h == 0 else place(z + d, x)}
        copy = remote(src, got.at[h, slot], ssem.at[h, slot], rsem.at[h, slot], peer)
        copy.start()
        started.append(copy)

    def recv(h, slot):
        ref = got.at[h, slot]
        remote(ref, ref, ssem.at[h, slot], rsem.at[h, slot], {"tensor": place(z, x + 1)}).wait_recv()

    def load(ref):
        return ref[...].astype(F32)

    step = min(512, quarter)

    def make(h, q):
        def column(c, carry):
            at = pl.multiple_of(q * quarter + c * step, step)
            out = multiply(h, pl.ds(h * half + at, step)).astype(BF16)
            mine[h, :, :, pl.ds(at, step)] = out.reshape(SIDE * UNITS, UNIT, step)
            return carry

        lax.fori_loop(0, quarter // step, column, 0)

    for q in range(2):
        for h in range(2):
            if q == 0:
                arrive(h)
            make(h, q)
            d = 1 - 2 * q
            send(h, 3 * q, block(h, 2, q), d)
            send(h, (4, 1)[q], block(h, -d, q), -d)
    for h in range(2):
        for slot, q, d in ((0, 0, 1), (3, 1, -1)):
            recv(h, slot)
            got[h, slot] = (load(got.at[h, slot]) + load(block(h, d, q))).astype(BF16)
            send(h, slot + 2, got.at[h, slot], d)
    for h in range(2):
        for slot in (1, 4, 2, 5):
            recv(h, slot)
        for q in range(2):
            a, b = ((2, 4), (1, 5))[q]
            value = load(block(h, 0, q)) + load(got.at[h, a]) + load(got.at[h, b])
            finish(pl.ds(h * half + q * quarter, quarter), flat(value))
    for copy in started:
        copy.wait_send()


def mix(moves, att, att_z, att_x, wo, part, mine, got, ssem, rsem, z, x, finish):
    def multiply(h, cols):
        own = flat(att[z] if h == 0 else att[:, pl.ds(x * UNITS, UNITS)])
        others = jnp.concatenate([flat((att_z, att_x)[h][n]) for n in range(SIDE - 1)], axis=1)
        out = jnp.dot(own, flat(wo[:, :, cols]), preferred_element_type=F32)
        weights = part[:, :, :, cols].reshape(others.shape[1], out.shape[1])
        return out + jnp.dot(others, weights, preferred_element_type=F32)

    short_reduce(mine, got, ssem, rsem, z, x, moves.arrive, multiply, finish)
    moves.drain()


def normalize(rows, gain):
    scale = lax.rsqrt(jnp.mean(rows * rows, axis=-1, keepdims=True) + EPSILON)
    return (rows * scale * gain).astype(BF16)


def row_group(all_ref, z, dz):
    rows, width = all_ref.shape[1:]
    zz = wrap(z + dz)
    lhs = all_ref[pl.ds(zz * SIDE, SIDE)].reshape(SIDE * rows, width)
    return lhs, pl.ds(pl.multiple_of(zz * SIDE * rows, 16), SIDE * rows)


def find_rows(ids_ref, all_ids, wanted_by, table, found, recv, emb_ref, t, peers, sources, load, ks, kr, xs, xr, asked, meanwhile):
    copies = []
    rows, width = emb_ref.shape
    wanted_by[...] = jnp.full_like(wanted_by, -1)
    wanted_by[:, :rows] = jnp.broadcast_to(ids_ref[...], (8, rows))
    for n, p in enumerate(peers):
        copy = remote(wanted_by, all_ids.at[t], ks.at[n], kr.at[n], {"tensor": p})
        copy.start()
        copies.append(copy)
    all_ids[t] = wanted_by[...]
    slots = GROUP * SLOTS
    owned = table.shape[0]
    square = (128, 128)
    row, lane = lax.broadcasted_iota(jnp.int32, square, 0), lax.broadcasted_iota(jnp.int32, square, 1)
    own = jnp.broadcast_to(wanted_by[:1, :], square)
    owner = jnp.right_shift(own, owned.bit_length() - 1).astype(F32)
    same = (owner == owner.T) & (row < lane)
    source = owner * SLOTS + jnp.sum(jnp.where(same, 1.0, 0.0), axis=0, keepdims=True)
    chosen = jnp.where((source == row.astype(F32)) & (own >= 0), 1.0, 0.0).T[:rows].astype(BF16)
    before = jnp.where(row < lane, 1.0, 0.0).astype(BF16)
    for n, p in enumerate(sources):
        remote(wanted_by, all_ids.at[p], ks.at[n], kr.at[n], {"tensor": p}).wait_recv()
    asked()
    local_rows = all_ids[...].reshape(slots, 128) - t * owned
    inside = (local_rows >= 0) & (local_rows < owned)
    rank = jnp.dot(jnp.where(inside, 1.0, 0.0).astype(BF16), before, preferred_element_type=F32)
    slot = lax.rem(row, SLOTS).astype(F32)
    wanted = jnp.sum(
        jnp.where(inside & (rank == slot), local_rows.astype(F32), 0.0), axis=1, keepdims=True
    )
    pick = lax.broadcasted_iota(jnp.int32, (slots, owned), 1).astype(F32) == wanted
    pick = jnp.where(pick, 1.0, 0.0).astype(BF16)
    load.wait()
    parts = 2
    step = width // parts
    for c in range(parts):
        def fetch(b, carry):
            cols = pl.ds(pl.multiple_of(c * step + b * 512, 512), 512)
            out = jnp.dot(pick, table[:, cols], preferred_element_type=F32).astype(BF16)
            found[:, :, cols] = out.reshape(GROUP, SLOTS, 512)
            return carry

        lax.fori_loop(0, step // 512, fetch, 0)
        cols = pl.ds(c * step, step)
        for n, p in enumerate(peers):
            copy = remote(found.at[p, :, cols], recv.at[t, :, cols], xs.at[c, n], xr.at[c, n], {"tensor": p})
            copy.start()
            copies.append(copy)
        recv[t, :, cols] = found[t, :, cols]
    meanwhile()
    total = jnp.zeros((rows, 1), F32)
    for c in range(parts):
        cols = pl.ds(c * step, step)
        for n, p in enumerate(sources):
            ref = recv.at[p, :, cols]
            remote(ref, ref, xs.at[c, n], xr.at[c, n], {"tensor": p}).wait_recv()
        for b in range(step // 1024):
            cols = pl.ds(c * step + b * 1024, 1024)
            picked = jnp.dot(chosen, recv[:, :, cols].reshape(slots, 1024), preferred_element_type=F32)
            emb_ref[:, cols] = picked.astype(BF16)
            total += jnp.sum(picked * picked, axis=-1, keepdims=True)
    return copies, total


def document_starts(lengths_ref, positions):
    first = jnp.zeros_like(positions)
    start = jnp.int32(0)
    for d in range(lengths_ref.shape[0]):
        first = jnp.where(positions >= start, start, first)
        start = start + lengths_ref[d]
    return first


def attention(q_ref, first_ref, pair_ref, att_ref, win_ref, relay, m_ref, l_ref, acc_ref, ssem, rsem, z, early, late, done):
    t = lax.axis_index("tensor")
    r = lax.axis_index("dp")
    y, c = r // 2, lax.rem(r, 2)
    kind = lax.rem(t, 2)
    rows = q_ref.shape[0]
    group = rows // SIDE
    partner = {"tensor": t + 1 - 2 * kind}
    up = {"dp": lax.rem(y + 1, SIDE) * 2 + c}
    down = {"dp": lax.rem(y + SIDE - 1, SIDE) * 2 + c}
    other = {"dp": y * 2 + 1 - c}

    def copy(n, src, dst, peer):
        return remote(src, dst, ssem.at[n], rsem.at[n], peer)

    def step(w, i, count, causal):
        span = pl.ds(pl.multiple_of(i * group, UNIT), group)
        q = jnp.concatenate([q_ref[span, :HD], q_ref[span, HD:]], axis=0)
        scores = lax.dot_general(
            win_ref[w, 0, :count, :], q, (((1,), (1,)), ((), ())), preferred_element_type=F32
        )
        at = lax.broadcasted_iota(jnp.int32, (count, 1), 0) + w * rows
        allowed = at >= first_ref[i]
        if causal:
            query = lax.rem(lax.broadcasted_iota(jnp.int32, (1, 2 * group), 1), group)
            allowed &= at <= query + (4 * rows + i * group)
        scores = jnp.where(allowed, scores, NEGATIVE)
        top = jnp.max(scores, axis=0, keepdims=True) * EXP_SCALE
        if not causal:
            old = m_ref[i]
            top = jnp.maximum(old, top)
            decay = jnp.exp2(old - top)
        weights = jnp.exp2(scores * EXP_SCALE - top)
        total = jnp.sum(weights, axis=0, keepdims=True)
        added = lax.dot_general(
            win_ref[w, 1, :count, :], weights.astype(BF16), (((0,), (0,)), ((), ())),
            preferred_element_type=F32,
        )
        l_ref[i] = total if causal else l_ref[i] * decay + total
        acc_ref[i] = added if causal else acc_ref[i] * decay + added
        m_ref[i] = top

    def earlier(w, steps=range(SIDE)):
        @pl.when(r + w >= 4)
        def _():
            for i in steps:
                step(w, i, rows, False)

    piece = rows // 2

    def block(w, k, p):
        return win_ref.at[w, k, pl.ds(p * piece, piece)]

    def pieces(n, src, dst, peer):
        return [copy(2 * n + p, src(p), dst(p), peer) for p in range(2)]

    def within(n, source, target, k, peer):
        return pieces(n, lambda p: block(source, k, p), lambda p: block(target, k, p), peer)

    def mine(p):
        return pair_ref.at[pl.ds(p * piece, piece)]

    def held(p):
        return relay.at[pl.ds(p * piece, piece)]

    def when(condition, *acts):
        @pl.when(condition)
        def _():
            for act in acts:
                act()

    def starts(copies):
        return [one.start for one in copies]

    def recvs(copies):
        return [one.wait_recv for one in copies]

    def sends(copies):
        return [one.wait_send for one in copies]

    lacking = 1 - kind
    swap = pieces(0, mine, lambda p: block(4, kind, p), partner)
    swap_in = pieces(0, mine, lambda p: block(4, lacking, p), partner)
    up_own = pieces(1, mine, lambda p: block(2, kind, p), up)
    up_other = within(2, 4, 2, lacking, up)
    down_own = pieces(3, mine, held, down)
    far_own = pieces(4, held, lambda p: block(0, kind, p), down)
    far_other = within(5, 2, 0, lacking, up)
    near_own = pieces(6, mine, lambda p: block(3, kind, p), other)
    near_other = within(7, 4, 3, lacking, other)
    cross0_own, cross0_other = within(8, 2, 1, kind, other), within(9, 2, 1, lacking, other)
    cross1_own, cross1_other = within(8, 2, 3, kind, other), within(9, 2, 3, lacking, other)
    far1 = within(10, 0, 1, kind, other) + within(11, 0, 1, lacking, other)
    has_up, has_far = y < SIDE - 1, y < SIDE - 2
    got_up, got_far = y > 0, y > 1
    relays = (y == SIDE - 1) | (y == 0)
    for p in range(2):
        swap[p].start()
    when(has_up, *starts(up_own))
    when(has_far, *starts(down_own))
    when(c == 0, *starts(near_own))
    win_ref[4, kind] = pair_ref[...]
    for p in range(2):
        swap_in[p].wait_recv()
        when(has_up, up_other[p].start)
        when(c == 0, near_other[p].start)
        when(relays, down_own[p].wait_recv, far_own[p].start)
    early()
    for i in range(SIDE):
        step(4, i, (i + 1) * group, True)

    when(got_up, *recvs(up_own))
    when(got_up & (c == 0), *starts(cross0_own))
    when(got_up & (c == 1), *starts(cross1_own))
    for p in range(2):
        when(got_up, up_other[p].wait_recv)
        when(got_up & has_up, far_other[p].start)
        when(got_up & (c == 0), cross0_other[p].start)
        when(got_up & (c == 1), cross1_other[p].start)
    when(c == 1, *recvs(near_own + near_other))
    earlier(2 + c)

    when(got_up & (c == 0), *recvs(cross1_own + cross1_other))
    earlier(3 - c)
    late()

    when(got_far, *recvs(far_own + far_other))
    when(got_far & (c == 1), *starts(far1))
    when(got_up & (c == 1), *recvs(cross0_own + cross0_other))
    order = [wrap(z + dz) for dz in (2, 1, -1, 0)]
    earlier(c, order[:2])

    when(got_far & (c == 0), *recvs(far1))
    for n, i in enumerate(order):
        if n > 1:
            earlier(c, [i])
        earlier(1 - c, [i])
        out = (acc_ref[i] / l_ref[i]).T.astype(BF16)
        for h in range(2):
            att_ref[i, :, :, h * HD:(h + 1) * HD] = flat_units(out[h * group:(h + 1) * group])
        done((2, 1, -1, 0)[n])

    when(c == 0, *sends(near_own + near_other))
    when(got_up & (c == 0), *sends(cross0_own + cross0_other))
    when(got_up & (c == 1), *sends(cross1_own + cross1_other))
    when(got_far & (c == 1), *sends(far1))
    when(has_far, *sends(down_own))
    when(has_up, *sends(up_own + up_other))
    when(relays, *sends(far_own))
    when(got_up & has_up, *sends(far_other))
    for one in swap:
        one.wait_send()


def layer_kernel(ids_ref, lengths_ref, inverse_ref, attn_gain_ref, mlp_gain_ref,
                 table_hbm, wq_hbm, wkv_hbm, wo_hbm, wg_hbm, wu_hbm, wd_hbm, out_ref,
                 table, wq, wkv, wo, wg, wu, wd, load_sem,
                 wanted_by, all_ids, found, recv, ks, kr, xs, xr,
                 emb, all_ref, q, pair, cos_ref, sin_ref, first_ref, gs, gr,
                 win, relay, m_ref, l_ref, acc_ref, att, as_, ar,
                 stream, hid, gs2, gr2,
                 part, att_z, att_x, mine, got, ss, sr, bs, br, bxs, bxr, ps, pr, ys, yr, cs, cr,
                 down_blocks, hid_z, hid_x, ss2, sr2, zs, zr, hs, hr, *down_sems):
    z, x = here()
    t = lax.axis_index("tensor")
    r = lax.axis_index("dp")
    y, c = r // 2, lax.rem(r, 2)
    loads = [
        pltpu.make_async_copy(src, dst, load_sem.at[n])
        for n, (src, dst) in enumerate((
            (table_hbm, table), (wq_hbm, wq), (wkv_hbm, wkv), (wo_hbm, wo), (wg_hbm, wg), (wu_hbm, wu), (wd_hbm, wd)
        ))
    ]
    for load in loads:
        load.start()
    peers = [lax.rem(t + n, GROUP) for n in range(1, GROUP)]
    sources = [lax.rem(t + GROUP - n, GROUP) for n in range(1, GROUP)]
    greet([{"tensor": p} for p in peers] + [
        {"dp": lax.rem(y + 1, SIDE) * 2 + c}, {"dp": lax.rem(y + SIDE - 1, SIDE) * 2 + c}, {"dp": y * 2 + 1 - c},
    ])
    rows, width = emb.shape
    span_rows = rows * GROUP
    spread = Spread(wo_hbm, part, ps, pr, ys, yr, cs, cr, z, x)
    down = SpreadDown(wd_hbm, down_blocks, down_sems, z, x)
    hidden_width = wg.shape[0]

    def positions():
        hid[:, :, :, hidden_width:] = jnp.zeros((*hid.shape[:3], hid.shape[3] - hidden_width), BF16)
        spread.plane(False)
        spread.plane_far(True)
        group = span_rows // SIDE
        for i in range(SIDE):
            lanes = lax.rem(lax.broadcasted_iota(jnp.int32, (1, 2 * group), 1), group) + (r * span_rows + i * group)
            first_ref[i] = document_starts(lengths_ref, lanes) - (r - 4) * span_rows
        sign = jnp.where(lax.broadcasted_iota(jnp.int32, (1, HD), 1) < HD // 2, -1.0, 1.0)

        def turn(b, carry):
            at = pl.ds(pl.multiple_of(b * 64, 64), 64)
            place_of = r * span_rows + b * 64 + lax.broadcasted_iota(jnp.int32, (64, HD), 0)
            angle = (place_of - document_starts(lengths_ref, place_of)).astype(F32) * inverse_ref[...]
            cos_ref[at, :] = jnp.cos(angle)
            sin_ref[at, :] = jnp.sin(angle) * sign
            return carry

        lax.fori_loop(0, span_rows // 64, turn, 0)

    copies, total = find_rows(
        ids_ref, all_ids, wanted_by, table, found, recv, emb, t, peers, sources, loads[0], ks, kr, xs, xr,
        functools.partial(spread.plane, True), positions,
    )
    scale = lax.rsqrt(total / width + EPSILON)
    for b in range(width // 1024):
        cols = pl.ds(b * 1024, 1024)
        all_ref[t, :, cols] = (emb[:, cols].astype(F32) * scale * attn_gain_ref[:, cols]).astype(BF16)
    loads[1].wait()
    loads[2].wait()
    keys_here = lax.rem(t, 2) == 0

    def begun():
        spread.plane_far(False)
        spread.ring(True)
        spread.cores(True, (0,))

    def project(dz):
        if dz == 0:
            spread.ring(False)
            spread.ring_far(True)
            spread.cores(True, (1, 3))
        lhs, span = row_group(all_ref, z, dz)
        cos, sin = cos_ref[span, :], sin_ref[span, :]
        queries = jnp.dot(lhs, wq[...], preferred_element_type=F32)
        for h in range(queries.shape[1] // HD):
            head = queries[:, h * HD:(h + 1) * HD]
            q[span, h * HD:(h + 1) * HD] = (head * cos + pltpu.roll(head, HD // 2, 1) * sin).astype(BF16)
        both = jnp.dot(lhs, wkv[...], preferred_element_type=F32)
        turned = both * cos + pltpu.roll(both, HD // 2, 1) * sin
        pair[span, :] = jnp.where(keys_here, turned, both).astype(BF16)

    ring_gather(all_ref, gs, gr, z, x, project, begun)
    spread.ring_far(False)
    spread.cores(True, (2,))

    moves_of = Moves(att, att_z, att_x, bs, br, bxs, bxr, z, x)

    def late():
        down.plane(False)
        down.plane_far(True)

    attention(
        q, first_ref, pair, att, win, relay, m_ref, l_ref, acc_ref, as_, ar, z,
        functools.partial(down.plane, True), late, moves_of.finished
    )
    spread.cores(False, (0, 1, 3))
    down.plane_far(False)
    down.ring(True)
    down.cores(True, (0,))

    def mixed(cols, value):
        stream[:, cols] = (emb[:, cols].astype(F32) + value).astype(BF16)

    loads[3].wait()
    spread.cores(False, (2,))
    mix(moves_of, att, att_z, att_x, wo, part, mine, got, ss, sr, z, x, mixed)
    spread.drain()
    all_ref[t] = normalize(stream[...].astype(F32), mlp_gain_ref[...])
    loads[4].wait()
    loads[5].wait()

    loads[6].wait()
    hidden = Moves(hid, hid_z, hid_x, zs, zr, hs, hr, z, x)

    def gate(dz):
        if dz == 0:
            down.ring(False)
            down.ring_far(True)
            down.cores(True, (1, 3))
        lhs, span = row_group(all_ref, z, dz)
        across = (((1,), (1,)), ((), ()))
        gated = lax.dot_general(lhs, wg[...], across, preferred_element_type=F32)
        upper = lax.dot_general(lhs, wu[...], across, preferred_element_type=F32)
        value = (gated / (1.0 + jnp.exp(-gated)) * upper).astype(BF16)
        hid[wrap(z + dz), :, :, :hidden_width] = value.reshape(SIDE * UNITS, UNIT, hidden_width)
        hidden.finished(dz)

    ring_gather(all_ref, gs2, gr2, z, x, gate)
    down.ring_far(False)
    down.cores(True, (2,))

    def arrive(h):
        hidden.arrive(h)
        if h == 0:
            down.cores(False, (0, 1, 3, 2))

    def multiply(h, cols):
        def left(block):
            return block.reshape(-1, hidden_width)

        own = hid[z, :, :, :hidden_width] if h == 0 else hid[:, pl.ds(x * UNITS, UNITS), :, :hidden_width]
        out = jnp.dot(left(own), flat(wd[:, :, cols]), preferred_element_type=F32)
        for n in range(SIDE - 1):
            block = hid_z[n, :, :, :hidden_width] if h == 0 else hid_x[n, :, :, :, :hidden_width]
            out = out + jnp.dot(left(block), flat(down_blocks[n, :, :, cols]), preferred_element_type=F32)
        return out

    def added(cols, value):
        out_ref[:, cols] = (stream[:, cols].astype(F32) + value).astype(BF16)

    short_reduce(mine, got, ss2, sr2, z, x, arrive, multiply, added)
    hidden.drain()
    down.drain()
    for copy in copies:
        copy.wait_send()


def layer(ids, lengths, inverse, attn_gain, mlp_gain, table, wq, wkv, wo, wg, wu, wd):
    rows, width = ids.shape[1], table.shape[1]
    span = rows * GROUP
    group = span // SIDE
    quarter = width // 4
    unit = (UNITS, UNIT)
    padded = -(-wg.shape[0] // 128) * 128
    whole = pl.BlockSpec(memory_space=VMEM)
    outside = pl.BlockSpec(memory_space=pl.ANY)
    peers = DMA((GROUP - 1,))
    return pl.pallas_call(
        layer_kernel,
        out_shape=jax.ShapeDtypeStruct((rows, width), BF16),
        in_specs=[whole, pl.BlockSpec(memory_space=pltpu.SMEM)] + [whole] * 3 + [outside] * 7,
        out_specs=whole,
        scratch_shapes=[
            *[VMEM(w.shape, BF16) for w in (table, wq, wkv, wo, wg, wu, wd)], DMA((7,)),
            VMEM((8, 128), jnp.int32), VMEM((GROUP, 8, 128), jnp.int32),
            VMEM((GROUP, SLOTS, width), BF16), VMEM((GROUP, SLOTS, width), BF16),
            peers, peers, DMA((2, GROUP - 1)), DMA((2, GROUP - 1)),
            VMEM((rows, width), BF16), VMEM((GROUP, rows, width), BF16),
            VMEM((span, wq.shape[1]), BF16), VMEM((span, HD), BF16),
            VMEM((span, HD), F32), VMEM((span, HD), F32), VMEM((SIDE, 1, 2 * group), jnp.int32), *GATHER_SEMS,
            VMEM((5, 2, span, HD), BF16), VMEM((span, HD), BF16),
            VMEM((SIDE, 1, 2 * group), F32), VMEM((SIDE, 1, 2 * group), F32), VMEM((SIDE, HD, 2 * group), F32),
            VMEM((SIDE, SIDE * UNITS, UNIT, 2 * HD), BF16), DMA((24,)), DMA((24,)),
            VMEM((rows, width), BF16), VMEM((SIDE, SIDE * UNITS, UNIT, padded), BF16), *GATHER_SEMS,
            VMEM((SIDE, SIDE * UNITS, UNIT, width), BF16),
            VMEM((SIDE - 1, SIDE * UNITS, UNIT, 2 * HD), BF16), VMEM((SIDE - 1, SIDE, *unit, 2 * HD), BF16),
            VMEM((2, SIDE * UNITS, UNIT, 2 * quarter), BF16), VMEM((2, 6, *unit, quarter), BF16),
            DMA((2, 6)), DMA((2, 6)),
            DMA((SIDE - 1,)), DMA((SIDE - 1,)), DMA((SIDE, SIDE - 1)), DMA((SIDE, SIDE - 1)),
            DMA((8,)), DMA((8,)), DMA((18,)), DMA((18,)), DMA((24,)), DMA((24,)),
            VMEM((SIDE - 1, *wd.shape), BF16),
            VMEM((SIDE - 1, SIDE * UNITS, UNIT, padded), BF16), VMEM((SIDE - 1, SIDE, *unit, padded), BF16),
            DMA((2, 6)), DMA((2, 6)), DMA((SIDE - 1,)), DMA((SIDE - 1,)), DMA((SIDE, SIDE - 1)), DMA((SIDE, SIDE - 1)),
            DMA((4,)), DMA((4,)), DMA((12,)), DMA((12,)), DMA((12,)), DMA((12,)),
        ],
        compiler_params=pltpu.CompilerParams(
            collective_id=0, has_side_effects=True, vmem_limit_bytes=63 * 2**20
        ),
        name="layer",
    )(ids, lengths, inverse, attn_gain, mlp_gain, table, wq, wkv, wo, wg, wu, wd)


def local(ids, doc_lengths, table, attn_gain, wq, wkv, wo, mlp_gain, w_gate, w_up, w_down):
    inverse = np.float32(ROPE_BASE) ** (-np.arange(HD // 2, dtype=np.float32) * np.float32(2.0 / HD))
    inverse = jnp.asarray(np.concatenate([inverse, inverse])[None, :], F32)
    return layer(
        ids[None, :], doc_lengths, inverse, attn_gain[None, :], mlp_gain[None, :],
        table, wq, wkv, wo.reshape(-1, UNIT, wo.shape[1]), w_gate.T, w_up.T, w_down.reshape(-1, UNIT, wo.shape[1]),
    )


def solution(mesh):
    placed = (
        P(("dp", "tensor")),
        P(),
        P("tensor", None),
        P(),
        P(None, "tensor"),
        P(None, "tensor"),
        P("tensor", None),
        P(),
        P(None, "tensor"),
        P(None, "tensor"),
        P("tensor", None),
    )
    return jax.shard_map(
        local, mesh=mesh, in_specs=placed, out_specs=P(("dp", "tensor"), None), check_vma=False
    )
```

```python
import functools

import jax
import jax.numpy as jnp
import numpy as np
from jax import lax
from jax.experimental import pallas as pl
from jax.experimental.pallas import tpu as pltpu
from jax.sharding import PartitionSpec as P

HD = 128
SIDE = 4
GROUP = SIDE * SIDE
SLOTS = 8
UNIT = 16
UNITS = 3

EPSILON = 1e-05
ROPE_BASE = 500000.0
NEGATIVE = -1e30
EXP_SCALE = HD ** (-0.5) * 1.4426950408889634
MESH = pl.DeviceIdType.MESH
VMEM = pltpu.VMEM
DMA = pltpu.SemaphoreType.DMA
BF16 = jnp.bfloat16
F32 = jnp.float32


def wrap(v):
    return lax.rem(v + 2 * SIDE, SIDE)


def place(z, x):
    return wrap(z) * SIDE + wrap(x)


def here():
    t = lax.axis_index("tensor")
    return t // SIDE, lax.rem(t, SIDE)


def greet(peers):
    barrier = pltpu.get_barrier_semaphore()
    for peer in peers:
        pl.semaphore_signal(barrier, inc=1, device_id=peer, device_id_type=MESH)
    pl.semaphore_wait(barrier, len(peers))


def remote(src, dst, send_sem, recv_sem, peer):
    return pltpu.make_async_remote_copy(
        src_ref=src, dst_ref=dst, send_sem=send_sem, recv_sem=recv_sem,
        device_id=peer, device_id_type=MESH,
    )


def ring_gather(buf, ssem, rsem, z, x, ready, begun=lambda: None):
    half = buf.shape[-1] // 2
    quarter = half // 2
    started = []

    def block(h, first, second):
        return place(z + second, x + first) if h == 0 else place(z + first, x + second)

    def view(h, first, second, part):
        start, size = (h * half, half) if part == 0 else (h * half + (part - 1) * quarter, quarter)
        return buf.at[block(h, first, second), :, pl.ds(start, size)]

    def send(h, n, first, second, part, axis, d):
        ref = view(h, first, second, part)
        peer = {"tensor": block(h, d, 0) if axis == 0 else block(h, 0, d)}
        copy = remote(ref, ref, ssem.at[h, n], rsem.at[h, n], peer)
        copy.start()
        started.append(copy)

    def recv(h, n, first, second, part):
        ref = view(h, first, second, part)
        remote(ref, ref, ssem.at[h, n], rsem.at[h, n], {"tensor": block(h, 1, 0)}).wait_recv()

    offsets = (0, -1, 1, 2)
    for h in range(2):
        send(h, 0, 0, 0, 0, 0, 1)
        send(h, 1, 0, 0, 0, 0, -1)
    for h in range(2):
        send(h, 4, 0, 0, 0, 1, 1)
        send(h, 5, 0, 0, 0, 1, -1)
    begun()
    for h in range(2):
        recv(h, 0, -1, 0, 0)
        send(h, 2, -1, 0, 1, 0, 1)
        recv(h, 1, 1, 0, 0)
        send(h, 3, 1, 0, 2, 0, -1)
        for n in (1, 2):
            send(h, 4 + 2 * n, offsets[n], 0, 0, 1, 1)
            send(h, 5 + 2 * n, offsets[n], 0, 0, 1, -1)

    def relay(n):
        k = offsets[n]
        for h in range(2):
            recv(h, 4 + 2 * n, k, -1, 0)
            send(h, 12 + 2 * n, k, -1, 1, 1, 1)
            recv(h, 5 + 2 * n, k, 1, 0)
            send(h, 13 + 2 * n, k, 1, 2, 1, -1)

    relay(0)
    for h in range(2):
        recv(h, 2, 2, 0, 1)
        recv(h, 3, 2, 0, 2)
        send(h, 10, 2, 0, 0, 1, 1)
        send(h, 11, 2, 0, 0, 1, -1)
    relay(1)
    relay(2)

    def far(h, n):
        recv(h, 12 + 2 * n, offsets[n], 2, 1)
        recv(h, 13 + 2 * n, offsets[n], 2, 2)

    far(1, 0)
    ready(0)
    relay(3)
    far(1, 1)
    ready(-1)
    far(1, 2)
    ready(1)
    for n in range(4):
        far(0, n)
    far(1, 3)
    ready(2)
    for copy in started:
        copy.wait_send()


GATHER_SEMS = [DMA((2, 20)), DMA((2, 20))]


def flat(block):
    return block.reshape(-1, block.shape[-1])


def flat_units(block):
    return block.reshape(-1, UNIT, block.shape[-1])


class Moves:
    def __init__(self, rows, to_z, to_x, zs, zr, xs, xr, z, x):
        self.refs = rows, to_z, to_x, zs, zr, xs, xr
        self.z, self.x = z, x
        self.started = []

    def along_z(self, dz):
        rows, to_z, to_x, zs, zr, xs, xr = self.refs
        o = dz % SIDE
        peer = {"tensor": place(self.z + o, self.x)}
        return remote(rows.at[wrap(self.z + dz)], to_z.at[SIDE - o - 1], zs.at[o - 1], zr.at[o - 1], peer)

    def along_x(self, dz, o):
        rows, to_z, to_x, zs, zr, xs, xr = self.refs
        zz = wrap(self.z + dz)
        src = rows.at[zz, pl.ds(wrap(self.x + o) * UNITS, UNITS)]
        sems = xs.at[dz % SIDE, o - 1], xr.at[dz % SIDE, o - 1]
        return remote(src, to_x.at[SIDE - o - 1, zz], *sems, {"tensor": place(self.z, self.x + o)})

    def finished(self, dz):
        moves = [self.along_z(dz)] if dz else []
        moves += [self.along_x(dz, o) for o in (2, 1, 3)]
        for move in moves:
            move.start()
        self.started += moves

    def arrive(self, h):
        if h == 0:
            for dz in (-1, 1, 2):
                self.along_z(dz).wait_recv()
        else:
            for dz in (2, 1, -1, 0):
                for o in (1, 3, 2):
                    self.along_x(dz, o).wait_recv()

    def drain(self):
        for move in self.started:
            move.wait_send()


class Spread:
    def __init__(self, wo_hbm, part, ssem, rsem, ysem, yrem, csem, crem, z, x):
        r = lax.axis_index("dp")
        self.y, self.c = r // 2, lax.rem(r, 2)
        self.wo, self.part, self.z, self.x = wo_hbm, part, z, x
        self.sems = (ssem, rsem), (ysem, yrem), (csem, crem)
        self.half = part.shape[-1] // 2
        self.started = []
        self.slices = [(o, h) for h in range(2) for o in (1, 2, 3)]

    def share(self, dy, other=False):
        c = 1 - self.c if other else self.c
        return lax.rem(self.y + dy + SIDE, SIDE) * 2 + c

    def columns(self, h, q):
        quarter = self.half // 2
        return pl.ds(h * self.half, self.half) if q is None else pl.ds(h * self.half + q * quarter, quarter)

    def view(self, o, share, h, q=None):
        unit = 16 * (o - 1) + 2 * share
        a = unit // 12
        return self.part.at[a, pl.ds(unit - a * 12, 2), :, self.columns(h, q)]

    def copy(self, phase, index, src, dst, peer, start):
        send, recv = self.sems[phase]
        copy = remote(src, dst, send.at[index], recv.at[index], peer)
        if start:
            copy.start()
            self.started.append(copy)
        else:
            copy.wait_recv()

    def along(self, h, d):
        return {"tensor": place(self.z + d, self.x) if h == 0 else place(self.z, self.x + d)}

    def plane(self, start):
        own = self.share(0)
        for h in range(2):
            mine = self.wo.at[pl.ds(2 * own, 2), :, self.columns(h, None)]
            for n, (o, d) in enumerate(((3, 1), (1, -1))):
                dst = self.view(o, own, h)
                self.copy(0, h * 4 + n, mine if start else dst, dst, self.along(h, d), start)

    def plane_far(self, start):
        own = self.share(0)
        for h in range(2):
            for n, (o, d) in enumerate(((3, 1), (1, -1))):
                dst = self.view(2, own, h, n)
                self.copy(0, h * 4 + 2 + n, self.view(o, own, h, n) if start else dst, dst, self.along(h, d), start)

    def around(self, d):
        return {"dp": lax.rem(self.y + d + SIDE, SIDE) * 2 + self.c}

    def ring(self, start):
        for n, (o, h) in enumerate(self.slices):
            for k, d in enumerate((1, -1)):
                ref = self.view(o, self.share(0 if start else -d), h)
                self.copy(1, k * 9 + n, ref, ref, self.around(d), start)

    def ring_far(self, start):
        for n in range(3):
            for k, d in enumerate((1, -1)):
                o, h = self.slices[3 * k + n]
                ref = self.view(o, self.share(-d if start else -2 * d), h)
                self.copy(1, k * 9 + 6 + n, ref, ref, self.around(d), start)

    def cores(self, start, steps):
        peer = {"dp": self.y * 2 + 1 - self.c}
        for dy in steps:
            for n, (o, h) in enumerate(self.slices):
                ref = self.view(o, self.share(dy, not start), h)
                self.copy(2, dy * 6 + n, ref, ref, peer, start)

    def drain(self):
        for copy in self.started:
            copy.wait_send()


class SpreadDown:
    def __init__(self, w_hbm, blocks, sems, z, x):
        r = lax.axis_index("dp")
        self.y, self.c = r // 2, lax.rem(r, 2)
        self.w, self.blocks, self.sems, self.z, self.x = w_hbm, blocks, sems, z, x
        self.units = blocks.shape[1] // SIDE
        self.half = blocks.shape[-1] // 2
        self.started = []

    def columns(self, c, q=None):
        size = self.half if q is None else self.half // 2
        start = c * self.half + (0 if q is None else q * size)
        return pl.ds(pl.multiple_of(start, size), size)

    def rows(self, dy):
        return pl.ds(lax.rem(self.y + dy + SIDE, SIDE) * self.units, self.units)

    def view(self, o, dy, c, q=None):
        return self.blocks.at[o - 1, self.rows(dy), :, self.columns(c, q)]

    def copy(self, phase, index, src, dst, peer, start):
        send, recv = self.sems[2 * phase:2 * phase + 2]
        copy = remote(src, dst, send.at[index], recv.at[index], peer)
        if start:
            copy.start()
            self.started.append(copy)
        else:
            copy.wait_recv()

    def along(self, d):
        return {"tensor": place(self.z + d * (1 - self.c), self.x + d * self.c)}

    def plane(self, start):
        for n, (o, d) in enumerate(((3, 1), (1, -1))):
            dst = self.view(o, 0, self.c)
            src = self.w.at[self.rows(0), :, self.columns(self.c)] if start else dst
            self.copy(0, n, src, dst, self.along(d), start)

    def plane_far(self, start):
        for n, (o, d) in enumerate(((3, 1), (1, -1))):
            dst = self.view(2, 0, self.c, n)
            self.copy(0, 2 + n, self.view(o, 0, self.c, n) if start else dst, dst, self.along(d), start)

    def around(self, d):
        return {"dp": lax.rem(self.y + d + SIDE, SIDE) * 2 + self.c}

    def ring(self, start):
        for o in (1, 2, 3):
            for k, d in enumerate((1, -1)):
                ref = self.view(o, 0 if start else -d, self.c)
                self.copy(1, k * 6 + o - 1, ref, ref, self.around(d), start)

    def ring_far(self, start):
        for o in (1, 2, 3):
            for k, d in enumerate((1, -1)):
                ref = self.view(o, -d if start else -2 * d, self.c, k)
                self.copy(1, k * 6 + 2 + o, ref, ref, self.around(d), start)

    def cores(self, start, steps):
        peer = {"dp": self.y * 2 + 1 - self.c}
        for dy in steps:
            for o in (1, 2, 3):
                ref = self.view(o, dy, self.c if start else 1 - self.c)
                self.copy(2, dy * 3 + o - 1, ref, ref, peer, start)

    def drain(self):
        for copy in self.started:
            copy.wait_send()


def short_reduce(mine, got, ssem, rsem, z, x, order, arrive, multiply, finish, begun=lambda: None):
    half = mine.shape[-1]
    quarter = half // 2
    started = []

    def block(h, j, q):
        n = wrap(x + j) if h == 0 else wrap(z + j)
        return mine.at[h, pl.ds(n * UNITS, UNITS), :, pl.ds(q * quarter, quarter)]

    def send(h, slot, src, d):
        peer = {"tensor": place(z, x + d) if h == 0 else place(z + d, x)}
        copy = remote(src, got.at[h, slot], ssem.at[h, slot], rsem.at[h, slot], peer)
        copy.start()
        started.append(copy)

    def recv(h, slot):
        ref = got.at[h, slot]
        remote(ref, ref, ssem.at[h, slot], rsem.at[h, slot], {"tensor": place(z, x + 1)}).wait_recv()

    def load(ref):
        return ref[...].astype(F32)

    step = min(512, quarter)

    def make(h, q):
        def column(c, carry):
            at = pl.multiple_of(q * quarter + c * step, step)
            out = multiply(h, pl.ds(h * half + at, step)).astype(BF16)
            mine[h, :, :, pl.ds(at, step)] = out.reshape(SIDE * UNITS, UNIT, step)
            return carry

        lax.fori_loop(0, quarter // step, column, 0)

    for q in range(2):
        for h in order:
            if q == 0:
                arrive(h)
            make(h, q)
            d = 1 - 2 * q
            send(h, 3 * q, block(h, 2, q), d)
            send(h, (4, 1)[q], block(h, -d, q), -d)
        if q == 0:
            begun()
    for h in order:
        for slot, q, d in ((0, 0, 1), (3, 1, -1)):
            recv(h, slot)
            got[h, slot] = (load(got.at[h, slot]) + load(block(h, d, q))).astype(BF16)
            send(h, slot + 2, got.at[h, slot], d)
    for h in order:
        for slot in (1, 4, 2, 5):
            recv(h, slot)
        for q in range(2):
            a, b = ((2, 4), (1, 5))[q]
            value = load(block(h, 0, q)) + load(got.at[h, a]) + load(got.at[h, b])
            finish(pl.ds(h * half + q * quarter, quarter), flat(value))
    for copy in started:
        copy.wait_send()


def mix(moves, att, att_z, att_x, wo, part, mine, got, ssem, rsem, z, x, finish, begun):
    def multiply(h, cols):
        own = flat(att[z] if h == 0 else att[:, pl.ds(x * UNITS, UNITS)])
        others = jnp.concatenate([flat((att_z, att_x)[h][n]) for n in range(SIDE - 1)], axis=1)
        out = jnp.dot(own, flat(wo[:, :, cols]), preferred_element_type=F32)
        weights = part[:, :, :, cols].reshape(others.shape[1], out.shape[1])
        return out + jnp.dot(others, weights, preferred_element_type=F32)

    short_reduce(mine, got, ssem, rsem, z, x, (0, 1), moves.arrive, multiply, finish, begun)
    moves.drain()


def normalize(rows, gain):
    scale = lax.rsqrt(jnp.mean(rows * rows, axis=-1, keepdims=True) + EPSILON)
    return (rows * scale * gain).astype(BF16)


def row_group(all_ref, z, dz):
    rows, width = all_ref.shape[1:]
    zz = wrap(z + dz)
    lhs = all_ref[pl.ds(zz * SIDE, SIDE)].reshape(SIDE * rows, width)
    return lhs, pl.ds(pl.multiple_of(zz * SIDE * rows, 16), SIDE * rows)


def find_rows(ids_ref, all_ids, wanted_by, table, found, recv, emb_ref, t, peers, sources, load, ks, kr, xs, xr, asked, meanwhile):
    copies = []
    rows, width = emb_ref.shape
    wanted_by[...] = jnp.full_like(wanted_by, -1)
    wanted_by[:, :rows] = jnp.broadcast_to(ids_ref[...], (8, rows))
    for n, p in enumerate(peers):
        copy = remote(wanted_by, all_ids.at[t], ks.at[n], kr.at[n], {"tensor": p})
        copy.start()
        copies.append(copy)
    all_ids[t] = wanted_by[...]
    slots = GROUP * SLOTS
    owned = table.shape[0]
    square = (128, 128)
    row, lane = lax.broadcasted_iota(jnp.int32, square, 0), lax.broadcasted_iota(jnp.int32, square, 1)
    own = jnp.broadcast_to(wanted_by[:1, :], square)
    owner = jnp.right_shift(own, owned.bit_length() - 1).astype(F32)
    same = (owner == owner.T) & (row < lane)
    source = owner * SLOTS + jnp.sum(jnp.where(same, 1.0, 0.0), axis=0, keepdims=True)
    chosen = jnp.where((source == row.astype(F32)) & (own >= 0), 1.0, 0.0).T[:rows].astype(BF16)
    before = jnp.where(row < lane, 1.0, 0.0).astype(BF16)
    for n, p in enumerate(sources):
        remote(wanted_by, all_ids.at[p], ks.at[n], kr.at[n], {"tensor": p}).wait_recv()
    asked()
    local_rows = all_ids[...].reshape(slots, 128) - t * owned
    inside = (local_rows >= 0) & (local_rows < owned)
    rank = jnp.dot(jnp.where(inside, 1.0, 0.0).astype(BF16), before, preferred_element_type=F32)
    slot = lax.rem(row, SLOTS).astype(F32)
    wanted = jnp.sum(
        jnp.where(inside & (rank == slot), local_rows.astype(F32), 0.0), axis=1, keepdims=True
    )
    pick = lax.broadcasted_iota(jnp.int32, (slots, owned), 1).astype(F32) == wanted
    pick = jnp.where(pick, 1.0, 0.0).astype(BF16)
    load.wait()
    parts = 2
    step = width // parts
    for c in range(parts):
        def fetch(b, carry):
            cols = pl.ds(pl.multiple_of(c * step + b * 512, 512), 512)
            out = jnp.dot(pick, table[:, cols], preferred_element_type=F32).astype(BF16)
            found[:, :, cols] = out.reshape(GROUP, SLOTS, 512)
            return carry

        lax.fori_loop(0, step // 512, fetch, 0)
        cols = pl.ds(c * step, step)
        for n, p in enumerate(peers):
            copy = remote(found.at[p, :, cols], recv.at[t, :, cols], xs.at[c, n], xr.at[c, n], {"tensor": p})
            copy.start()
            copies.append(copy)
        recv[t, :, cols] = found[t, :, cols]
    meanwhile()
    total = jnp.zeros((rows, 1), F32)
    for c in range(parts):
        cols = pl.ds(c * step, step)
        for n, p in enumerate(sources):
            ref = recv.at[p, :, cols]
            remote(ref, ref, xs.at[c, n], xr.at[c, n], {"tensor": p}).wait_recv()
        for b in range(step // 1024):
            cols = pl.ds(c * step + b * 1024, 1024)
            picked = jnp.dot(chosen, recv[:, :, cols].reshape(slots, 1024), preferred_element_type=F32)
            emb_ref[:, cols] = picked.astype(BF16)
            total += jnp.sum(picked * picked, axis=-1, keepdims=True)
    return copies, total


def document_starts(lengths_ref, positions):
    first = jnp.zeros_like(positions)
    start = jnp.int32(0)
    for d in range(lengths_ref.shape[0]):
        first = jnp.where(positions >= start, start, first)
        start = start + lengths_ref[d]
    return first


def attention(q_ref, first_ref, pair_ref, att_ref, win_ref, relay, m_ref, l_ref, acc_ref, ssem, rsem, z, early, late, done):
    t = lax.axis_index("tensor")
    r = lax.axis_index("dp")
    y, c = r // 2, lax.rem(r, 2)
    kind = lax.rem(t, 2)
    rows = q_ref.shape[0]
    group = rows // SIDE
    partner = {"tensor": t + 1 - 2 * kind}
    up = {"dp": lax.rem(y + 1, SIDE) * 2 + c}
    down = {"dp": lax.rem(y + SIDE - 1, SIDE) * 2 + c}
    other = {"dp": y * 2 + 1 - c}

    def copy(n, src, dst, peer):
        return remote(src, dst, ssem.at[n], rsem.at[n], peer)

    def step(w, i, count, causal):
        span = pl.ds(pl.multiple_of(i * group, UNIT), group)
        q = jnp.concatenate([q_ref[span, :HD], q_ref[span, HD:]], axis=0)
        scores = lax.dot_general(
            win_ref[w, 0, :count, :], q, (((1,), (1,)), ((), ())), preferred_element_type=F32
        )
        at = lax.broadcasted_iota(jnp.int32, (count, 1), 0) + w * rows
        allowed = at >= first_ref[i]
        if causal:
            query = lax.rem(lax.broadcasted_iota(jnp.int32, (1, 2 * group), 1), group)
            allowed &= at <= query + (4 * rows + i * group)
        scores = jnp.where(allowed, scores, NEGATIVE)
        top = jnp.max(scores, axis=0, keepdims=True) * EXP_SCALE
        if not causal:
            old = m_ref[i]
            top = jnp.maximum(old, top)
            decay = jnp.exp2(old - top)
        weights = jnp.exp2(scores * EXP_SCALE - top)
        total = jnp.sum(weights, axis=0, keepdims=True)
        added = lax.dot_general(
            win_ref[w, 1, :count, :], weights.astype(BF16), (((0,), (0,)), ((), ())),
            preferred_element_type=F32,
        )
        l_ref[i] = total if causal else l_ref[i] * decay + total
        acc_ref[i] = added if causal else acc_ref[i] * decay + added
        m_ref[i] = top

    def earlier(w, steps=range(SIDE)):
        @pl.when(r + w >= 4)
        def _():
            for i in steps:
                step(w, i, rows, False)

    piece = rows // 2

    def block(w, k, p):
        return win_ref.at[w, k, pl.ds(p * piece, piece)]

    def pieces(n, src, dst, peer):
        return [copy(2 * n + p, src(p), dst(p), peer) for p in range(2)]

    def within(n, source, target, k, peer):
        return pieces(n, lambda p: block(source, k, p), lambda p: block(target, k, p), peer)

    def mine(p):
        return pair_ref.at[pl.ds(p * piece, piece)]

    def held(p):
        return relay.at[pl.ds(p * piece, piece)]

    def when(condition, *acts):
        @pl.when(condition)
        def _():
            for act in acts:
                act()

    def starts(copies):
        return [one.start for one in copies]

    def recvs(copies):
        return [one.wait_recv for one in copies]

    def sends(copies):
        return [one.wait_send for one in copies]

    lacking = 1 - kind
    swap = pieces(0, mine, lambda p: block(4, kind, p), partner)
    swap_in = pieces(0, mine, lambda p: block(4, lacking, p), partner)
    up_own = pieces(1, mine, lambda p: block(2, kind, p), up)
    up_other = within(2, 4, 2, lacking, up)
    down_own = pieces(3, mine, held, down)
    far_own = pieces(4, held, lambda p: block(0, kind, p), down)
    far_other = within(5, 2, 0, lacking, up)
    near_own = pieces(6, mine, lambda p: block(3, kind, p), other)
    near_other = within(7, 4, 3, lacking, other)
    cross0_own, cross0_other = within(8, 2, 1, kind, other), within(9, 2, 1, lacking, other)
    cross1_own, cross1_other = within(8, 2, 3, kind, other), within(9, 2, 3, lacking, other)
    far1 = within(10, 0, 1, kind, other) + within(11, 0, 1, lacking, other)
    has_up, has_far = y < SIDE - 1, y < SIDE - 2
    got_up, got_far = y > 0, y > 1
    relays = (y == SIDE - 1) | (y == 0)
    for p in range(2):
        swap[p].start()
    when(has_up, *starts(up_own))
    when(has_far, *starts(down_own))
    when(c == 0, *starts(near_own))
    win_ref[4, kind] = pair_ref[...]
    for p in range(2):
        swap_in[p].wait_recv()
        when(has_up, up_other[p].start)
        when(c == 0, near_other[p].start)
        when(relays, down_own[p].wait_recv, far_own[p].start)
    early()
    for i in range(SIDE):
        step(4, i, (i + 1) * group, True)

    when(got_up, *recvs(up_own))
    when(got_up & (c == 0), *starts(cross0_own))
    when(got_up & (c == 1), *starts(cross1_own))
    for p in range(2):
        when(got_up, up_other[p].wait_recv)
        when(got_up & has_up, far_other[p].start)
        when(got_up & (c == 0), cross0_other[p].start)
        when(got_up & (c == 1), cross1_other[p].start)
    when(c == 1, *recvs(near_own + near_other))
    earlier(2 + c)

    when(got_up & (c == 0), *recvs(cross1_own + cross1_other))
    earlier(3 - c)
    late()

    when(got_far, *recvs(far_own + far_other))
    when(got_far & (c == 1), *starts(far1))
    when(got_up & (c == 1), *recvs(cross0_own + cross0_other))
    order = [wrap(z + dz) for dz in (2, 1, -1, 0)]
    earlier(c, order[:2])

    when(got_far & (c == 0), *recvs(far1))
    for n, i in enumerate(order):
        if n > 1:
            earlier(c, [i])
        earlier(1 - c, [i])
        out = (acc_ref[i] / l_ref[i]).T.astype(BF16)
        for h in range(2):
            att_ref[i, :, :, h * HD:(h + 1) * HD] = flat_units(out[h * group:(h + 1) * group])
        done((2, 1, -1, 0)[n])

    when(c == 0, *sends(near_own + near_other))
    when(got_up & (c == 0), *sends(cross0_own + cross0_other))
    when(got_up & (c == 1), *sends(cross1_own + cross1_other))
    when(got_far & (c == 1), *sends(far1))
    when(has_far, *sends(down_own))
    when(has_up, *sends(up_own + up_other))
    when(relays, *sends(far_own))
    when(got_up & has_up, *sends(far_other))
    for one in swap:
        one.wait_send()


def layer_kernel(ids_ref, lengths_ref, inverse_ref, attn_gain_ref, mlp_gain_ref,
                 table_hbm, wq_hbm, wkv_hbm, wo_hbm, wg_hbm, wu_hbm, wd_hbm, out_ref,
                 table, wq, wkv, wo, wg, wu, wd, load_sem,
                 wanted_by, all_ids, found, recv, ks, kr, xs, xr,
                 emb, all_ref, q, pair, cos_ref, sin_ref, first_ref, gs, gr,
                 win, relay, m_ref, l_ref, acc_ref, att, as_, ar,
                 stream, hid, gs2, gr2,
                 part, att_z, att_x, mine, got, ss, sr, bs, br, bxs, bxr, ps, pr, ys, yr, cs, cr,
                 down_blocks, hid_z, hid_x, ss2, sr2, zs, zr, hs, hr, *down_sems):
    z, x = here()
    t = lax.axis_index("tensor")
    r = lax.axis_index("dp")
    y, c = r // 2, lax.rem(r, 2)
    loads = [
        pltpu.make_async_copy(src, dst, load_sem.at[n])
        for n, (src, dst) in enumerate((
            (table_hbm, table), (wq_hbm, wq), (wkv_hbm, wkv), (wo_hbm, wo), (wg_hbm, wg), (wu_hbm, wu), (wd_hbm, wd)
        ))
    ]
    for load in loads:
        load.start()
    peers = [lax.rem(t + n, GROUP) for n in range(1, GROUP)]
    sources = [lax.rem(t + GROUP - n, GROUP) for n in range(1, GROUP)]
    greet([{"tensor": p} for p in peers] + [
        {"dp": lax.rem(y + 1, SIDE) * 2 + c}, {"dp": lax.rem(y + SIDE - 1, SIDE) * 2 + c}, {"dp": y * 2 + 1 - c},
    ])
    rows, width = emb.shape
    span_rows = rows * GROUP
    spread = Spread(wo_hbm, part, ps, pr, ys, yr, cs, cr, z, x)
    down = SpreadDown(wd_hbm, down_blocks, down_sems, z, x)
    hidden_width = wg.shape[0]

    def positions():
        hid[:, :, :, hidden_width:] = jnp.zeros((*hid.shape[:3], hid.shape[3] - hidden_width), BF16)
        spread.plane(False)
        spread.plane_far(True)
        group = span_rows // SIDE
        for i in range(SIDE):
            lanes = lax.rem(lax.broadcasted_iota(jnp.int32, (1, 2 * group), 1), group) + (r * span_rows + i * group)
            first_ref[i] = document_starts(lengths_ref, lanes) - (r - 4) * span_rows
        sign = jnp.where(lax.broadcasted_iota(jnp.int32, (1, HD), 1) < HD // 2, -1.0, 1.0)

        def turn(b, carry):
            at = pl.ds(pl.multiple_of(b * 64, 64), 64)
            place_of = r * span_rows + b * 64 + lax.broadcasted_iota(jnp.int32, (64, HD), 0)
            angle = (place_of - document_starts(lengths_ref, place_of)).astype(F32) * inverse_ref[...]
            cos_ref[at, :] = jnp.cos(angle)
            sin_ref[at, :] = jnp.sin(angle) * sign
            return carry

        lax.fori_loop(0, span_rows // 64, turn, 0)

    copies, total = find_rows(
        ids_ref, all_ids, wanted_by, table, found, recv, emb, t, peers, sources, loads[0], ks, kr, xs, xr,
        functools.partial(spread.plane, True), positions,
    )
    scale = lax.rsqrt(total / width + EPSILON)
    for b in range(width // 1024):
        cols = pl.ds(b * 1024, 1024)
        all_ref[t, :, cols] = (emb[:, cols].astype(F32) * scale * attn_gain_ref[:, cols]).astype(BF16)
    loads[1].wait()
    loads[2].wait()
    keys_here = lax.rem(t, 2) == 0

    def begun():
        spread.plane_far(False)
        spread.ring(True)
        spread.cores(True, (0,))

    def project(dz):
        if dz == 0:
            spread.ring(False)
            spread.ring_far(True)
            spread.cores(True, (1, 3))
        lhs, span = row_group(all_ref, z, dz)
        cos, sin = cos_ref[span, :], sin_ref[span, :]
        queries = jnp.dot(lhs, wq[...], preferred_element_type=F32)
        for h in range(queries.shape[1] // HD):
            head = queries[:, h * HD:(h + 1) * HD]
            q[span, h * HD:(h + 1) * HD] = (head * cos + pltpu.roll(head, HD // 2, 1) * sin).astype(BF16)
        both = jnp.dot(lhs, wkv[...], preferred_element_type=F32)
        turned = both * cos + pltpu.roll(both, HD // 2, 1) * sin
        pair[span, :] = jnp.where(keys_here, turned, both).astype(BF16)

    ring_gather(all_ref, gs, gr, z, x, project, begun)
    spread.ring_far(False)
    spread.cores(True, (2,))

    moves_of = Moves(att, att_z, att_x, bs, br, bxs, bxr, z, x)

    def late():
        down.plane(False)
        down.plane_far(True)

    attention(
        q, first_ref, pair, att, win, relay, m_ref, l_ref, acc_ref, as_, ar, z,
        functools.partial(down.plane, True), late, moves_of.finished
    )
    spread.cores(False, (0, 1, 3))

    def onward():
        down.plane_far(False)
        down.ring(True)
        down.cores(True, (0,))

    def mixed(cols, value):
        stream[:, cols] = (emb[:, cols].astype(F32) + value).astype(BF16)

    loads[3].wait()
    spread.cores(False, (2,))
    mix(moves_of, att, att_z, att_x, wo, part, mine, got, ss, sr, z, x, mixed, onward)
    spread.drain()
    all_ref[t] = normalize(stream[...].astype(F32), mlp_gain_ref[...])
    loads[4].wait()
    loads[5].wait()

    loads[6].wait()
    hidden = Moves(hid, hid_z, hid_x, zs, zr, hs, hr, z, x)

    def gate(dz):
        if dz == 0:
            down.ring(False)
            down.ring_far(True)
            down.cores(True, (1, 3))
        lhs, span = row_group(all_ref, z, dz)
        across = (((1,), (1,)), ((), ()))
        gated = lax.dot_general(lhs, wg[...], across, preferred_element_type=F32)
        upper = lax.dot_general(lhs, wu[...], across, preferred_element_type=F32)
        value = (gated / (1.0 + jnp.exp(-gated)) * upper).astype(BF16)
        hid[wrap(z + dz), :, :, :hidden_width] = value.reshape(SIDE * UNITS, UNIT, hidden_width)
        hidden.finished(dz)

    ring_gather(all_ref, gs2, gr2, z, x, gate)
    down.ring_far(False)
    down.cores(True, (2,))

    def arrive(h):
        hidden.arrive(h)
        if h == 1:
            down.cores(False, (0, 1, 3, 2))

    def multiply(h, cols):
        def left(block):
            return block.reshape(-1, hidden_width)

        own = hid[z, :, :, :hidden_width] if h == 0 else hid[:, pl.ds(x * UNITS, UNITS), :, :hidden_width]
        out = jnp.dot(left(own), flat(wd[:, :, cols]), preferred_element_type=F32)
        for n in range(SIDE - 1):
            block = hid_z[n, :, :, :hidden_width] if h == 0 else hid_x[n, :, :, :, :hidden_width]
            out = out + jnp.dot(left(block), flat(down_blocks[n, :, :, cols]), preferred_element_type=F32)
        return out

    def added(cols, value):
        out_ref[:, cols] = (stream[:, cols].astype(F32) + value).astype(BF16)

    short_reduce(mine, got, ss2, sr2, z, x, (1, 0), arrive, multiply, added)
    hidden.drain()
    down.drain()
    for copy in copies:
        copy.wait_send()


def layer(ids, lengths, inverse, attn_gain, mlp_gain, table, wq, wkv, wo, wg, wu, wd):
    rows, width = ids.shape[1], table.shape[1]
    span = rows * GROUP
    group = span // SIDE
    quarter = width // 4
    unit = (UNITS, UNIT)
    padded = -(-wg.shape[0] // 128) * 128
    whole = pl.BlockSpec(memory_space=VMEM)
    outside = pl.BlockSpec(memory_space=pl.ANY)
    peers = DMA((GROUP - 1,))
    return pl.pallas_call(
        layer_kernel,
        out_shape=jax.ShapeDtypeStruct((rows, width), BF16),
        in_specs=[whole, pl.BlockSpec(memory_space=pltpu.SMEM)] + [whole] * 3 + [outside] * 7,
        out_specs=whole,
        scratch_shapes=[
            *[VMEM(w.shape, BF16) for w in (table, wq, wkv, wo, wg, wu, wd)], DMA((7,)),
            VMEM((8, 128), jnp.int32), VMEM((GROUP, 8, 128), jnp.int32),
            VMEM((GROUP, SLOTS, width), BF16), VMEM((GROUP, SLOTS, width), BF16),
            peers, peers, DMA((2, GROUP - 1)), DMA((2, GROUP - 1)),
            VMEM((rows, width), BF16), VMEM((GROUP, rows, width), BF16),
            VMEM((span, wq.shape[1]), BF16), VMEM((span, HD), BF16),
            VMEM((span, HD), F32), VMEM((span, HD), F32), VMEM((SIDE, 1, 2 * group), jnp.int32), *GATHER_SEMS,
            VMEM((5, 2, span, HD), BF16), VMEM((span, HD), BF16),
            VMEM((SIDE, 1, 2 * group), F32), VMEM((SIDE, 1, 2 * group), F32), VMEM((SIDE, HD, 2 * group), F32),
            VMEM((SIDE, SIDE * UNITS, UNIT, 2 * HD), BF16), DMA((24,)), DMA((24,)),
            VMEM((rows, width), BF16), VMEM((SIDE, SIDE * UNITS, UNIT, padded), BF16), *GATHER_SEMS,
            VMEM((SIDE, SIDE * UNITS, UNIT, width), BF16),
            VMEM((SIDE - 1, SIDE * UNITS, UNIT, 2 * HD), BF16), VMEM((SIDE - 1, SIDE, *unit, 2 * HD), BF16),
            VMEM((2, SIDE * UNITS, UNIT, 2 * quarter), BF16), VMEM((2, 6, *unit, quarter), BF16),
            DMA((2, 6)), DMA((2, 6)),
            DMA((SIDE - 1,)), DMA((SIDE - 1,)), DMA((SIDE, SIDE - 1)), DMA((SIDE, SIDE - 1)),
            DMA((8,)), DMA((8,)), DMA((18,)), DMA((18,)), DMA((24,)), DMA((24,)),
            VMEM((SIDE - 1, *wd.shape), BF16),
            VMEM((SIDE - 1, SIDE * UNITS, UNIT, padded), BF16), VMEM((SIDE - 1, SIDE, *unit, padded), BF16),
            DMA((2, 6)), DMA((2, 6)), DMA((SIDE - 1,)), DMA((SIDE - 1,)), DMA((SIDE, SIDE - 1)), DMA((SIDE, SIDE - 1)),
            DMA((4,)), DMA((4,)), DMA((12,)), DMA((12,)), DMA((12,)), DMA((12,)),
        ],
        compiler_params=pltpu.CompilerParams(
            collective_id=0, has_side_effects=True, vmem_limit_bytes=63 * 2**20
        ),
        name="layer",
    )(ids, lengths, inverse, attn_gain, mlp_gain, table, wq, wkv, wo, wg, wu, wd)


def local(ids, doc_lengths, table, attn_gain, wq, wkv, wo, mlp_gain, w_gate, w_up, w_down):
    inverse = np.float32(ROPE_BASE) ** (-np.arange(HD // 2, dtype=np.float32) * np.float32(2.0 / HD))
    inverse = jnp.asarray(np.concatenate([inverse, inverse])[None, :], F32)
    return layer(
        ids[None, :], doc_lengths, inverse, attn_gain[None, :], mlp_gain[None, :],
        table, wq, wkv, wo.reshape(-1, UNIT, wo.shape[1]), w_gate.T, w_up.T, w_down.reshape(-1, UNIT, wo.shape[1]),
    )


def solution(mesh):
    placed = (
        P(("dp", "tensor")),
        P(),
        P("tensor", None),
        P(),
        P(None, "tensor"),
        P(None, "tensor"),
        P("tensor", None),
        P(),
        P(None, "tensor"),
        P(None, "tensor"),
        P("tensor", None),
    )
    return jax.shard_map(
        local, mesh=mesh, in_specs=placed, out_specs=P(("dp", "tensor"), None), check_vma=False
    )
```

```python
import functools

import jax
import jax.numpy as jnp
import numpy as np
from jax import lax
from jax.experimental import pallas as pl
from jax.experimental.pallas import tpu as pltpu
from jax.sharding import PartitionSpec as P

HD = 128
SIDE = 4
GROUP = SIDE * SIDE
SLOTS = 8
PARTS = 4
UNIT = 16
UNITS = 3

EPSILON = 1e-05
ROPE_BASE = 500000.0
NEGATIVE = -1e30
EXP_SCALE = HD ** (-0.5) * 1.4426950408889634
MESH = pl.DeviceIdType.MESH
VMEM = pltpu.VMEM
DMA = pltpu.SemaphoreType.DMA
BF16 = jnp.bfloat16
F32 = jnp.float32


def wrap(v):
    return lax.rem(v + 2 * SIDE, SIDE)


def place(z, x):
    return wrap(z) * SIDE + wrap(x)


def here():
    t = lax.axis_index("tensor")
    return t // SIDE, lax.rem(t, SIDE)


def greet(peers):
    barrier = pltpu.get_barrier_semaphore()
    for peer in peers:
        pl.semaphore_signal(barrier, inc=1, device_id=peer, device_id_type=MESH)
    pl.semaphore_wait(barrier, len(peers))


def remote(src, dst, send_sem, recv_sem, peer):
    return pltpu.make_async_remote_copy(
        src_ref=src, dst_ref=dst, send_sem=send_sem, recv_sem=recv_sem,
        device_id=peer, device_id_type=MESH,
    )


def ring_gather(buf, ssem, rsem, z, x, ready, begun=lambda: None):
    half = buf.shape[-1] // 2
    quarter = half // 2
    started = []

    def block(h, first, second):
        return place(z + second, x + first) if h == 0 else place(z + first, x + second)

    def view(h, first, second, part):
        start, size = (h * half, half) if part == 0 else (h * half + (part - 1) * quarter, quarter)
        return buf.at[block(h, first, second), :, pl.ds(start, size)]

    def send(h, n, first, second, part, axis, d):
        ref = view(h, first, second, part)
        peer = {"tensor": block(h, d, 0) if axis == 0 else block(h, 0, d)}
        copy = remote(ref, ref, ssem.at[h, n], rsem.at[h, n], peer)
        copy.start()
        started.append(copy)

    def recv(h, n, first, second, part):
        ref = view(h, first, second, part)
        remote(ref, ref, ssem.at[h, n], rsem.at[h, n], {"tensor": block(h, 1, 0)}).wait_recv()

    offsets = (0, -1, 1, 2)
    for h in range(2):
        send(h, 0, 0, 0, 0, 0, 1)
        send(h, 1, 0, 0, 0, 0, -1)
    for h in range(2):
        send(h, 4, 0, 0, 0, 1, 1)
        send(h, 5, 0, 0, 0, 1, -1)
    begun()
    for h in range(2):
        recv(h, 0, -1, 0, 0)
        send(h, 2, -1, 0, 1, 0, 1)
        recv(h, 1, 1, 0, 0)
        send(h, 3, 1, 0, 2, 0, -1)
        for n in (1, 2):
            send(h, 4 + 2 * n, offsets[n], 0, 0, 1, 1)
            send(h, 5 + 2 * n, offsets[n], 0, 0, 1, -1)

    def relay(n):
        k = offsets[n]
        for h in range(2):
            recv(h, 4 + 2 * n, k, -1, 0)
            send(h, 12 + 2 * n, k, -1, 1, 1, 1)
            recv(h, 5 + 2 * n, k, 1, 0)
            send(h, 13 + 2 * n, k, 1, 2, 1, -1)

    relay(0)
    for h in range(2):
        recv(h, 2, 2, 0, 1)
        recv(h, 3, 2, 0, 2)
        send(h, 10, 2, 0, 0, 1, 1)
        send(h, 11, 2, 0, 0, 1, -1)
    relay(1)
    relay(2)

    def far(h, n):
        recv(h, 12 + 2 * n, offsets[n], 2, 1)
        recv(h, 13 + 2 * n, offsets[n], 2, 2)

    far(1, 0)
    ready(0)
    relay(3)
    far(1, 1)
    ready(-1)
    far(1, 2)
    ready(1)
    for n in range(4):
        far(0, n)
    far(1, 3)
    ready(2)
    for copy in started:
        copy.wait_send()


GATHER_SEMS = [DMA((2, 20)), DMA((2, 20))]


def flat(block):
    return block.reshape(-1, block.shape[-1])


def flat_units(block):
    return block.reshape(-1, UNIT, block.shape[-1])


class Moves:
    def __init__(self, rows, to_z, to_x, zs, zr, xs, xr, z, x):
        self.refs = rows, to_z, to_x, zs, zr, xs, xr
        self.z, self.x = z, x
        self.started = []

    def along_z(self, dz):
        rows, to_z, to_x, zs, zr, xs, xr = self.refs
        o = dz % SIDE
        peer = {"tensor": place(self.z + o, self.x)}
        return remote(rows.at[wrap(self.z + dz)], to_z.at[SIDE - o - 1], zs.at[o - 1], zr.at[o - 1], peer)

    def along_x(self, dz, o):
        rows, to_z, to_x, zs, zr, xs, xr = self.refs
        zz = wrap(self.z + dz)
        src = rows.at[zz, pl.ds(wrap(self.x + o) * UNITS, UNITS)]
        sems = xs.at[dz % SIDE, o - 1], xr.at[dz % SIDE, o - 1]
        return remote(src, to_x.at[SIDE - o - 1, zz], *sems, {"tensor": place(self.z, self.x + o)})

    def finished(self, dz):
        moves = [self.along_z(dz)] if dz else []
        moves += [self.along_x(dz, o) for o in (2, 1, 3)]
        for move in moves:
            move.start()
        self.started += moves

    def arrive(self, h):
        if h == 0:
            for dz in (-1, 1, 2):
                self.along_z(dz).wait_recv()
        else:
            for dz in (2, 1, -1, 0):
                for o in (1, 3, 2):
                    self.along_x(dz, o).wait_recv()

    def drain(self):
        for move in self.started:
            move.wait_send()


class Spread:
    def __init__(self, wo_hbm, part, ssem, rsem, ysem, yrem, csem, crem, z, x):
        r = lax.axis_index("dp")
        self.y, self.c = r // 2, lax.rem(r, 2)
        self.wo, self.part, self.z, self.x = wo_hbm, part, z, x
        self.sems = (ssem, rsem), (ysem, yrem), (csem, crem)
        self.half = part.shape[-1] // 2
        self.started = []
        self.slices = [(o, h) for h in range(2) for o in (1, 2, 3)]

    def share(self, dy, other=False):
        c = 1 - self.c if other else self.c
        return lax.rem(self.y + dy + SIDE, SIDE) * 2 + c

    def columns(self, h, q):
        quarter = self.half // 2
        return pl.ds(h * self.half, self.half) if q is None else pl.ds(h * self.half + q * quarter, quarter)

    def view(self, o, share, h, q=None):
        unit = 16 * (o - 1) + 2 * share
        a = unit // 12
        return self.part.at[a, pl.ds(unit - a * 12, 2), :, self.columns(h, q)]

    def copy(self, phase, index, src, dst, peer, start):
        send, recv = self.sems[phase]
        copy = remote(src, dst, send.at[index], recv.at[index], peer)
        if start:
            copy.start()
            self.started.append(copy)
        else:
            copy.wait_recv()

    def along(self, h, d):
        return {"tensor": place(self.z + d, self.x) if h == 0 else place(self.z, self.x + d)}

    def plane(self, start):
        own = self.share(0)
        for h in range(2):
            mine = self.wo.at[pl.ds(2 * own, 2), :, self.columns(h, None)]
            for n, (o, d) in enumerate(((3, 1), (1, -1))):
                dst = self.view(o, own, h)
                self.copy(0, h * 4 + n, mine if start else dst, dst, self.along(h, d), start)

    def plane_far(self, start):
        own = self.share(0)
        for h in range(2):
            for n, (o, d) in enumerate(((3, 1), (1, -1))):
                dst = self.view(2, own, h, n)
                self.copy(0, h * 4 + 2 + n, self.view(o, own, h, n) if start else dst, dst, self.along(h, d), start)

    def around(self, d):
        return {"dp": lax.rem(self.y + d + SIDE, SIDE) * 2 + self.c}

    def ring(self, start):
        for n, (o, h) in enumerate(self.slices):
            for k, d in enumerate((1, -1)):
                ref = self.view(o, self.share(0 if start else -d), h)
                self.copy(1, k * 9 + n, ref, ref, self.around(d), start)

    def ring_far(self, start):
        for n in range(3):
            for k, d in enumerate((1, -1)):
                o, h = self.slices[3 * k + n]
                ref = self.view(o, self.share(-d if start else -2 * d), h)
                self.copy(1, k * 9 + 6 + n, ref, ref, self.around(d), start)

    def cores(self, start, steps):
        peer = {"dp": self.y * 2 + 1 - self.c}
        for dy in steps:
            for n, (o, h) in enumerate(self.slices):
                ref = self.view(o, self.share(dy, not start), h)
                self.copy(2, dy * 6 + n, ref, ref, peer, start)

    def drain(self):
        for copy in self.started:
            copy.wait_send()


class SpreadDown:
    def __init__(self, w_hbm, blocks, sems, z, x):
        r = lax.axis_index("dp")
        self.y, self.c = r // 2, lax.rem(r, 2)
        self.w, self.blocks, self.sems, self.z, self.x = w_hbm, blocks, sems, z, x
        self.units = blocks.shape[1] // SIDE
        self.half = blocks.shape[-1] // 2
        self.started = []

    def columns(self, c, q=None):
        size = self.half if q is None else self.half // 2
        start = c * self.half + (0 if q is None else q * size)
        return pl.ds(pl.multiple_of(start, size), size)

    def rows(self, dy):
        return pl.ds(lax.rem(self.y + dy + SIDE, SIDE) * self.units, self.units)

    def view(self, o, dy, c, q=None):
        return self.blocks.at[o - 1, self.rows(dy), :, self.columns(c, q)]

    def copy(self, phase, index, src, dst, peer, start):
        send, recv = self.sems[2 * phase:2 * phase + 2]
        copy = remote(src, dst, send.at[index], recv.at[index], peer)
        if start:
            copy.start()
            self.started.append(copy)
        else:
            copy.wait_recv()

    def along(self, d):
        return {"tensor": place(self.z + d * (1 - self.c), self.x + d * self.c)}

    def plane(self, start):
        for n, (o, d) in enumerate(((3, 1), (1, -1))):
            dst = self.view(o, 0, self.c)
            src = self.w.at[self.rows(0), :, self.columns(self.c)] if start else dst
            self.copy(0, n, src, dst, self.along(d), start)

    def plane_far(self, start):
        for n, (o, d) in enumerate(((3, 1), (1, -1))):
            dst = self.view(2, 0, self.c, n)
            self.copy(0, 2 + n, self.view(o, 0, self.c, n) if start else dst, dst, self.along(d), start)

    def around(self, d):
        return {"dp": lax.rem(self.y + d + SIDE, SIDE) * 2 + self.c}

    def ring(self, start):
        for o in (1, 2, 3):
            for k, d in enumerate((1, -1)):
                ref = self.view(o, 0 if start else -d, self.c)
                self.copy(1, k * 6 + o - 1, ref, ref, self.around(d), start)

    def ring_far(self, start):
        for o in (1, 2, 3):
            for k, d in enumerate((1, -1)):
                ref = self.view(o, -d if start else -2 * d, self.c, k)
                self.copy(1, k * 6 + 2 + o, ref, ref, self.around(d), start)

    def cores(self, start, steps):
        peer = {"dp": self.y * 2 + 1 - self.c}
        for dy in steps:
            for o in (1, 2, 3):
                ref = self.view(o, dy, self.c if start else 1 - self.c)
                self.copy(2, dy * 3 + o - 1, ref, ref, peer, start)

    def drain(self):
        for copy in self.started:
            copy.wait_send()


def short_reduce(mine, got, ssem, rsem, z, x, order, arrive, multiply, finish, begun=lambda: None):
    half = mine.shape[-1]
    quarter = half // 2
    started = []

    def block(h, j, q):
        n = wrap(x + j) if h == 0 else wrap(z + j)
        return mine.at[h, pl.ds(n * UNITS, UNITS), :, pl.ds(q * quarter, quarter)]

    def send(h, slot, src, d):
        peer = {"tensor": place(z, x + d) if h == 0 else place(z + d, x)}
        copy = remote(src, got.at[h, slot], ssem.at[h, slot], rsem.at[h, slot], peer)
        copy.start()
        started.append(copy)

    def recv(h, slot):
        ref = got.at[h, slot]
        remote(ref, ref, ssem.at[h, slot], rsem.at[h, slot], {"tensor": place(z, x + 1)}).wait_recv()

    def load(ref):
        return ref[...].astype(F32)

    step = min(512, quarter)

    def make(h, q):
        def column(c, carry):
            at = pl.multiple_of(q * quarter + c * step, step)
            out = multiply(h, pl.ds(h * half + at, step)).astype(BF16)
            mine[h, :, :, pl.ds(at, step)] = out.reshape(SIDE * UNITS, UNIT, step)
            return carry

        lax.fori_loop(0, quarter // step, column, 0)

    for q in range(2):
        for h in order:
            if q == 0:
                arrive(h)
            make(h, q)
            d = 1 - 2 * q
            send(h, 3 * q, block(h, 2, q), d)
            send(h, (4, 1)[q], block(h, -d, q), -d)
        if q == 0:
            begun()
    for h in order:
        for slot, q, d in ((0, 0, 1), (3, 1, -1)):
            recv(h, slot)
            got[h, slot] = (load(got.at[h, slot]) + load(block(h, d, q))).astype(BF16)
            send(h, slot + 2, got.at[h, slot], d)
    for h in order:
        for slot in (1, 4, 2, 5):
            recv(h, slot)
        for q in range(2):
            a, b = ((2, 4), (1, 5))[q]
            value = load(block(h, 0, q)) + load(got.at[h, a]) + load(got.at[h, b])
            finish(pl.ds(h * half + q * quarter, quarter), flat(value))
    for copy in started:
        copy.wait_send()


def mix(moves, att, att_z, att_x, wo, part, mine, got, ssem, rsem, z, x, finish, begun):
    def multiply(h, cols):
        own = flat(att[z] if h == 0 else att[:, pl.ds(x * UNITS, UNITS)])
        others = jnp.concatenate([flat((att_z, att_x)[h][n]) for n in range(SIDE - 1)], axis=1)
        out = jnp.dot(own, flat(wo[:, :, cols]), preferred_element_type=F32)
        weights = part[:, :, :, cols].reshape(others.shape[1], out.shape[1])
        return out + jnp.dot(others, weights, preferred_element_type=F32)

    short_reduce(mine, got, ssem, rsem, z, x, (0, 1), moves.arrive, multiply, finish, begun)
    moves.drain()


def normalize(rows, gain):
    scale = lax.rsqrt(jnp.mean(rows * rows, axis=-1, keepdims=True) + EPSILON)
    return (rows * scale * gain).astype(BF16)


def row_group(all_ref, z, dz):
    rows, width = all_ref.shape[1:]
    zz = wrap(z + dz)
    lhs = all_ref[pl.ds(zz * SIDE, SIDE)].reshape(SIDE * rows, width)
    return lhs, pl.ds(pl.multiple_of(zz * SIDE * rows, 16), SIDE * rows)


def find_rows(ids_ref, all_ids, wanted_by, table, found, recv, emb_ref, t, peers, sources, load, ks, kr, xs, xr, asked, meanwhile):
    copies = []
    rows, width = emb_ref.shape
    wanted_by[...] = jnp.full_like(wanted_by, -1)
    wanted_by[:, :rows] = jnp.broadcast_to(ids_ref[...], (8, rows))
    for n, p in enumerate(peers):
        copy = remote(wanted_by, all_ids.at[t], ks.at[n], kr.at[n], {"tensor": p})
        copy.start()
        copies.append(copy)
    all_ids[t] = wanted_by[...]
    slots = GROUP * SLOTS
    owned = table.shape[0]
    square = (128, 128)
    row, lane = lax.broadcasted_iota(jnp.int32, square, 0), lax.broadcasted_iota(jnp.int32, square, 1)
    own = jnp.broadcast_to(wanted_by[:1, :], square)
    owner = jnp.right_shift(own, owned.bit_length() - 1).astype(F32)
    same = (owner == owner.T) & (row < lane)
    source = owner * SLOTS + jnp.sum(jnp.where(same, 1.0, 0.0), axis=0, keepdims=True)
    chosen = jnp.where((source == row.astype(F32)) & (own >= 0), 1.0, 0.0).T[:rows].astype(BF16)
    before = jnp.where(row < lane, 1.0, 0.0).astype(BF16)
    for n, p in enumerate(sources):
        remote(wanted_by, all_ids.at[p], ks.at[n], kr.at[n], {"tensor": p}).wait_recv()
    asked()
    local_rows = all_ids[...].reshape(slots, 128) - t * owned
    inside = (local_rows >= 0) & (local_rows < owned)
    rank = jnp.dot(jnp.where(inside, 1.0, 0.0).astype(BF16), before, preferred_element_type=F32)
    slot = lax.rem(row, SLOTS).astype(F32)
    wanted = jnp.sum(
        jnp.where(inside & (rank == slot), local_rows.astype(F32), 0.0), axis=1, keepdims=True
    )
    pick = lax.broadcasted_iota(jnp.int32, (slots, owned), 1).astype(F32) == wanted
    pick = jnp.where(pick, 1.0, 0.0).astype(BF16)
    load.wait()
    parts = PARTS
    step = width // parts
    for c in range(parts):
        def fetch(b, carry):
            cols = pl.ds(pl.multiple_of(c * step + b * 512, 512), 512)
            out = jnp.dot(pick, table[:, cols], preferred_element_type=F32).astype(BF16)
            found[:, :, cols] = out.reshape(GROUP, SLOTS, 512)
            return carry

        lax.fori_loop(0, step // 512, fetch, 0)
        cols = pl.ds(c * step, step)
        for n, p in enumerate(peers):
            copy = remote(found.at[p, :, cols], recv.at[t, :, cols], xs.at[c, n], xr.at[c, n], {"tensor": p})
            copy.start()
            copies.append(copy)
        recv[t, :, cols] = found[t, :, cols]
    meanwhile()
    total = jnp.zeros((rows, 1), F32)
    for c in range(parts):
        cols = pl.ds(c * step, step)
        for n, p in enumerate(sources):
            ref = recv.at[p, :, cols]
            remote(ref, ref, xs.at[c, n], xr.at[c, n], {"tensor": p}).wait_recv()
        for b in range(step // 1024):
            cols = pl.ds(c * step + b * 1024, 1024)
            picked = jnp.dot(chosen, recv[:, :, cols].reshape(slots, 1024), preferred_element_type=F32)
            emb_ref[:, cols] = picked.astype(BF16)
            total += jnp.sum(picked * picked, axis=-1, keepdims=True)
    return copies, total


def document_starts(lengths_ref, positions):
    first = jnp.zeros_like(positions)
    start = jnp.int32(0)
    for d in range(lengths_ref.shape[0]):
        first = jnp.where(positions >= start, start, first)
        start = start + lengths_ref[d]
    return first


def attention(q_ref, first_ref, pair_ref, att_ref, win_ref, relay, m_ref, l_ref, acc_ref, ssem, rsem, z, early, late, done):
    t = lax.axis_index("tensor")
    r = lax.axis_index("dp")
    y, c = r // 2, lax.rem(r, 2)
    kind = lax.rem(t, 2)
    rows = q_ref.shape[0]
    group = rows // SIDE
    partner = {"tensor": t + 1 - 2 * kind}
    up = {"dp": lax.rem(y + 1, SIDE) * 2 + c}
    down = {"dp": lax.rem(y + SIDE - 1, SIDE) * 2 + c}
    other = {"dp": y * 2 + 1 - c}

    def copy(n, src, dst, peer):
        return remote(src, dst, ssem.at[n], rsem.at[n], peer)

    def step(w, i, count, causal):
        span = pl.ds(pl.multiple_of(i * group, UNIT), group)
        q = jnp.concatenate([q_ref[span, :HD], q_ref[span, HD:]], axis=0)
        scores = lax.dot_general(
            win_ref[w, 0, :count, :], q, (((1,), (1,)), ((), ())), preferred_element_type=F32
        )
        at = lax.broadcasted_iota(jnp.int32, (count, 1), 0) + w * rows
        allowed = at >= first_ref[i]
        if causal:
            query = lax.rem(lax.broadcasted_iota(jnp.int32, (1, 2 * group), 1), group)
            allowed &= at <= query + (4 * rows + i * group)
        scores = jnp.where(allowed, scores, NEGATIVE)
        top = jnp.max(scores, axis=0, keepdims=True) * EXP_SCALE
        if not causal:
            old = m_ref[i]
            top = jnp.maximum(old, top)
            decay = jnp.exp2(old - top)
        weights = jnp.exp2(scores * EXP_SCALE - top)
        total = jnp.sum(weights, axis=0, keepdims=True)
        added = lax.dot_general(
            win_ref[w, 1, :count, :], weights.astype(BF16), (((0,), (0,)), ((), ())),
            preferred_element_type=F32,
        )
        l_ref[i] = total if causal else l_ref[i] * decay + total
        acc_ref[i] = added if causal else acc_ref[i] * decay + added
        m_ref[i] = top

    def earlier(w, steps=range(SIDE)):
        @pl.when(r + w >= 4)
        def _():
            for i in steps:
                step(w, i, rows, False)

    piece = rows // 2

    def block(w, k, p):
        return win_ref.at[w, k, pl.ds(p * piece, piece)]

    def pieces(n, src, dst, peer):
        return [copy(2 * n + p, src(p), dst(p), peer) for p in range(2)]

    def within(n, source, target, k, peer):
        return pieces(n, lambda p: block(source, k, p), lambda p: block(target, k, p), peer)

    def mine(p):
        return pair_ref.at[pl.ds(p * piece, piece)]

    def held(p):
        return relay.at[pl.ds(p * piece, piece)]

    def when(condition, *acts):
        @pl.when(condition)
        def _():
            for act in acts:
                act()

    def starts(copies):
        return [one.start for one in copies]

    def recvs(copies):
        return [one.wait_recv for one in copies]

    def sends(copies):
        return [one.wait_send for one in copies]

    lacking = 1 - kind
    swap = pieces(0, mine, lambda p: block(4, kind, p), partner)
    swap_in = pieces(0, mine, lambda p: block(4, lacking, p), partner)
    up_own = pieces(1, mine, lambda p: block(2, kind, p), up)
    up_other = within(2, 4, 2, lacking, up)
    down_own = pieces(3, mine, held, down)
    far_own = pieces(4, held, lambda p: block(0, kind, p), down)
    far_other = within(5, 2, 0, lacking, up)
    near_own = pieces(6, mine, lambda p: block(3, kind, p), other)
    near_other = within(7, 4, 3, lacking, other)
    cross0_own, cross0_other = within(8, 2, 1, kind, other), within(9, 2, 1, lacking, other)
    cross1_own, cross1_other = within(8, 2, 3, kind, other), within(9, 2, 3, lacking, other)
    far1 = within(10, 0, 1, kind, other) + within(11, 0, 1, lacking, other)
    has_up, has_far = y < SIDE - 1, y < SIDE - 2
    got_up, got_far = y > 0, y > 1
    relays = (y == SIDE - 1) | (y == 0)
    for p in range(2):
        swap[p].start()
    when(has_up, *starts(up_own))
    when(has_far, *starts(down_own))
    when(c == 0, *starts(near_own))
    win_ref[4, kind] = pair_ref[...]
    for p in range(2):
        swap_in[p].wait_recv()
        when(has_up, up_other[p].start)
        when(c == 0, near_other[p].start)
        when(relays, down_own[p].wait_recv, far_own[p].start)
    early()
    for i in range(SIDE):
        step(4, i, (i + 1) * group, True)

    when(got_up, *recvs(up_own))
    when(got_up & (c == 0), *starts(cross0_own))
    when(got_up & (c == 1), *starts(cross1_own))
    for p in range(2):
        when(got_up, up_other[p].wait_recv)
        when(got_up & has_up, far_other[p].start)
        when(got_up & (c == 0), cross0_other[p].start)
        when(got_up & (c == 1), cross1_other[p].start)
    when(c == 1, *recvs(near_own + near_other))
    earlier(2 + c)

    when(got_up & (c == 0), *recvs(cross1_own + cross1_other))
    earlier(3 - c)
    late()

    when(got_far, *recvs(far_own + far_other))
    when(got_far & (c == 1), *starts(far1))
    when(got_up & (c == 1), *recvs(cross0_own + cross0_other))
    order = [wrap(z + dz) for dz in (2, 1, -1, 0)]
    earlier(c, order[:2])

    when(got_far & (c == 0), *recvs(far1))
    for n, i in enumerate(order):
        if n > 1:
            earlier(c, [i])
        earlier(1 - c, [i])
        out = (acc_ref[i] / l_ref[i]).T.astype(BF16)
        for h in range(2):
            att_ref[i, :, :, h * HD:(h + 1) * HD] = flat_units(out[h * group:(h + 1) * group])
        done((2, 1, -1, 0)[n])

    when(c == 0, *sends(near_own + near_other))
    when(got_up & (c == 0), *sends(cross0_own + cross0_other))
    when(got_up & (c == 1), *sends(cross1_own + cross1_other))
    when(got_far & (c == 1), *sends(far1))
    when(has_far, *sends(down_own))
    when(has_up, *sends(up_own + up_other))
    when(relays, *sends(far_own))
    when(got_up & has_up, *sends(far_other))
    for one in swap:
        one.wait_send()


def layer_kernel(ids_ref, lengths_ref, inverse_ref, attn_gain_ref, mlp_gain_ref,
                 table_hbm, wq_hbm, wkv_hbm, wo_hbm, wg_hbm, wu_hbm, wd_hbm, out_ref,
                 table, wq, wkv, wo, wg, wu, wd, load_sem,
                 wanted_by, all_ids, found, recv, ks, kr, xs, xr,
                 emb, all_ref, q, pair, cos_ref, sin_ref, first_ref, gs, gr,
                 win, relay, m_ref, l_ref, acc_ref, att, as_, ar,
                 stream, hid, gs2, gr2,
                 part, att_z, att_x, mine, got, ss, sr, bs, br, bxs, bxr, ps, pr, ys, yr, cs, cr,
                 down_blocks, hid_z, hid_x, ss2, sr2, zs, zr, hs, hr, *down_sems):
    z, x = here()
    t = lax.axis_index("tensor")
    r = lax.axis_index("dp")
    y, c = r // 2, lax.rem(r, 2)
    loads = [
        pltpu.make_async_copy(src, dst, load_sem.at[n])
        for n, (src, dst) in enumerate((
            (table_hbm, table), (wq_hbm, wq), (wkv_hbm, wkv), (wo_hbm, wo), (wg_hbm, wg), (wu_hbm, wu), (wd_hbm, wd)
        ))
    ]
    for load in loads:
        load.start()
    peers = [lax.rem(t + n, GROUP) for n in range(1, GROUP)]
    sources = [lax.rem(t + GROUP - n, GROUP) for n in range(1, GROUP)]
    greet([{"tensor": p} for p in peers] + [
        {"dp": lax.rem(y + 1, SIDE) * 2 + c}, {"dp": lax.rem(y + SIDE - 1, SIDE) * 2 + c}, {"dp": y * 2 + 1 - c},
    ])
    rows, width = emb.shape
    span_rows = rows * GROUP
    spread = Spread(wo_hbm, part, ps, pr, ys, yr, cs, cr, z, x)
    down = SpreadDown(wd_hbm, down_blocks, down_sems, z, x)
    hidden_width = wg.shape[0]

    def positions():
        hid[:, :, :, hidden_width:] = jnp.zeros((*hid.shape[:3], hid.shape[3] - hidden_width), BF16)
        spread.plane(False)
        spread.plane_far(True)
        group = span_rows // SIDE
        for i in range(SIDE):
            lanes = lax.rem(lax.broadcasted_iota(jnp.int32, (1, 2 * group), 1), group) + (r * span_rows + i * group)
            first_ref[i] = document_starts(lengths_ref, lanes) - (r - 4) * span_rows
        sign = jnp.where(lax.broadcasted_iota(jnp.int32, (1, HD), 1) < HD // 2, -1.0, 1.0)

        def turn(b, carry):
            at = pl.ds(pl.multiple_of(b * 64, 64), 64)
            place_of = r * span_rows + b * 64 + lax.broadcasted_iota(jnp.int32, (64, HD), 0)
            angle = (place_of - document_starts(lengths_ref, place_of)).astype(F32) * inverse_ref[...]
            cos_ref[at, :] = jnp.cos(angle)
            sin_ref[at, :] = jnp.sin(angle) * sign
            return carry

        lax.fori_loop(0, span_rows // 64, turn, 0)

    copies, total = find_rows(
        ids_ref, all_ids, wanted_by, table, found, recv, emb, t, peers, sources, loads[0], ks, kr, xs, xr,
        functools.partial(spread.plane, True), positions,
    )
    scale = lax.rsqrt(total / width + EPSILON)
    for b in range(width // 1024):
        cols = pl.ds(b * 1024, 1024)
        all_ref[t, :, cols] = (emb[:, cols].astype(F32) * scale * attn_gain_ref[:, cols]).astype(BF16)
    loads[1].wait()
    loads[2].wait()
    keys_here = lax.rem(t, 2) == 0

    def begun():
        spread.plane_far(False)
        spread.ring(True)
        spread.cores(True, (0,))

    def project(dz):
        if dz == 0:
            spread.ring(False)
            spread.ring_far(True)
            spread.cores(True, (1, 3))
        lhs, span = row_group(all_ref, z, dz)
        cos, sin = cos_ref[span, :], sin_ref[span, :]
        queries = jnp.dot(lhs, wq[...], preferred_element_type=F32)
        for h in range(queries.shape[1] // HD):
            head = queries[:, h * HD:(h + 1) * HD]
            q[span, h * HD:(h + 1) * HD] = (head * cos + pltpu.roll(head, HD // 2, 1) * sin).astype(BF16)
        both = jnp.dot(lhs, wkv[...], preferred_element_type=F32)
        turned = both * cos + pltpu.roll(both, HD // 2, 1) * sin
        pair[span, :] = jnp.where(keys_here, turned, both).astype(BF16)

    ring_gather(all_ref, gs, gr, z, x, project, begun)
    spread.ring_far(False)
    spread.cores(True, (2,))

    moves_of = Moves(att, att_z, att_x, bs, br, bxs, bxr, z, x)

    def late():
        down.plane(False)
        down.plane_far(True)

    attention(
        q, first_ref, pair, att, win, relay, m_ref, l_ref, acc_ref, as_, ar, z,
        functools.partial(down.plane, True), late, moves_of.finished
    )
    spread.cores(False, (0, 1, 3))

    def onward():
        down.plane_far(False)
        down.ring(True)
        down.cores(True, (0,))

    def mixed(cols, value):
        stream[:, cols] = (emb[:, cols].astype(F32) + value).astype(BF16)

    loads[3].wait()
    spread.cores(False, (2,))
    mix(moves_of, att, att_z, att_x, wo, part, mine, got, ss, sr, z, x, mixed, onward)
    spread.drain()
    all_ref[t] = normalize(stream[...].astype(F32), mlp_gain_ref[...])
    loads[4].wait()
    loads[5].wait()

    loads[6].wait()
    hidden = Moves(hid, hid_z, hid_x, zs, zr, hs, hr, z, x)

    def gate(dz):
        if dz == 0:
            down.ring(False)
            down.ring_far(True)
            down.cores(True, (1, 3))
        lhs, span = row_group(all_ref, z, dz)
        across = (((1,), (1,)), ((), ()))
        gated = lax.dot_general(lhs, wg[...], across, preferred_element_type=F32)
        upper = lax.dot_general(lhs, wu[...], across, preferred_element_type=F32)
        value = (gated / (1.0 + jnp.exp(-gated)) * upper).astype(BF16)
        hid[wrap(z + dz), :, :, :hidden_width] = value.reshape(SIDE * UNITS, UNIT, hidden_width)
        hidden.finished(dz)

    ring_gather(all_ref, gs2, gr2, z, x, gate)
    down.ring_far(False)
    down.cores(True, (2,))

    def arrive(h):
        hidden.arrive(h)
        if h == 1:
            down.cores(False, (0, 1, 3, 2))

    def multiply(h, cols):
        def left(block):
            return block.reshape(-1, hidden_width)

        own = hid[z, :, :, :hidden_width] if h == 0 else hid[:, pl.ds(x * UNITS, UNITS), :, :hidden_width]
        out = jnp.dot(left(own), flat(wd[:, :, cols]), preferred_element_type=F32)
        for n in range(SIDE - 1):
            block = hid_z[n, :, :, :hidden_width] if h == 0 else hid_x[n, :, :, :, :hidden_width]
            out = out + jnp.dot(left(block), flat(down_blocks[n, :, :, cols]), preferred_element_type=F32)
        return out

    def added(cols, value):
        out_ref[:, cols] = (stream[:, cols].astype(F32) + value).astype(BF16)

    short_reduce(mine, got, ss2, sr2, z, x, (1, 0), arrive, multiply, added)
    hidden.drain()
    down.drain()
    for copy in copies:
        copy.wait_send()


def layer(ids, lengths, inverse, attn_gain, mlp_gain, table, wq, wkv, wo, wg, wu, wd):
    rows, width = ids.shape[1], table.shape[1]
    span = rows * GROUP
    group = span // SIDE
    quarter = width // 4
    unit = (UNITS, UNIT)
    padded = -(-wg.shape[0] // 128) * 128
    whole = pl.BlockSpec(memory_space=VMEM)
    outside = pl.BlockSpec(memory_space=pl.ANY)
    peers = DMA((GROUP - 1,))
    return pl.pallas_call(
        layer_kernel,
        out_shape=jax.ShapeDtypeStruct((rows, width), BF16),
        in_specs=[whole, pl.BlockSpec(memory_space=pltpu.SMEM)] + [whole] * 3 + [outside] * 7,
        out_specs=whole,
        scratch_shapes=[
            *[VMEM(w.shape, BF16) for w in (table, wq, wkv, wo, wg, wu, wd)], DMA((7,)),
            VMEM((8, 128), jnp.int32), VMEM((GROUP, 8, 128), jnp.int32),
            VMEM((GROUP, SLOTS, width), BF16), VMEM((GROUP, SLOTS, width), BF16),
            peers, peers, DMA((PARTS, GROUP - 1)), DMA((PARTS, GROUP - 1)),
            VMEM((rows, width), BF16), VMEM((GROUP, rows, width), BF16),
            VMEM((span, wq.shape[1]), BF16), VMEM((span, HD), BF16),
            VMEM((span, HD), F32), VMEM((span, HD), F32), VMEM((SIDE, 1, 2 * group), jnp.int32), *GATHER_SEMS,
            VMEM((5, 2, span, HD), BF16), VMEM((span, HD), BF16),
            VMEM((SIDE, 1, 2 * group), F32), VMEM((SIDE, 1, 2 * group), F32), VMEM((SIDE, HD, 2 * group), F32),
            VMEM((SIDE, SIDE * UNITS, UNIT, 2 * HD), BF16), DMA((24,)), DMA((24,)),
            VMEM((rows, width), BF16), VMEM((SIDE, SIDE * UNITS, UNIT, padded), BF16), *GATHER_SEMS,
            VMEM((SIDE, SIDE * UNITS, UNIT, width), BF16),
            VMEM((SIDE - 1, SIDE * UNITS, UNIT, 2 * HD), BF16), VMEM((SIDE - 1, SIDE, *unit, 2 * HD), BF16),
            VMEM((2, SIDE * UNITS, UNIT, 2 * quarter), BF16), VMEM((2, 6, *unit, quarter), BF16),
            DMA((2, 6)), DMA((2, 6)),
            DMA((SIDE - 1,)), DMA((SIDE - 1,)), DMA((SIDE, SIDE - 1)), DMA((SIDE, SIDE - 1)),
            DMA((8,)), DMA((8,)), DMA((18,)), DMA((18,)), DMA((24,)), DMA((24,)),
            VMEM((SIDE - 1, *wd.shape), BF16),
            VMEM((SIDE - 1, SIDE * UNITS, UNIT, padded), BF16), VMEM((SIDE - 1, SIDE, *unit, padded), BF16),
            DMA((2, 6)), DMA((2, 6)), DMA((SIDE - 1,)), DMA((SIDE - 1,)), DMA((SIDE, SIDE - 1)), DMA((SIDE, SIDE - 1)),
            DMA((4,)), DMA((4,)), DMA((12,)), DMA((12,)), DMA((12,)), DMA((12,)),
        ],
        compiler_params=pltpu.CompilerParams(
            collective_id=0, has_side_effects=True, vmem_limit_bytes=63 * 2**20
        ),
        name="layer",
    )(ids, lengths, inverse, attn_gain, mlp_gain, table, wq, wkv, wo, wg, wu, wd)


def local(ids, doc_lengths, table, attn_gain, wq, wkv, wo, mlp_gain, w_gate, w_up, w_down):
    inverse = np.float32(ROPE_BASE) ** (-np.arange(HD // 2, dtype=np.float32) * np.float32(2.0 / HD))
    inverse = jnp.asarray(np.concatenate([inverse, inverse])[None, :], F32)
    return layer(
        ids[None, :], doc_lengths, inverse, attn_gain[None, :], mlp_gain[None, :],
        table, wq, wkv, wo.reshape(-1, UNIT, wo.shape[1]), w_gate.T, w_up.T, w_down.reshape(-1, UNIT, wo.shape[1]),
    )


def solution(mesh):
    placed = (
        P(("dp", "tensor")),
        P(),
        P("tensor", None),
        P(),
        P(None, "tensor"),
        P(None, "tensor"),
        P("tensor", None),
        P(),
        P(None, "tensor"),
        P(None, "tensor"),
        P("tensor", None),
    )
    return jax.shard_map(
        local, mesh=mesh, in_specs=placed, out_specs=P(("dp", "tensor"), None), check_vma=False
    )
```
